256 devices in a mesh: cuts: 2 (over z_hi), region: 128 (over y, x, z_lo, core).
Axes of the slice: x: 4, y: 4, z: 8 (z_hi: 2, z_lo: 4; z = z_hi * 4 + z_lo), core: 2. Of those that a mesh axis runs over, the one named last changes fastest.
Arguments:
- objects: float32 [2, 2, 32768, 1024], P('cuts', None, 'region'), may hold values from -4 to 4
- probes: bfloat16 [4, 2, 256, 256], replicated, may hold values from -4 to 4
- amplitudes: float32 [512, 256, 256], P('region'), may hold values from 0.2 to 2.5
- prop_phase: float32 [256, 256], replicated, may hold values from -3.140625 to 3.140625
- scan_rows: int32 [512], P('region'), may hold values from -128 to 128, as said below
- scan_cols: int32 [512], P('region'), may hold values from 0 to 768
- probe_choice: int32 [512], P('region'), may hold values from 0 to 3
Outputs:
- gradient: float32 [2, 2, 32768, 1024], P('cuts', None, 'region')
The draws below stay inside these ranges and needn't reach their ends.
Inputs may be any that keep to these rules, and one draw needn't show every extreme that they name: `scan_rows`: in every region, half of the positions start between 64 and 128 rows above the band's first row, and the other half end between 64 and 128 rows below its last row.
All inputs are finite; a program needn't handle non-finite values.
Results may differ from the reference program's by a relative error of at most 0.039.
Values may be sent and summed in bfloat16 or wider, within the bound.
No kernel may reach another device: no remote copies, remote signals or barrier semaphores. Data moves between devices by JAX's collectives and lax.ppermute only.
A program may use at most 64 MiB of HBM per device.

```python
import math
import jax
import jax.numpy as jnp
from jax import lax

PATCH = 256
HALO = 128
SLICES = 2
BATCHES = 4
PER_BATCH = 1
PROBES = 4
ROWS = 256
COLS = 1024
POS_DEV = 4
NPOS = 512
NROWS = 32768


def draw_scan_rows(key, part):
    key_order = jax.random.fold_in(key, 11)
    key_upper = jax.random.fold_in(key, 12)
    key_lower = jax.random.fold_in(key, 13)
    regions = NPOS // POS_DEV
    upper_rows = jax.random.randint(key_upper, (regions, POS_DEV), -HALO, -(HALO // 2) + 1, dtype=jnp.int32)
    lower_rows = jax.random.randint(key_lower, (regions, POS_DEV), ROWS - PATCH + HALO // 2, ROWS - PATCH + HALO + 1, dtype=jnp.int32)
    scores = jax.random.randint(key_order, (regions, POS_DEV), 0, 1 << 20, dtype=jnp.int32) * POS_DEV + jnp.arange(POS_DEV, dtype=jnp.int32)[None, :]
    ranking = jnp.argsort(jnp.argsort(scores, axis=1), axis=1)
    return jnp.where(ranking < POS_DEV // 2, upper_rows, lower_rows).astype(jnp.int32).reshape(-1)


def touch_ends(values, key, least, largest):
    dims = values.shape
    index_at = [jax.random.randint(jax.random.fold_in(key, axis), (), 0, dims[axis]) for axis in range(len(dims))]
    values = values.at[tuple(index_at)].set(least)
    longest = dims.index(max(dims))
    index_at[longest] = (index_at[longest] + 1) % dims[longest]
    return values.at[tuple(index_at)].set(largest)


def steps_of(rng, dims, cuts, least, top_value):
    def one(dim, shards_of):
        draws = jax.random.uniform(jax.random.fold_in(jax.random.fold_in(rng, 6), dim), (shards_of,), jnp.float32, least / len(cuts), top_value / len(cuts))
        return jnp.repeat(jnp.exp(draws), dims[dim] // shards_of).reshape((-1,) + (1,) * (len(dims) - dim - 1))

    level = one(*cuts[0])
    for cut in cuts[1:]:
        level = level * one(*cut)
    return level


def gaussian(own_key, shape, width, most, split=(), held_as=jnp.bfloat16):
    drawn = jax.random.normal(own_key, shape, jnp.float32) * width
    if len(split) > 0:
        drawn = steps_of(own_key, shape, split, -0.22, 0.18) * drawn
    return jnp.clip(drawn, min=-most, max=most).astype(held_as)


def setup_inputs(seed: int = 0) -> dict:
    key_list = jax.random.split(jax.random.key(seed), 8)
    objects = gaussian(key_list[0], (SLICES, 2, NROWS, COLS), 0.7, 4.0, ((0, 2), (2, 128)), jnp.float32)
    probes = gaussian(key_list[1], (PROBES, 2, PATCH, PATCH), 0.7, 4.0)
    amplitudes = jnp.clip(jnp.exp(math.log(2.5) - 2.5257286 * jax.random.uniform(key_list[2], (NPOS, PATCH, PATCH), jnp.float32) ** steps_of(key_list[2], (NPOS, PATCH, PATCH), ((0, 128),), -0.2, 0.2)), 0.2, 2.5)
    prop_phase = jnp.clip(jax.random.uniform(key_list[3], (PATCH, PATCH), jnp.float32, -3.140625, 3.140625), -3.140625, 3.140625)
    scan_rows = draw_scan_rows(jax.random.fold_in(key_list[7], 71), 0)
    scan_cols = touch_ends(jax.random.randint(key_list[5], (NPOS,), 0, COLS - PATCH + 1), jax.random.fold_in(key_list[5], 1), 0, COLS - PATCH).astype(jnp.int32)
    probe_choice = touch_ends(jax.random.randint(key_list[6], (NPOS,), 0, PROBES), jax.random.fold_in(key_list[6], 1), 0, PROBES - 1).astype(jnp.int32)
    return {"objects": objects, "probes": probes, "amplitudes": amplitudes, "prop_phase": prop_phase, "scan_rows": scan_rows, "scan_cols": scan_cols, "probe_choice": probe_choice}


modulus_floor = 0.25

def widened(narrow):
    return lax.optimization_barrier(narrow).astype(jnp.float32)

def dft_tables(length, direction):
    indices = jnp.arange(length, dtype=jnp.int32)
    product = indices[:, None] * indices[None, :] % length
    angles = product.astype(jnp.float32) * (2.0 * jnp.pi / length)
    scaling = 1.0 / jnp.sqrt(jnp.float32(length))
    return jnp.stack([jnp.cos(angles) * scaling, direction * jnp.sin(angles) * scaling]).astype(jnp.bfloat16)

def complex_join(part_stack):
    return jnp.stack([part_stack[0, :, 0] - part_stack[1, :, 1], part_stack[0, :, 1] + part_stack[1, :, 0]], axis=1)

def transform(input_field, dft_table):
    wide_table = dft_table.astype(jnp.float32)
    narrow_field = widened(input_field.astype(jnp.bfloat16))
    left_part = jnp.einsum('ajk,nckl->ancjl', wide_table, narrow_field)
    middle = widened(complex_join(left_part).astype(jnp.bfloat16))
    right_part = jnp.einsum('nckl,alm->anckm', middle, wide_table)
    return complex_join(right_part)

def multiply_complex(left_field, right_field):
    real_part = left_field[..., 0, :, :] * right_field[..., 0, :, :] - left_field[..., 1, :, :] * right_field[..., 1, :, :]
    imag_part = left_field[..., 0, :, :] * right_field[..., 1, :, :] + left_field[..., 1, :, :] * right_field[..., 0, :, :]
    return jnp.stack([real_part, imag_part], axis=-3)

def multiply_conjugate(left_field, right_field):
    real_part = left_field[..., 0, :, :] * right_field[..., 0, :, :] + left_field[..., 1, :, :] * right_field[..., 1, :, :]
    imag_part = left_field[..., 0, :, :] * right_field[..., 1, :, :] - left_field[..., 1, :, :] * right_field[..., 0, :, :]
    return jnp.stack([real_part, imag_part], axis=-3)

def propagate(input_field, optics):
    propagator, forward_table, inverse_table = optics
    return transform(multiply_complex(propagator, transform(input_field, forward_table)), inverse_table)

def propagate_adjoint(input_field, optics):
    propagator, forward_table, inverse_table = optics
    return transform(multiply_conjugate(propagator, transform(input_field, forward_table)), inverse_table)

def reference(objects, probes, amplitudes, prop_phase, scan_rows, scan_cols, probe_choice):
    slice_count = objects.shape[0]
    total_rows = objects.shape[2]
    rim_depth = PATCH // 2
    per_region = BATCHES * PER_BATCH
    optics = (jnp.stack([jnp.cos(prop_phase), jnp.sin(prop_phase)]), dft_tables(PATCH, -1.0), dft_tables(PATCH, 1.0))
    zero_index = jnp.zeros((), jnp.int32)
    window_steps = jnp.arange(PATCH, dtype=jnp.int32)

    def visit_position(running, position):
        region = position // per_region
        top_row = (region * ROWS + scan_rows[position]).astype(jnp.int32)
        left_col = scan_cols[position].astype(jnp.int32)
        row_ids = ((top_row + total_rows + window_steps) % total_rows).astype(jnp.int32)
        band_part = jnp.take(objects, row_ids, axis=2)
        window = lax.dynamic_slice(band_part, (zero_index, zero_index, zero_index, left_col), (slice_count, 2, PATCH, PATCH))
        current = probes[probe_choice[position]][None]
        measured = amplitudes[position][None]
        stored = []
        for slice_index in range(slice_count):
            stored.append(current)
            exit_field = multiply_complex(widened(current), window[slice_index][None])
            if slice_index < slice_count - 1:
                current = propagate(exit_field, optics).astype(jnp.bfloat16)
            else:
                far_field = transform(exit_field, optics[1])
                modulus = jnp.sqrt(far_field[:, 0] * far_field[:, 0] + far_field[:, 1] * far_field[:, 1])
                factor = 1.0 - measured / jnp.maximum(modulus, modulus_floor)
                current = transform(far_field * factor[:, None], optics[2]).astype(jnp.bfloat16)
        pieces = [None] * slice_count
        for slice_index in reversed(range(slice_count)):
            arriving = widened(current)
            pieces[slice_index] = multiply_conjugate(widened(stored[slice_index]), arriving)[0]
            if slice_index > 0:
                backward = multiply_conjugate(window[slice_index][None], arriving)
                current = propagate_adjoint(backward, optics).astype(jnp.bfloat16)
        deposit_block = jnp.stack(pieces)
        corner = (zero_index, zero_index, (top_row + rim_depth).astype(jnp.int32), left_col)
        existing = lax.dynamic_slice(running, corner, deposit_block.shape)
        return (lax.dynamic_update_slice(running, existing + deposit_block, corner), None)
    padded_shape = (slice_count, 2, total_rows + 2 * rim_depth, objects.shape[3])
    summed, unused = lax.scan(visit_position, jnp.zeros(padded_shape, jnp.float32), jnp.arange(NPOS, dtype=jnp.int32))
    gradient = summed[:, :, rim_depth:rim_depth + total_rows]
    gradient = gradient.at[:, :, :rim_depth].add(summed[:, :, total_rows + rim_depth:])
    gradient = gradient.at[:, :, total_rows - rim_depth:].add(summed[:, :, :rim_depth])
    return gradient
```

```python
import functools

import jax
import jax.numpy as jnp
import ml_dtypes
import numpy as np
from jax import lax
from jax.experimental import pallas as pl
from jax.experimental.pallas import tpu as pltpu
from jax.sharding import PartitionSpec as P

modulus_floor = 0.25
AXES = ("cuts", "region")
BF = jnp.bfloat16
F32 = jnp.float32
SIDE = 256
HALF = 128
BAND = 256
COLS = 1024
EXT = BAND + 2 * HALF
WIDE = SIDE + 128
VM = pl.BlockSpec(memory_space=pltpu.VMEM)
SM = pl.BlockSpec(memory_space=pltpu.SMEM)


def routes(regions):
    at = lambda c, r: c * regions + r % regions
    both = [(c, r) for c in range(2) for r in range(regions)]
    return {
        "mate": [(at(c, r), at(1 - c, r)) for c, r in both],
        "next": [(at(c, r), at(c, r + 1)) for c, r in both],
        "prev": [(at(c, r), at(c, r - 1)) for c, r in both],
        "solo": [(at(c, r), at(c, r - 1 if c == 0 else r + 1)) for c, r in both],
        "relay": [(at(c, r), at(c, r + 1 if c == 0 else r - 1)) for c, r in both],
    }


def dft_blocks():
    index = np.arange(SIDE)
    angles = (index[:, None] * index[None, :] % SIDE) * (2.0 * np.pi / SIDE)
    real = np.cos(angles) / np.sqrt(SIDE)
    imag = -np.sin(angles) / np.sqrt(SIDE)
    first = np.block([[real, -imag], [imag, real]]).astype(ml_dtypes.bfloat16)
    second = np.block([[real, imag], [-imag, real]]).astype(ml_dtypes.bfloat16)
    return first, second


def places(rows):
    up = [rows[i] < 0 for i in range(4)]
    first = lambda a, b: jnp.where(a, 0, jnp.where(b, 1, 2))
    last = lambda a, b: jnp.where(a, 3, jnp.where(b, 2, 1))
    no = [jnp.logical_not(u) for u in up]
    return first(up[0], up[1]), last(up[3], up[2]), first(no[0], no[1]), last(no[3], no[2])


def column_split(left):
    base = jnp.minimum(lax.shift_right_logical(left, 7), (COLS - WIDE) // 128) * 128
    return pl.multiple_of(base, 128), left - base


def row_split(top, most):
    base = jnp.minimum(lax.shift_right_logical(top, 3), most // 8) * 8
    return pl.multiple_of(base, 8), top - base


def cut_window(load, top, left, count, total):
    row_base, row_shift = row_split(top, total - count - 8)
    col_base, col_shift = column_split(left)
    block = load(pl.ds(row_base, count + 8), pl.ds(col_base, WIDE))
    block = pltpu.roll(block, lax.rem(count + 8 - row_shift, count + 8), 0)[:count]
    return pltpu.roll(block, lax.rem(WIDE - col_shift, WIDE), 1)[:, :SIDE]


def put_window(total_ref, channel, top, left, block):
    count = block.shape[0]
    row_base, row_shift = row_split(top, EXT - count - 8)
    col_base, col_shift = column_split(left)
    block = jnp.concatenate([block, jnp.zeros((count, WIDE - SIDE), F32)], axis=1)
    block = pltpu.roll(block, col_shift, 1)
    block = jnp.concatenate([block, jnp.zeros((8, WIDE), F32)], axis=0)
    block = pltpu.roll(block, row_shift, 0)
    where = (channel, pl.ds(row_base, count + 8), pl.ds(col_base, WIDE))
    total_ref[where] = total_ref[where] + block


def inband_kernel(rows, cols, objects, inband, low, high):
    cut = lax.axis_index("cuts")
    u0, u1, l0, l1 = places(rows)
    other_up = cut == 1
    for slot, (place, up) in enumerate(
        [(jnp.where(other_up, u1, l1), other_up), (u0, None), (l0, None)]
    ):
        offset = jnp.where(up, HALF, 0) if slot == 0 else (HALF if slot == 1 else 0)
        for channel in range(2):
            inband[slot, channel] = cut_window(
                lambda r, c: objects[0, channel, r, c], rows[place] + offset, cols[place], HALF, BAND
            ).astype(BF)
    for channel in range(2):
        low[channel] = objects[0, channel, :HALF].astype(BF)
        high[channel] = objects[0, channel, HALF:].astype(BF)


def outer_kernel(rows, cols, objects, above, below, half0, half1, half2, windows, ext):
    cut = lax.axis_index("cuts")
    u0, u1, l0, l1 = places(rows)
    other_up = cut == 1
    for channel in range(2):
        ext[channel, :HALF] = above[channel].astype(F32)
        ext[channel, HALF : HALF + BAND] = objects[0, channel]
        ext[channel, HALF + BAND :] = below[channel].astype(F32)
    other = jnp.where(other_up, u1, l1)
    solo = jnp.where(other_up, l1, u1)
    for channel in range(2):
        load = lambda r, c: ext[channel, r, c]
        top = rows[other] + jnp.where(other_up, HALF, 2 * HALF)
        half0[channel] = cut_window(load, top, cols[other], HALF, EXT).astype(BF)
        for slot, place in enumerate((solo, u0, l0)):
            window = cut_window(load, rows[place] + HALF, cols[place], SIDE, EXT).astype(BF)
            windows[slot, channel] = window
            if slot == 1:
                half1[channel] = window[:HALF]
            if slot == 2:
                half2[channel] = window[HALF:]


def transform(fields, left, right):
    count = len(fields)
    stacked = jnp.concatenate(
        [jnp.concatenate([f[part].astype(BF) for f in fields], axis=1) for part in range(2)], axis=0
    )
    middle = jnp.dot(left, stacked, preferred_element_type=F32).astype(BF)
    spans = [slice(SIDE * k, SIDE * (k + 1)) for k in range(count)]
    middle = jnp.concatenate(
        [jnp.concatenate([middle[:SIDE, s], middle[SIDE:, s]], axis=1) for s in spans], axis=0
    )
    result = jnp.dot(middle, right, preferred_element_type=F32)
    return [(result[s, :SIDE], result[s, SIDE:]) for s in spans]


def times(a, b):
    return a[0] * b[0] - a[1] * b[1], a[0] * b[1] + a[1] * b[0]


def conj_times(a, b):
    return a[0] * b[0] + a[1] * b[1], a[0] * b[1] - a[1] * b[0]


def wide(pair):
    return pair[0].astype(F32), pair[1].astype(F32)


def chain(incoming, patches, measured, wave, first, second, store):
    spots = range(len(incoming))
    propagator = (wave[0], wave[1])
    fields = [times(wide(incoming[k]()), patches[k](0)) for k in spots]
    fields = [times(propagator, f) for f in transform(fields, first, second)]
    psi = [(f[0].astype(BF), f[1].astype(BF)) for f in transform(fields, second, first)]
    fields = [times(wide(psi[k]), patches[k](1)) for k in spots]
    detected = []
    for k, (real, imag) in enumerate(transform(fields, first, second)):
        modulus = jnp.sqrt(real * real + imag * imag)
        factor = 1.0 - measured[k]() / jnp.maximum(modulus, modulus_floor)
        detected.append((real * factor, imag * factor))
    arriving = [(f[0].astype(BF), f[1].astype(BF)) for f in transform(detected, second, first)]
    arriving = [wide(f) for f in arriving]
    for k in spots:
        store(k, 1, conj_times(wide(psi[k]), arriving[k]))
    fields = [conj_times(patches[k](1), arriving[k]) for k in spots]
    fields = [conj_times(propagator, f) for f in transform(fields, first, second)]
    for k, (real, imag) in enumerate(transform(fields, second, first)):
        arrived = real.astype(BF).astype(F32), imag.astype(BF).astype(F32)
        store(k, 0, conj_times(wide(incoming[k]()), arrived))


def fill_patches(held, own, inband, outer, cut, start):
    for channel in range(2):
        held[cut, channel] = own[channel]
        held[1 - cut, channel, pl.ds(start, HALF)] = outer[channel]
        held[1 - cut, channel, pl.ds(HALF - start, HALF)] = inband[channel]


def patch_of(held):
    return lambda which: wide((held[which, 0], held[which, 1]))


def probe_of(probes, choice):
    return lambda: (probes[choice, 0], probes[choice, 1])


def solo_kernel(
    rows, picks, windows, inband, outer, probes, amplitudes, wave, first, second,
    sent_outer, sent_inband, kept, edge, held, made,
):
    cut = lax.axis_index("cuts")
    u0, u1, l0, l1 = places(rows)
    place = jnp.where(cut == 0, u1, l1)
    start = pl.multiple_of(jnp.where(cut == 0, 0, HALF), HALF)
    fill_patches(held, windows.at[0], inband.at[0], outer, cut, start)

    def store(k, which, value):
        made[which, 0], made[which, 1] = value

    chain(
        [probe_of(probes, picks[place])], [patch_of(held)], [lambda: amplitudes[place]],
        wave, first[...], second[...], store,
    )
    for channel in range(2):
        sent_outer[channel] = made[1 - cut, channel, pl.ds(start, HALF)].astype(BF)
        sent_inband[channel] = made[1 - cut, channel, pl.ds(HALF - start, HALF)].astype(BF)
        kept[channel] = made[cut, channel]
        edge[channel] = made[cut, channel, pl.ds(start, HALF)].astype(BF)


def shared_kernel(
    rows, picks, windows, inband, outer1, outer2, probes, amplitudes, wave, first, second,
    kept, edge_up, edge_low, held, made,
):
    cut = lax.axis_index("cuts")
    u0, u1, l0, l1 = places(rows)
    fill_patches(held.at[0], windows.at[1], inband.at[1], outer1, cut, 0)
    fill_patches(held.at[1], windows.at[2], inband.at[2], outer2, cut, HALF)

    def store(k, which, value):
        made[k, which, 0], made[k, which, 1] = value

    chain(
        [probe_of(probes, picks[u0]), probe_of(probes, picks[l0])],
        [patch_of(held.at[0]), patch_of(held.at[1])],
        [lambda: amplitudes[u0], lambda: amplitudes[l0]],
        wave, first[...], second[...], store,
    )
    for channel in range(2):
        for k in range(2):
            kept[k, channel] = made[k, cut, channel]
        edge_up[channel] = made[0, cut, channel, :HALF].astype(BF)
        edge_low[channel] = made[1, cut, channel, HALF:].astype(BF)


def gather_kernel(
    rows, cols, after, before, solo, shared, from_outer, from_inband,
    edge_solo, edge_relay, edge_up, edge_low, output, total,
):
    cut = lax.axis_index("cuts")
    u0, u1, l0, l1 = places(rows)
    after_rows = [after[i] for i in range(4)]
    before_rows = [before[i] for i in range(4)]
    next_u0, next_u1, _, _ = places(after_rows)
    _, _, last_l0, last_l1 = places(before_rows)
    total[...] = jnp.zeros_like(total)
    own = jnp.where(cut == 0, u1, l1)
    other = jnp.where(cut == 0, l1, u1)
    start = jnp.where(cut == 0, HALF, 0)
    next_top = lambda place: after[place] + HALF + BAND
    last_top = lambda place: before[place]
    solo_top = jnp.where(cut == 0, next_top(next_u1), last_top(last_l1))
    solo_left = jnp.where(cut == 0, after[4 + next_u1], before[4 + last_l1])
    relay_top = jnp.where(cut == 0, last_top(last_l1), next_top(next_u1))
    relay_left = jnp.where(cut == 0, before[4 + last_l1], after[4 + next_u1])
    for channel in range(2):
        put = functools.partial(put_window, total, channel)
        put(rows[own] + HALF, cols[own], solo[channel])
        put(rows[u0] + HALF, cols[u0], shared[0, channel])
        put(rows[l0] + HALF, cols[l0], shared[1, channel])
        put(rows[other] + HALF + start, cols[other], from_outer[channel].astype(F32))
        put(rows[other] + 2 * HALF - start, cols[other], from_inband[channel].astype(F32))
        put(solo_top, solo_left, edge_solo[channel].astype(F32))
        put(relay_top, relay_left, edge_relay[channel].astype(F32))
        put(next_top(next_u0), after[4 + next_u0], edge_up[channel].astype(F32))
        put(last_top(last_l0), before[4 + last_l0], edge_low[channel].astype(F32))
        output[0, channel] = total[channel, HALF : HALF + BAND]


def call(kernel, name, inputs, outputs, scratch=(), flops=0):
    scalars = [x for x in inputs if x.dtype == jnp.int32]
    moved = sum(x.size * x.dtype.itemsize for x in list(inputs) + list(outputs))
    return pl.pallas_call(
        kernel,
        name=name,
        out_shape=outputs,
        in_specs=[SM] * len(scalars) + [VM] * (len(inputs) - len(scalars)),
        out_specs=[VM] * len(outputs),
        scratch_shapes=list(scratch),
        cost_estimate=pl.CostEstimate(flops=flops, bytes_accessed=moved, transcendentals=0),
        compiler_params=pltpu.CompilerParams(vmem_limit_bytes=40 << 20),
    )(*inputs)


def arr(*shape, dtype=BF):
    return jax.ShapeDtypeStruct(shape, dtype)


def shards(objects, probes, amplitudes, prop_phase, scan_rows, scan_cols, probe_choice):
    route = routes(lax.axis_size("region"))
    move = lambda x, way: lax.ppermute(x, AXES, route[way])
    first, second = (jnp.asarray(t) for t in dft_blocks())
    wave = jnp.stack([jnp.cos(prop_phase), jnp.sin(prop_phase)])
    half = arr(2, HALF, SIDE)
    product = 2 * 2 * 512 * 512 * 256

    inband, low, high = call(
        inband_kernel, "inband", [scan_rows, scan_cols, objects],
        [arr(3, 2, HALF, SIDE), arr(2, HALF, COLS), arr(2, HALF, COLS)],
    )
    mate_inband = move(inband, "mate")
    above = move(high, "next")
    below = move(low, "prev")
    scan = jnp.concatenate([scan_rows, scan_cols])
    before = move(scan, "next")
    after = move(scan, "prev")
    half0, half1, half2, windows = call(
        outer_kernel, "outer", [scan_rows, scan_cols, objects, above, below],
        [half, half, half, arr(3, 2, SIDE, SIDE)],
        [pltpu.VMEM((2, EXT, COLS), F32)],
    )
    mate0 = move(half0, "mate")
    mate1 = move(half1, "mate")
    mate2 = move(half2, "mate")
    sent_outer, sent_inband, solo, edge = call(
        solo_kernel, "solo",
        [scan_rows, probe_choice, windows, mate_inband, mate0, probes, amplitudes, wave, first, second],
        [half, half, arr(2, SIDE, SIDE, dtype=F32), half],
        [pltpu.VMEM((2, 2, SIDE, SIDE), BF), pltpu.VMEM((2, 2, SIDE, SIDE), F32)],
        flops=6 * product,
    )
    from_outer = move(sent_outer, "mate")
    from_inband = move(sent_inband, "mate")
    edge_solo = move(edge, "solo")
    shared, up, down = call(
        shared_kernel, "shared",
        [scan_rows, probe_choice, windows, mate_inband, mate1, mate2, probes, amplitudes, wave, first, second],
        [arr(2, 2, SIDE, SIDE, dtype=F32), half, half],
        [pltpu.VMEM((2, 2, 2, SIDE, SIDE), BF), pltpu.VMEM((2, 2, 2, SIDE, SIDE), F32)],
        flops=12 * product,
    )
    edge_up = move(up, "prev")
    edge_low = move(down, "next")
    edge_relay = move(from_outer, "relay")
    (gradient,) = call(
        gather_kernel, "gather",
        [scan_rows, scan_cols, after, before, solo, shared, from_outer, from_inband,
         edge_solo, edge_relay, edge_up, edge_low],
        [arr(1, 2, BAND, COLS, dtype=F32)],
        [pltpu.VMEM((2, EXT, COLS), F32)],
    )
    return gradient


def solution(mesh):
    return jax.shard_map(
        shards,
        mesh=mesh,
        in_specs=(
            P("cuts", None, "region", None),
            P(),
            P("region", None, None),
            P(),
            P("region"),
            P("region"),
            P("region"),
        ),
        out_specs=P("cuts", None, "region", None),
        check_vma=False,
    )
```

```python
import functools

import jax
import jax.numpy as jnp
import ml_dtypes
import numpy as np
from jax import lax
from jax.experimental import pallas as pl
from jax.experimental.pallas import tpu as pltpu
from jax.sharding import PartitionSpec as P

modulus_floor = 0.25
AXES = ("cuts", "region")
BF = jnp.bfloat16
F32 = jnp.float32
SIDE = 256
HALF = 128
BAND = 256
COLS = 1024
EXT = BAND + 2 * HALF
WIDE = SIDE + 128
VM = pl.BlockSpec(memory_space=pltpu.VMEM)
SM = pl.BlockSpec(memory_space=pltpu.SMEM)
HB = pl.BlockSpec(memory_space=pltpu.HBM)


def routes(regions):
    at = lambda c, r: c * regions + r % regions
    both = [(c, r) for c in range(2) for r in range(regions)]
    return {
        "mate": [(at(c, r), at(1 - c, r)) for c, r in both],
        "next": [(at(c, r), at(c, r + 1)) for c, r in both],
        "prev": [(at(c, r), at(c, r - 1)) for c, r in both],
    }


def dft_blocks():
    index = np.arange(SIDE)
    angles = (index[:, None] * index[None, :] % SIDE) * (2.0 * np.pi / SIDE)
    real = np.cos(angles) / np.sqrt(SIDE)
    imag = -np.sin(angles) / np.sqrt(SIDE)
    first = np.block([[real, -imag], [imag, real]]).astype(ml_dtypes.bfloat16)
    second = np.block([[real, imag], [-imag, real]]).astype(ml_dtypes.bfloat16)
    return first, second


def places(rows):
    up = [rows[i] < 0 for i in range(4)]
    first = lambda a, b: jnp.where(a, 0, jnp.where(b, 1, 2))
    last = lambda a, b: jnp.where(a, 3, jnp.where(b, 2, 1))
    no = [jnp.logical_not(u) for u in up]
    return first(up[0], up[1]), last(up[3], up[2]), first(no[0], no[1]), last(no[3], no[2])


def column_split(left):
    base = jnp.minimum(lax.shift_right_logical(left, 7), (COLS - WIDE) // 128) * 128
    return pl.multiple_of(base, 128), left - base


def row_split(top, most):
    base = jnp.minimum(lax.shift_right_logical(top, 3), most // 8) * 8
    return pl.multiple_of(base, 8), top - base


def cut_window(load, top, left, count, total):
    row_base, row_shift = row_split(top, total - count - 8)
    col_base, col_shift = column_split(left)
    block = load(pl.ds(row_base, count + 8), pl.ds(col_base, WIDE))
    block = pltpu.roll(block, lax.rem(count + 8 - row_shift, count + 8), 0)[:count]
    return pltpu.roll(block, lax.rem(WIDE - col_shift, WIDE), 1)[:, :SIDE]


def put_window(total_ref, channel, top, left, block):
    count = block.shape[0]
    row_base, row_shift = row_split(top, EXT - count - 8)
    col_base, col_shift = column_split(left)
    block = jnp.concatenate([block, jnp.zeros((count, WIDE - SIDE), F32)], axis=1)
    block = pltpu.roll(block, col_shift, 1)
    block = jnp.concatenate([block, jnp.zeros((8, WIDE), F32)], axis=0)
    block = pltpu.roll(block, row_shift, 0)
    where = (channel, pl.ds(row_base, count + 8), pl.ds(col_base, WIDE))
    total_ref[where] = total_ref[where] + block


def inband_kernel(rows_in, cols_in, objects_in, inband, low, high, rows, cols, objects, sems):
    cut = lax.axis_index("cuts")
    copies = [
        pltpu.make_async_copy(rows_in, rows, sems.at[0]),
        pltpu.make_async_copy(cols_in, cols, sems.at[1]),
        pltpu.make_async_copy(objects_in.at[0, 0], objects.at[0], sems.at[2]),
        pltpu.make_async_copy(objects_in.at[0, 1], objects.at[1], sems.at[3]),
    ]
    for copy in copies:
        copy.start()
    copies[0].wait()
    copies[1].wait()
    u0, u1, l0, l1 = places(rows)
    other_up = cut == 1
    spots = [
        (jnp.where(other_up, u1, l1), jnp.where(other_up, HALF, 0)), (u0, HALF), (l0, 0)
    ]
    for channel in range(2):
        copies[2 + channel].wait()
        low[channel] = objects[channel, :HALF].astype(BF)
        high[channel] = objects[channel, HALF:].astype(BF)
        for slot, (place, offset) in enumerate(spots):
            inband[slot, channel] = cut_window(
                lambda r, c: objects[channel, r, c], rows[place] + offset, cols[place], HALF, BAND
            ).astype(BF)


def outer_kernel(rows, cols, objects, above, below, half0, half12, windows, ext):
    cut = lax.axis_index("cuts")
    u0, u1, l0, l1 = places(rows)
    other_up = cut == 1
    for channel in range(2):
        ext[channel, :HALF] = above[channel].astype(F32)
        ext[channel, HALF : HALF + BAND] = objects[0, channel]
        ext[channel, HALF + BAND :] = below[channel].astype(F32)
    other = jnp.where(other_up, u1, l1)
    solo = jnp.where(other_up, l1, u1)
    for channel in range(2):
        load = lambda r, c: ext[channel, r, c]
        top = rows[other] + jnp.where(other_up, HALF, 2 * HALF)
        half0[channel] = cut_window(load, top, cols[other], HALF, EXT).astype(BF)
        for slot, place in enumerate((solo, u0, l0)):
            window = cut_window(load, rows[place] + HALF, cols[place], SIDE, EXT).astype(BF)
            windows[slot, channel] = window
            if slot == 1:
                half12[0, channel] = window[:HALF]
            if slot == 2:
                half12[1, channel] = window[HALF:]


def transform(fields, left, right):
    count = len(fields)
    stacked = jnp.concatenate(
        [jnp.concatenate([f[part].astype(BF) for f in fields], axis=1) for part in range(2)], axis=0
    )
    middle = jnp.dot(left, stacked, preferred_element_type=F32).astype(BF)
    spans = [slice(SIDE * k, SIDE * (k + 1)) for k in range(count)]
    middle = jnp.concatenate(
        [jnp.concatenate([middle[:SIDE, s], middle[SIDE:, s]], axis=1) for s in spans], axis=0
    )
    result = jnp.dot(middle, right, preferred_element_type=F32)
    return [(result[s, :SIDE], result[s, SIDE:]) for s in spans]


def times(a, b):
    return a[0] * b[0] - a[1] * b[1], a[0] * b[1] + a[1] * b[0]


def conj_times(a, b):
    return a[0] * b[0] + a[1] * b[1], a[0] * b[1] - a[1] * b[0]


def wide(pair):
    return pair[0].astype(F32), pair[1].astype(F32)


def chain(incoming, patches, measured, wave, first, second, store):
    spots = range(len(incoming))
    propagator = (wave[0], wave[1])
    fields = [times(wide(incoming[k]()), patches[k](0)) for k in spots]
    fields = [times(propagator, f) for f in transform(fields, first, second)]
    psi = [(f[0].astype(BF), f[1].astype(BF)) for f in transform(fields, second, first)]
    fields = [times(wide(psi[k]), patches[k](1)) for k in spots]
    detected = []
    for k, (real, imag) in enumerate(transform(fields, first, second)):
        modulus = jnp.sqrt(real * real + imag * imag)
        factor = 1.0 - measured[k]() / jnp.maximum(modulus, modulus_floor)
        detected.append((real * factor, imag * factor))
    arriving = [(f[0].astype(BF), f[1].astype(BF)) for f in transform(detected, second, first)]
    arriving = [wide(f) for f in arriving]
    for k in spots:
        store(k, 1, conj_times(wide(psi[k]), arriving[k]))
    fields = [conj_times(patches[k](1), arriving[k]) for k in spots]
    fields = [conj_times(propagator, f) for f in transform(fields, first, second)]
    for k, (real, imag) in enumerate(transform(fields, second, first)):
        arrived = real.astype(BF).astype(F32), imag.astype(BF).astype(F32)
        store(k, 0, conj_times(wide(incoming[k]()), arrived))


def fill_patches(held, own, inband, outer, cut, start):
    for channel in range(2):
        held[cut, channel] = own[channel]
        held[1 - cut, channel, pl.ds(start, HALF)] = outer[channel]
        held[1 - cut, channel, pl.ds(HALF - start, HALF)] = inband[channel]


def patch_of(held):
    return lambda which: wide((held[which, 0], held[which, 1]))


def probe_of(probes, choice):
    return lambda: (probes[choice, 0], probes[choice, 1])


def solo_kernel(
    rows, picks, windows, inband, outer, probes, amplitudes, wave, first, second,
    sent_outer, sent_inband, kept, edge, held, made,
):
    cut = lax.axis_index("cuts")
    u0, u1, l0, l1 = places(rows)
    place = jnp.where(cut == 0, u1, l1)
    start = pl.multiple_of(jnp.where(cut == 0, 0, HALF), HALF)
    fill_patches(held, windows.at[0], inband.at[0], outer, cut, start)

    def store(k, which, value):
        made[which, 0], made[which, 1] = value

    chain(
        [probe_of(probes, picks[place])], [patch_of(held)], [lambda: amplitudes[place]],
        wave, first[...], second[...], store,
    )
    for channel in range(2):
        sent_outer[channel] = made[1 - cut, channel, pl.ds(start, HALF)].astype(BF)
        sent_inband[channel] = made[1 - cut, channel, pl.ds(HALF - start, HALF)].astype(BF)
        kept[channel] = made[cut, channel]
        edge[channel] = made[cut, channel, pl.ds(start, HALF)].astype(BF)


def shared_kernel(
    rows, picks, windows, inband, outer, probes, amplitudes, wave, first, second,
    kept, edge_up, edge_low, held, made,
):
    cut = lax.axis_index("cuts")
    u0, u1, l0, l1 = places(rows)
    fill_patches(held.at[0], windows.at[1], inband.at[1], outer.at[0], cut, 0)
    fill_patches(held.at[1], windows.at[2], inband.at[2], outer.at[1], cut, HALF)

    def store(k, which, value):
        made[k, which, 0], made[k, which, 1] = value

    chain(
        [probe_of(probes, picks[u0]), probe_of(probes, picks[l0])],
        [patch_of(held.at[0]), patch_of(held.at[1])],
        [lambda: amplitudes[u0], lambda: amplitudes[l0]],
        wave, first[...], second[...], store,
    )
    for channel in range(2):
        for k in range(2):
            kept[k, channel] = made[k, cut, channel]
        edge_up[channel] = made[0, cut, channel, :HALF].astype(BF)
        edge_low[channel] = made[1, cut, channel, HALF:].astype(BF)


def edges_kernel(solo, up, low, relay, to_prev, to_next):
    cut = lax.axis_index("cuts")
    to_prev[0] = up[...]
    to_next[0] = low[...]

    @pl.when(cut == 0)
    def _():
        to_prev[1] = solo[...]
        to_next[1] = relay[...]

    @pl.when(cut == 1)
    def _():
        to_prev[1] = relay[...]
        to_next[1] = solo[...]


def own_kernel(rows, cols, solo, shared, from_inband, total):
    cut = lax.axis_index("cuts")
    u0, u1, l0, l1 = places(rows)
    own = jnp.where(cut == 0, u1, l1)
    other = jnp.where(cut == 0, l1, u1)
    start = jnp.where(cut == 0, HALF, 0)
    total[...] = jnp.zeros_like(total)
    for channel in range(2):
        put = functools.partial(put_window, total, channel)
        put(rows[own] + HALF, cols[own], solo[channel])
        put(rows[u0] + HALF, cols[u0], shared[0, channel])
        put(rows[l0] + HALF, cols[l0], shared[1, channel])
        put(rows[other] + 2 * HALF - start, cols[other], from_inband[channel].astype(F32))


def rest_kernel(rows, cols, after, before, given, from_outer, from_next, from_prev, total, output, sems):
    cut = lax.axis_index("cuts")
    u0, u1, l0, l1 = places(rows)
    next_spots = places([after[i] for i in range(4)])[:2]
    prev_spots = places([before[i] for i in range(4)])[2:]
    other = jnp.where(cut == 0, l1, u1)
    start = jnp.where(cut == 0, HALF, 0)
    copies = []
    for channel in range(2):
        put = functools.partial(put_window, total, channel)
        put(rows[other] + HALF + start, cols[other], from_outer[channel].astype(F32))
        for k in range(2):
            spot = next_spots[k]
            put(after[spot] + HALF + BAND, after[4 + spot], from_next[k, channel].astype(F32))
            spot = prev_spots[k]
            put(before[spot], before[4 + spot], from_prev[k, channel].astype(F32))
        copies.append(
            pltpu.make_async_copy(
                total.at[channel, pl.ds(HALF, BAND)], output.at[0, channel], sems.at[channel]
            )
        )
        copies[channel].start()
    for copy in copies:
        copy.wait()


def call(kernel, name, inputs, outputs, scratch=(), in_specs=None, out_specs=None, aliases={}, vmem=40, flops=1):
    scalars = [x for x in inputs if x.dtype == jnp.int32]
    return pl.pallas_call(
        kernel,
        name=name,
        out_shape=outputs,
        in_specs=in_specs or [SM] * len(scalars) + [VM] * (len(inputs) - len(scalars)),
        out_specs=out_specs or [VM] * len(outputs),
        scratch_shapes=list(scratch),
        input_output_aliases=aliases,
        cost_estimate=pl.CostEstimate(flops=flops, bytes_accessed=1, transcendentals=0),
        compiler_params=pltpu.CompilerParams(vmem_limit_bytes=vmem << 20),
    )(*inputs)


def arr(*shape, dtype=BF):
    return jax.ShapeDtypeStruct(shape, dtype)


def shards(objects, probes, amplitudes, prop_phase, scan_rows, scan_cols, probe_choice):
    route = routes(lax.axis_size("region"))
    move = lambda x, way: lax.ppermute(x, AXES, route[way])
    first, second = (jnp.asarray(t) for t in dft_blocks())
    wave = jnp.stack([jnp.cos(prop_phase), jnp.sin(prop_phase)])
    half = arr(2, HALF, SIDE)

    inband, low, high = call(
        inband_kernel, "inband", [scan_rows, scan_cols, objects],
        [arr(3, 2, HALF, SIDE), arr(2, HALF, COLS), arr(2, HALF, COLS)],
        [pltpu.SMEM((4,), jnp.int32), pltpu.SMEM((4,), jnp.int32), pltpu.VMEM((2, BAND, COLS), F32),
         pltpu.SemaphoreType.DMA((4,))],
        in_specs=[HB] * 3, vmem=56,
    )
    above = move(high, "next")
    below = move(low, "prev")
    mate_inband = move(inband, "mate")
    half0, half12, windows = call(
        outer_kernel, "outer", [scan_rows, scan_cols, objects, above, below],
        [half, arr(2, 2, HALF, SIDE), arr(3, 2, SIDE, SIDE)],
        [pltpu.VMEM((2, EXT, COLS), F32)],
    )
    mate0 = move(half0, "mate")
    mate12 = move(half12, "mate")
    scan, half0 = lax.optimization_barrier((jnp.concatenate([scan_rows, scan_cols]), half0))
    before = move(scan, "next")
    after = move(scan, "prev")
    mate0, before, after = lax.optimization_barrier((mate0, before, after))
    sent_outer, sent_inband, solo, edge = call(
        solo_kernel, "solo",
        [scan_rows, probe_choice, windows, mate_inband, mate0, probes, amplitudes, wave, first, second],
        [half, half, arr(2, SIDE, SIDE, dtype=F32), half],
        [pltpu.VMEM((2, 2, SIDE, SIDE), BF), pltpu.VMEM((2, 2, SIDE, SIDE), F32)],
    )
    from_outer = move(sent_outer, "mate")
    from_inband = move(sent_inband, "mate")
    shared, up, down = call(
        shared_kernel, "shared",
        [scan_rows, probe_choice, windows, mate_inband, mate12, probes, amplitudes, wave, first, second],
        [arr(2, 2, SIDE, SIDE, dtype=F32), half, half],
        [pltpu.VMEM((2, 2, 2, SIDE, SIDE), BF), pltpu.VMEM((2, 2, 2, SIDE, SIDE), F32)],
    )
    to_prev, to_next = call(
        edges_kernel, "edges", [edge, up, down, from_outer], [arr(2, 2, HALF, SIDE)] * 2
    )
    from_next = move(to_prev, "prev")
    from_prev = move(to_next, "next")
    (total,) = call(
        own_kernel, "own", [scan_rows, scan_cols, solo, shared, from_inband],
        [arr(2, EXT, COLS, dtype=F32)], flops=10**11,
    )
    _, gradient = call(
        rest_kernel, "rest",
        [scan_rows, scan_cols, after, before, total, from_outer, from_next, from_prev],
        [arr(2, EXT, COLS, dtype=F32), arr(1, 2, BAND, COLS, dtype=F32)],
        [pltpu.SemaphoreType.DMA((2,))],
        out_specs=[VM, HB],
        aliases={4: 0},
    )
    return gradient


def solution(mesh):
    return jax.shard_map(
        shards,
        mesh=mesh,
        in_specs=(
            P("cuts", None, "region", None),
            P(),
            P("region", None, None),
            P(),
            P("region"),
            P("region"),
            P("region"),
        ),
        out_specs=P("cuts", None, "region", None),
        check_vma=False,
    )
```

```python
import functools

import jax
import jax.numpy as jnp
import ml_dtypes
import numpy as np
from jax import lax
from jax.experimental import pallas as pl
from jax.experimental.pallas import tpu as pltpu
from jax.sharding import PartitionSpec as P

modulus_floor = 0.25
AXES = ("cuts", "region")
BF = jnp.bfloat16
F32 = jnp.float32
SIDE = 256
HALF = 128
BAND = 256
COLS = 1024
EXT = BAND + 2 * HALF
EDGE = 2 * HALF * COLS // 128
WIDE = SIDE + 128
VM = pl.BlockSpec(memory_space=pltpu.VMEM)
SM = pl.BlockSpec(memory_space=pltpu.SMEM)
HB = pl.BlockSpec(memory_space=pltpu.HBM)


def routes(regions):
    at = lambda c, r: c * regions + r % regions
    both = [(c, r) for c in range(2) for r in range(regions)]
    return {
        "mate": [(at(c, r), at(1 - c, r)) for c, r in both],
        "next": [(at(c, r), at(c, r + 1)) for c, r in both],
        "prev": [(at(c, r), at(c, r - 1)) for c, r in both],
        "early": [(at(c, r), at(c, r - 1 if c == 0 else r + 1)) for c, r in both],
        "late": [(at(c, r), at(c, r + 1 if c == 0 else r - 1)) for c, r in both],
    }


def dft_blocks():
    index = np.arange(SIDE)
    angles = (index[:, None] * index[None, :] % SIDE) * (2.0 * np.pi / SIDE)
    real = np.cos(angles) / np.sqrt(SIDE)
    imag = -np.sin(angles) / np.sqrt(SIDE)
    first = np.block([[real, -imag], [imag, real]]).astype(ml_dtypes.bfloat16)
    second = np.block([[real, imag], [-imag, real]]).astype(ml_dtypes.bfloat16)
    return first, second


def places(rows):
    up = [rows[i] < 0 for i in range(4)]
    first = lambda a, b: jnp.where(a, 0, jnp.where(b, 1, 2))
    last = lambda a, b: jnp.where(a, 3, jnp.where(b, 2, 1))
    no = [jnp.logical_not(u) for u in up]
    return first(up[0], up[1]), last(up[3], up[2]), first(no[0], no[1]), last(no[3], no[2])


def column_split(left):
    base = jnp.minimum(lax.shift_right_logical(left, 7), (COLS - WIDE) // 128) * 128
    return pl.multiple_of(base, 128), left - base


def row_split(top, most):
    base = jnp.minimum(lax.shift_right_logical(top, 3), most // 8) * 8
    return pl.multiple_of(base, 8), top - base


def cut_window(load, top, left, count, total):
    row_base, row_shift = row_split(top, total - count - 8)
    col_base, col_shift = column_split(left)
    block = load(pl.ds(row_base, count + 8), pl.ds(col_base, WIDE))
    block = pltpu.roll(block, lax.rem(count + 8 - row_shift, count + 8), 0)[:count]
    return pltpu.roll(block, lax.rem(WIDE - col_shift, WIDE), 1)[:, :SIDE]


def put_window(total_ref, channel, top, left, block):
    count = block.shape[0]
    row_base, row_shift = row_split(top, EXT - count - 8)
    col_base, col_shift = column_split(left)
    block = jnp.concatenate([block, jnp.zeros((count, WIDE - SIDE), F32)], axis=1)
    block = pltpu.roll(block, col_shift, 1)
    block = jnp.concatenate([block, jnp.zeros((8, WIDE), F32)], axis=0)
    block = pltpu.roll(block, row_shift, 0)
    where = (channel, pl.ds(row_base, count + 8), pl.ds(col_base, WIDE))
    total_ref[where] = total_ref[where] + block


def tagged(rows, cols, spots):
    line = lax.broadcasted_iota(jnp.int32, (16, 128), 0)
    lane = lax.broadcasted_iota(jnp.int32, (16, 128), 1)
    tile = jnp.zeros((16, 128), jnp.int32)
    for k, spot in enumerate(spots):
        left = cols[spot]
        parts = (rows[spot] + HALF, lax.shift_right_logical(left, 3), jnp.bitwise_and(left, 7))
        for n, part in enumerate(parts):
            tile = jnp.where((line == k) & (lane == n), part, tile)
    return tile.astype(F32).astype(BF)


def inband_kernel(rows_in, cols_in, objects_in, inband, early, late, objects, rows, cols, sems):
    cut = lax.axis_index("cuts")
    copies = [
        pltpu.make_async_copy(rows_in, rows, sems.at[0]),
        pltpu.make_async_copy(cols_in, cols, sems.at[1]),
        pltpu.make_async_copy(objects_in.at[0, 0], objects.at[0], sems.at[2]),
        pltpu.make_async_copy(objects_in.at[0, 1], objects.at[1], sems.at[3]),
    ]
    for copy in copies:
        copy.start()
    copies[0].wait()
    copies[1].wait()
    u0, u1, l0, l1 = places(rows)
    up = cut == 0
    early[EDGE:] = tagged(rows, cols, (jnp.where(up, u0, l0), jnp.where(up, u1, l1)))
    late[EDGE:] = tagged(rows, cols, (jnp.where(up, l0, u0), jnp.where(up, l1, u1)))
    start = pl.multiple_of(jnp.where(up, 0, HALF), HALF)
    spots = [(jnp.where(up, l1, u1), jnp.where(up, 0, HALF)), (u0, HALF), (l0, 0)]
    for channel in range(2):
        copies[2 + channel].wait()
        for k in range(COLS // 128):
            where = pl.ds((channel * (COLS // 128) + k) * HALF, HALF)
            lanes = slice(128 * k, 128 * (k + 1))
            early[where] = objects[channel, pl.ds(start, HALF), lanes].astype(BF)
            late[where] = objects[channel, pl.ds(HALF - start, HALF), lanes].astype(BF)
        for slot, (place, offset) in enumerate(spots):
            inband[slot, channel] = cut_window(
                lambda r, c: objects[channel, r, c], rows[place] + offset, cols[place], HALF, BAND
            ).astype(BF)


def spread(target, channel, start, edge):
    for k in range(COLS // 128):
        target[channel, pl.ds(start, HALF), 128 * k : 128 * (k + 1)] = edge[
            pl.ds((channel * (COLS // 128) + k) * HALF, HALF)
        ].astype(F32)


def first_kernel(rows, cols, objects, early, half0, near):
    cut = lax.axis_index("cuts")
    u0, u1, l0, l1 = places(rows)
    other = jnp.where(cut == 0, l1, u1)
    start = pl.multiple_of(jnp.where(cut == 0, HALF, 0), HALF)
    top = rows[other] + jnp.where(cut == 0, 0, HALF)
    for channel in range(2):
        spread(near, channel, start, early)
        near[channel, pl.ds(HALF - start, HALF)] = objects[channel, pl.ds(start, HALF)]
        half0[channel] = cut_window(
            lambda r, c: near[channel, r, c], top, cols[other], HALF, BAND
        ).astype(BF)


def outer_kernel(rows, cols, objects, early, late, half12, windows, ext):
    cut = lax.axis_index("cuts")
    u0, u1, l0, l1 = places(rows)
    solo = jnp.where(cut == 0, u1, l1)
    far = HALF + BAND
    start = pl.multiple_of(jnp.where(cut == 0, far, 0), HALF)
    for channel in range(2):
        spread(ext, channel, start, early)
        spread(ext, channel, far - start, late)
        ext[channel, HALF:far] = objects[channel]
        load = lambda r, c: ext[channel, r, c]
        for slot, place in enumerate((solo, u0, l0)):
            window = cut_window(load, rows[place] + HALF, cols[place], SIDE, EXT).astype(BF)
            windows[slot, channel] = window
            if slot == 1:
                half12[0, channel] = window[:HALF]
            if slot == 2:
                half12[1, channel] = window[HALF:]


def decode_kernel(early, late, spots):
    line = lax.broadcasted_iota(jnp.int32, (16, 128), 0)
    lane = lax.broadcasted_iota(jnp.int32, (16, 128), 1)
    for n, edge in enumerate((early, late)):
        tile = edge[EDGE:].astype(F32)
        left = jnp.where(lane == 1, tile * 8.0, jnp.where(lane == 2, tile, 0.0))
        top = jnp.where(lane == 0, tile, 0.0)
        for k in range(2):
            for m, part in enumerate((top, left)):
                spots[4 * n + 2 * k + m] = jnp.sum(jnp.where(line == k, part, 0.0)).astype(jnp.int32)


def transform(fields, left, right):
    count = len(fields)
    stacked = jnp.concatenate(
        [jnp.concatenate([f[part].astype(BF) for f in fields], axis=1) for part in range(2)], axis=0
    )
    middle = jnp.dot(left, stacked, preferred_element_type=F32).astype(BF)
    spans = [slice(SIDE * k, SIDE * (k + 1)) for k in range(count)]
    middle = jnp.concatenate(
        [jnp.concatenate([middle[:SIDE, s], middle[SIDE:, s]], axis=1) for s in spans], axis=0
    )
    result = jnp.dot(middle, right, preferred_element_type=F32)
    return [(result[s, :SIDE], result[s, SIDE:]) for s in spans]


def times(a, b):
    return a[0] * b[0] - a[1] * b[1], a[0] * b[1] + a[1] * b[0]


def conj_times(a, b):
    return a[0] * b[0] + a[1] * b[1], a[0] * b[1] - a[1] * b[0]


def wide(pair):
    return pair[0].astype(F32), pair[1].astype(F32)


def chain(incoming, patches, measured, wave, first, second, store):
    spots = range(len(incoming))
    propagator = (wave[0], wave[1])
    fields = [times(wide(incoming[k]()), patches[k](0)) for k in spots]
    fields = [times(propagator, f) for f in transform(fields, first, second)]
    psi = [(f[0].astype(BF), f[1].astype(BF)) for f in transform(fields, second, first)]
    fields = [times(wide(psi[k]), patches[k](1)) for k in spots]
    detected = []
    for k, (real, imag) in enumerate(transform(fields, first, second)):
        modulus = jnp.sqrt(real * real + imag * imag)
        factor = 1.0 - measured[k]() / jnp.maximum(modulus, modulus_floor)
        detected.append((real * factor, imag * factor))
    arriving = [(f[0].astype(BF), f[1].astype(BF)) for f in transform(detected, second, first)]
    arriving = [wide(f) for f in arriving]
    for k in spots:
        store(k, 1, conj_times(wide(psi[k]), arriving[k]))
    fields = [conj_times(patches[k](1), arriving[k]) for k in spots]
    fields = [conj_times(propagator, f) for f in transform(fields, first, second)]
    for k, (real, imag) in enumerate(transform(fields, second, first)):
        arrived = real.astype(BF).astype(F32), imag.astype(BF).astype(F32)
        store(k, 0, conj_times(wide(incoming[k]()), arrived))


def fill_patches(held, own, inband, outer, cut, start):
    for channel in range(2):
        held[cut, channel] = own[channel]
        held[1 - cut, channel, pl.ds(start, HALF)] = outer[channel]
        held[1 - cut, channel, pl.ds(HALF - start, HALF)] = inband[channel]


def patch_of(held):
    return lambda which: wide((held[which, 0], held[which, 1]))


def probe_of(probes, choice):
    return lambda: (probes[choice, 0], probes[choice, 1])


def solo_kernel(
    rows, picks, windows, inband, outer, probes, amplitudes, wave, first, second,
    sent_outer, sent_inband, kept, edge, held, made,
):
    cut = lax.axis_index("cuts")
    u0, u1, l0, l1 = places(rows)
    place = jnp.where(cut == 0, u1, l1)
    start = pl.multiple_of(jnp.where(cut == 0, 0, HALF), HALF)
    fill_patches(held, windows.at[0], inband.at[0], outer, cut, start)

    def store(k, which, value):
        made[which, 0], made[which, 1] = value

    chain(
        [probe_of(probes, picks[place])], [patch_of(held)], [lambda: amplitudes[place]],
        wave, first[...], second[...], store,
    )
    for channel in range(2):
        sent_outer[channel] = made[1 - cut, channel, pl.ds(start, HALF)].astype(BF)
        sent_inband[channel] = made[1 - cut, channel, pl.ds(HALF - start, HALF)].astype(BF)
        kept[channel] = made[cut, channel]
        edge[channel] = made[cut, channel, pl.ds(start, HALF)].astype(BF)


def shared_kernel(
    rows, picks, windows, inband, outer, probes, amplitudes, wave, first, second,
    kept, edge_up, edge_low, held, made,
):
    cut = lax.axis_index("cuts")
    u0, u1, l0, l1 = places(rows)
    fill_patches(held.at[0], windows.at[1], inband.at[1], outer.at[0], cut, 0)
    fill_patches(held.at[1], windows.at[2], inband.at[2], outer.at[1], cut, HALF)

    def store(k, which, value):
        made[k, which, 0], made[k, which, 1] = value

    chain(
        [probe_of(probes, picks[u0]), probe_of(probes, picks[l0])],
        [patch_of(held.at[0]), patch_of(held.at[1])],
        [lambda: amplitudes[u0], lambda: amplitudes[l0]],
        wave, first[...], second[...], store,
    )
    for channel in range(2):
        for k in range(2):
            kept[k, channel] = made[k, cut, channel]
        edge_up[channel] = made[0, cut, channel, :HALF].astype(BF)
        edge_low[channel] = made[1, cut, channel, HALF:].astype(BF)


def edges_kernel(solo, up, low, relay, to_prev, to_next):
    cut = lax.axis_index("cuts")
    to_prev[0] = up[...]
    to_next[0] = low[...]

    @pl.when(cut == 0)
    def _():
        to_prev[1] = solo[...]
        to_next[1] = relay[...]

    @pl.when(cut == 1)
    def _():
        to_prev[1] = relay[...]
        to_next[1] = solo[...]


def own_kernel(rows, cols, solo, shared, from_inband, total):
    cut = lax.axis_index("cuts")
    u0, u1, l0, l1 = places(rows)
    own = jnp.where(cut == 0, u1, l1)
    other = jnp.where(cut == 0, l1, u1)
    start = jnp.where(cut == 0, HALF, 0)
    total[...] = jnp.zeros_like(total)
    for channel in range(2):
        put = functools.partial(put_window, total, channel)
        put(rows[own] + HALF, cols[own], solo[channel])
        put(rows[u0] + HALF, cols[u0], shared[0, channel])
        put(rows[l0] + HALF, cols[l0], shared[1, channel])
        put(rows[other] + 2 * HALF - start, cols[other], from_inband[channel].astype(F32))


def rest_kernel(rows, cols, spots, given, from_outer, from_next, from_prev, total, output, sems):
    cut = lax.axis_index("cuts")
    u0, u1, l0, l1 = places(rows)
    other = jnp.where(cut == 0, l1, u1)
    start = jnp.where(cut == 0, HALF, 0)
    after = jnp.where(cut == 0, 0, 4)
    before = 4 - after
    copies = []
    for channel in range(2):
        put = functools.partial(put_window, total, channel)
        put(rows[other] + HALF + start, cols[other], from_outer[channel].astype(F32))
        for k in range(2):
            top, left = spots[after + 2 * k] + BAND, spots[after + 2 * k + 1]
            put(top, left, from_next[k, channel].astype(F32))
            top, left = spots[before + 2 * k] - HALF, spots[before + 2 * k + 1]
            put(top, left, from_prev[k, channel].astype(F32))
        copies.append(
            pltpu.make_async_copy(
                total.at[channel, pl.ds(HALF, BAND)], output.at[0, channel], sems.at[channel]
            )
        )
        copies[channel].start()
    for copy in copies:
        copy.wait()


def call(kernel, name, inputs, outputs, scratch=(), in_specs=None, out_specs=None, aliases={}, vmem=40, flops=1):
    scalars = [x for x in inputs if x.dtype == jnp.int32]
    return pl.pallas_call(
        kernel,
        name=name,
        out_shape=outputs,
        in_specs=in_specs or [SM] * len(scalars) + [VM] * (len(inputs) - len(scalars)),
        out_specs=out_specs or [VM] * len(outputs),
        scratch_shapes=list(scratch),
        input_output_aliases=aliases,
        cost_estimate=pl.CostEstimate(flops=flops, bytes_accessed=1, transcendentals=0),
        compiler_params=pltpu.CompilerParams(vmem_limit_bytes=vmem << 20),
    )(*inputs)


def arr(*shape, dtype=BF):
    return jax.ShapeDtypeStruct(shape, dtype)


def shards(objects, probes, amplitudes, prop_phase, scan_rows, scan_cols, probe_choice):
    route = routes(lax.axis_size("region"))
    move = lambda x, way: lax.ppermute(x, AXES, route[way])
    first, second = (jnp.asarray(t) for t in dft_blocks())
    wave = jnp.stack([jnp.cos(prop_phase), jnp.sin(prop_phase)])
    half = arr(2, HALF, SIDE)

    inband, early, late, band, rows, cols = call(
        inband_kernel, "inband",
        [pltpu.with_memory_space_constraint(x, pltpu.HBM) for x in (scan_rows, scan_cols, objects)],
        [arr(3, 2, HALF, SIDE), arr(EDGE + 16, 128), arr(EDGE + 16, 128),
         arr(2, BAND, COLS, dtype=F32), arr(4, dtype=jnp.int32), arr(4, dtype=jnp.int32)],
        [pltpu.SemaphoreType.DMA((4,))],
        in_specs=[HB] * 3, out_specs=[VM] * 4 + [SM] * 2, vmem=50,
    )
    early = move(early, "early")
    late = move(late, "late")
    mate_inband = move(inband, "mate")
    (half0,) = call(
        first_kernel, "first", [rows, cols, band, early], [half],
        [pltpu.VMEM((2, BAND, COLS), F32)],
    )
    mate0 = move(half0, "mate")
    half12, windows = call(
        outer_kernel, "outer", [rows, cols, band, early, late],
        [arr(2, 2, HALF, SIDE), arr(3, 2, SIDE, SIDE)],
        [pltpu.VMEM((2, EXT, COLS), F32)],
    )
    mate12 = move(half12, "mate")
    (spots,) = call(
        decode_kernel, "decode", [early, late], [arr(8, dtype=jnp.int32)], out_specs=[SM]
    )
    sent_outer, sent_inband, solo, edge = call(
        solo_kernel, "solo",
        [rows, probe_choice, windows, mate_inband, mate0, probes, amplitudes, wave, first, second],
        [half, half, arr(2, SIDE, SIDE, dtype=F32), half],
        [pltpu.VMEM((2, 2, SIDE, SIDE), BF), pltpu.VMEM((2, 2, SIDE, SIDE), F32)],
    )
    from_outer = move(sent_outer, "mate")
    from_inband = move(sent_inband, "mate")
    shared, up, down = call(
        shared_kernel, "shared",
        [rows, probe_choice, windows, mate_inband, mate12, probes, amplitudes, wave, first, second],
        [arr(2, 2, SIDE, SIDE, dtype=F32), half, half],
        [pltpu.VMEM((2, 2, 2, SIDE, SIDE), BF), pltpu.VMEM((2, 2, 2, SIDE, SIDE), F32)],
    )
    to_prev, to_next = call(
        edges_kernel, "edges", [edge, up, down, from_outer], [arr(2, 2, HALF, SIDE)] * 2
    )
    from_next = move(to_prev, "prev")
    from_prev = move(to_next, "next")
    (total,) = call(
        own_kernel, "own", [rows, cols, solo, shared, from_inband],
        [arr(2, EXT, COLS, dtype=F32)], flops=10**11,
    )
    _, gradient = call(
        rest_kernel, "rest",
        [rows, cols, spots, total, from_outer, from_next, from_prev],
        [arr(2, EXT, COLS, dtype=F32), arr(1, 2, BAND, COLS, dtype=F32)],
        [pltpu.SemaphoreType.DMA((2,))],
        out_specs=[VM, HB],
        aliases={3: 0},
    )
    return gradient


def solution(mesh):
    return jax.shard_map(
        shards,
        mesh=mesh,
        in_specs=(
            P("cuts", None, "region", None),
            P(),
            P("region", None, None),
            P(),
            P("region"),
            P("region"),
            P("region"),
        ),
        out_specs=P("cuts", None, "region", None),
        check_vma=False,
    )
```

```python
import functools

import jax
import jax.numpy as jnp
import ml_dtypes
import numpy as np
from jax import lax
from jax.experimental import pallas as pl
from jax.experimental.pallas import tpu as pltpu
from jax.sharding import PartitionSpec as P

modulus_floor = 0.25
AXES = ("cuts", "region")
BF = jnp.bfloat16
F32 = jnp.float32
SIDE = 256
HALF = 128
BAND = 256
COLS = 1024
EXT = BAND + 2 * HALF
EDGE = 2 * HALF * COLS // 128
WIDE = SIDE + 128
VM = pl.BlockSpec(memory_space=pltpu.VMEM)
SM = pl.BlockSpec(memory_space=pltpu.SMEM)
HB = pl.BlockSpec(memory_space=pltpu.HBM)


def routes(regions):
    at = lambda c, r: c * regions + r % regions
    both = [(c, r) for c in range(2) for r in range(regions)]
    return {
        "mate": [(at(c, r), at(1 - c, r)) for c, r in both],
        "early": [(at(c, r), at(c, r - 1 if c == 0 else r + 1)) for c, r in both],
        "late": [(at(c, r), at(c, r + 1 if c == 0 else r - 1)) for c, r in both],
    }


def dft_blocks():
    index = np.arange(SIDE)
    angles = (index[:, None] * index[None, :] % SIDE) * (2.0 * np.pi / SIDE)
    real = np.cos(angles) / np.sqrt(SIDE)
    imag = -np.sin(angles) / np.sqrt(SIDE)
    first = np.block([[real, -imag], [imag, real]]).astype(ml_dtypes.bfloat16)
    second = np.block([[real, imag], [-imag, real]]).astype(ml_dtypes.bfloat16)
    return first, second


def places(rows):
    up = [rows[i] < 0 for i in range(4)]
    first = lambda a, b: jnp.where(a, 0, jnp.where(b, 1, 2))
    last = lambda a, b: jnp.where(a, 3, jnp.where(b, 2, 1))
    no = [jnp.logical_not(u) for u in up]
    return first(up[0], up[1]), last(up[3], up[2]), first(no[0], no[1]), last(no[3], no[2])


def column_split(left):
    base = jnp.minimum(lax.shift_right_logical(left, 7), (COLS - WIDE) // 128) * 128
    return pl.multiple_of(base, 128), left - base


def row_split(top, most):
    base = jnp.minimum(lax.shift_right_logical(top, 3), most // 8) * 8
    return pl.multiple_of(base, 8), top - base


def cut_window(load, top, left, count, total):
    row_base, row_shift = row_split(top, total - count - 8)
    col_base, col_shift = column_split(left)
    block = load(pl.ds(row_base, count + 8), pl.ds(col_base, WIDE))
    block = pltpu.roll(block, lax.rem(count + 8 - row_shift, count + 8), 0)[:count]
    return pltpu.roll(block, lax.rem(WIDE - col_shift, WIDE), 1)[:, :SIDE]


def put_window(total_ref, channel, top, left, block):
    count = block.shape[0]
    row_base, row_shift = row_split(top, EXT - count - 8)
    col_base, col_shift = column_split(left)
    block = jnp.concatenate([block, jnp.zeros((count, WIDE - SIDE), F32)], axis=1)
    block = pltpu.roll(block, col_shift, 1)
    block = jnp.concatenate([block, jnp.zeros((8, WIDE), F32)], axis=0)
    block = pltpu.roll(block, row_shift, 0)
    where = (channel, pl.ds(row_base, count + 8), pl.ds(col_base, WIDE))
    total_ref[where] = total_ref[where] + block


def tagged(rows, cols, spots):
    line = lax.broadcasted_iota(jnp.int32, (16, 128), 0)
    lane = lax.broadcasted_iota(jnp.int32, (16, 128), 1)
    tile = jnp.zeros((16, 128), jnp.int32)
    for k, spot in enumerate(spots):
        left = cols[spot]
        parts = (rows[spot] + HALF, lax.shift_right_logical(left, 3), jnp.bitwise_and(left, 7))
        for n, part in enumerate(parts):
            tile = jnp.where((line == k) & (lane == n), part, tile)
    return tile.astype(F32).astype(BF)


def edge_kernel(rows_in, cols_in, objects_in, early, late, objects, rows, cols, sems):
    cut = lax.axis_index("cuts")
    copies = [
        pltpu.make_async_copy(rows_in, rows, sems.at[0]),
        pltpu.make_async_copy(cols_in, cols, sems.at[1]),
        pltpu.make_async_copy(objects_in.at[0, 0], objects.at[0], sems.at[2]),
        pltpu.make_async_copy(objects_in.at[0, 1], objects.at[1], sems.at[3]),
    ]
    for copy in copies:
        copy.start()
    copies[0].wait()
    copies[1].wait()
    u0, u1, l0, l1 = places(rows)
    up = cut == 0
    early[EDGE:] = tagged(rows, cols, (jnp.where(up, u0, l0), jnp.where(up, u1, l1)))
    late[EDGE:] = tagged(rows, cols, (jnp.where(up, l0, u0), jnp.where(up, l1, u1)))
    start = pl.multiple_of(jnp.where(up, 0, HALF), HALF)
    for channel in range(2):
        copies[2 + channel].wait()
        for k in range(COLS // 128):
            where = pl.ds((channel * (COLS // 128) + k) * HALF, HALF)
            lanes = slice(128 * k, 128 * (k + 1))
            early[where] = objects[channel, pl.ds(start, HALF), lanes].astype(BF)
            late[where] = objects[channel, pl.ds(HALF - start, HALF), lanes].astype(BF)


def cut_pair(rows, cols, objects, edge, lower, spots, outputs, near):
    start = pl.multiple_of(jnp.where(lower, BAND, 0), HALF)
    own = pl.multiple_of(jnp.where(lower, 0, HALF), HALF)
    for channel in range(2):
        for k in range(COLS // 128):
            near[channel, pl.ds(start, HALF), 128 * k : 128 * (k + 1)] = edge[
                pl.ds((channel * (COLS // 128) + k) * HALF, HALF)
            ].astype(F32)
        near[channel, pl.ds(own, BAND)] = objects[channel]
        for spot, output in zip(spots, outputs):
            output[channel] = cut_window(
                lambda r, c: near[channel, r, c], rows[spot] + own, cols[spot], SIDE, BAND + HALF
            ).astype(BF)


def mate_kernel(rows, cols, objects, early, window0, window1, near):
    lower = lax.axis_index("cuts") == 0
    u0, u1, l0, l1 = places(rows)
    spots = jnp.where(lower, l0, u0), jnp.where(lower, l1, u1)
    cut_pair(rows, cols, objects, early, lower, spots, (window0, window1), near)


def own_windows_kernel(rows, cols, objects, early, late, window0, window1, spots, near):
    lower = lax.axis_index("cuts") == 1
    u0, u1, l0, l1 = places(rows)
    mine = jnp.where(lower, l0, u0), jnp.where(lower, l1, u1)
    cut_pair(rows, cols, objects, late, lower, mine, (window0, window1), near)
    decode(early, late, spots)


def decode(early, late, spots):
    line = lax.broadcasted_iota(jnp.int32, (16, 128), 0)
    lane = lax.broadcasted_iota(jnp.int32, (16, 128), 1)
    for n, edge in enumerate((early, late)):
        tile = edge[EDGE:].astype(F32)
        left = jnp.where(lane == 1, tile * 8.0, jnp.where(lane == 2, tile, 0.0))
        top = jnp.where(lane == 0, tile, 0.0)
        for k in range(2):
            for m, part in enumerate((top, left)):
                spots[4 * n + 2 * k + m] = jnp.sum(jnp.where(line == k, part, 0.0)).astype(jnp.int32)


def transform(fields, left, right):
    count = len(fields)
    stacked = jnp.concatenate(
        [jnp.concatenate([f[part].astype(BF) for f in fields], axis=1) for part in range(2)], axis=0
    )
    middle = jnp.dot(left, stacked, preferred_element_type=F32).astype(BF)
    spans = [slice(SIDE * k, SIDE * (k + 1)) for k in range(count)]
    middle = jnp.concatenate(
        [jnp.concatenate([middle[:SIDE, s], middle[SIDE:, s]], axis=1) for s in spans], axis=0
    )
    result = jnp.dot(middle, right, preferred_element_type=F32)
    return [(result[s, :SIDE], result[s, SIDE:]) for s in spans]


def times(a, b):
    return a[0] * b[0] - a[1] * b[1], a[0] * b[1] + a[1] * b[0]


def conj_times(a, b):
    return a[0] * b[0] + a[1] * b[1], a[0] * b[1] - a[1] * b[0]


def wide(pair):
    return pair[0].astype(F32), pair[1].astype(F32)


def chain(incoming, patches, measured, wave, first, second, store):
    spots = range(len(incoming))
    propagator = (wave[0], wave[1])
    fields = [times(wide(incoming[k]()), patches[k](0)) for k in spots]
    fields = [times(propagator, f) for f in transform(fields, first, second)]
    psi = [(f[0].astype(BF), f[1].astype(BF)) for f in transform(fields, second, first)]
    fields = [times(wide(psi[k]), patches[k](1)) for k in spots]
    detected = []
    for k, (real, imag) in enumerate(transform(fields, first, second)):
        modulus = jnp.sqrt(real * real + imag * imag)
        factor = 1.0 - measured[k]() / jnp.maximum(modulus, modulus_floor)
        detected.append((real * factor, imag * factor))
    arriving = [(f[0].astype(BF), f[1].astype(BF)) for f in transform(detected, second, first)]
    arriving = [wide(f) for f in arriving]
    for k in spots:
        store(k, 1, conj_times(wide(psi[k]), arriving[k]))
    fields = [conj_times(patches[k](1), arriving[k]) for k in spots]
    fields = [conj_times(propagator, f) for f in transform(fields, first, second)]
    for k, (real, imag) in enumerate(transform(fields, second, first)):
        arrived = real.astype(BF).astype(F32), imag.astype(BF).astype(F32)
        store(k, 0, conj_times(wide(incoming[k]()), arrived))


def solo_kernel(
    number, rows, picks, own, mate, probes, amplitudes, wave, first, second, *refs
):
    if number == 0:
        sent_outer, sent_inband, kept, edge, held, made = refs
        edges = edge
    else:
        before, sent_outer, sent_inband, kept, both, held, made = refs
        both[0] = before[...]
        edges = both.at[1]
    cut = lax.axis_index("cuts")
    spots = places(rows)
    place = jnp.where(cut == 0, spots[number], spots[2 + number])
    start = pl.multiple_of(jnp.where(cut == 0, 0, HALF), HALF)
    held[cut] = own[...]
    held[1 - cut] = mate[...]

    def store(k, which, value):
        made[which, 0], made[which, 1] = value

    chain(
        [lambda: (probes[picks[place], 0], probes[picks[place], 1])],
        [lambda which: wide((held[which, 0], held[which, 1]))],
        [lambda: amplitudes[place]],
        wave, first[...], second[...], store,
    )
    for channel in range(2):
        sent_outer[channel] = made[1 - cut, channel, pl.ds(start, HALF)].astype(BF)
        sent_inband[channel] = made[1 - cut, channel, pl.ds(HALF - start, HALF)].astype(BF)
        kept[channel] = made[cut, channel]
        edges[channel] = made[cut, channel, pl.ds(start, HALF)].astype(BF)


def put_mate(put, rows, cols, number, outer, inband, channel):
    upper = lax.axis_index("cuts") == 1
    spots = places(rows)
    spot = jnp.where(upper, spots[number], spots[2 + number])
    start = jnp.where(upper, 0, HALF)
    put(rows[spot] + HALF + start, cols[spot], outer[channel].astype(F32))
    put(rows[spot] + 2 * HALF - start, cols[spot], inband[channel].astype(F32))


def own_kernel(rows, cols, kept0, kept1, outer, inband, total):
    cut = lax.axis_index("cuts")
    places_here = places(rows)
    total[...] = jnp.zeros_like(total)
    for channel in range(2):
        put = functools.partial(put_window, total, channel)
        for number, kept in enumerate((kept0, kept1)):
            spot = jnp.where(cut == 0, places_here[number], places_here[2 + number])
            put(rows[spot] + HALF, cols[spot], kept[channel])
        put_mate(put, rows, cols, 0, outer, inband, channel)


def rest_kernel(
    rows, cols, spots, given, outer, inband, edges, relay0, relay1, total, output, sems
):
    cut = lax.axis_index("cuts")
    shift = jnp.where(cut == 0, BAND, -HALF)
    copies = []
    for channel in range(2):
        put = functools.partial(put_window, total, channel)
        put_mate(put, rows, cols, 1, outer, inband, channel)
        for number, relay in enumerate((relay0, relay1)):
            k = 2 * number
            put(spots[k] + shift, spots[k + 1], edges[number, channel].astype(F32))
            put(spots[4 + k] + BAND - HALF - shift, spots[5 + k], relay[channel].astype(F32))
        copies.append(
            pltpu.make_async_copy(
                total.at[channel, pl.ds(HALF, BAND)], output.at[0, channel], sems.at[channel]
            )
        )
        copies[channel].start()
    for copy in copies:
        copy.wait()


def call(kernel, name, inputs, outputs, scratch=(), in_specs=None, out_specs=None, aliases={}, vmem=40, flops=1):
    scalars = [x for x in inputs if x.dtype == jnp.int32]
    return pl.pallas_call(
        kernel,
        name=name,
        out_shape=outputs,
        in_specs=in_specs or [SM] * len(scalars) + [VM] * (len(inputs) - len(scalars)),
        out_specs=out_specs or [VM] * len(outputs),
        scratch_shapes=list(scratch),
        input_output_aliases=aliases,
        cost_estimate=pl.CostEstimate(flops=flops, bytes_accessed=1, transcendentals=0),
        compiler_params=pltpu.CompilerParams(vmem_limit_bytes=vmem << 20),
    )(*inputs)


def arr(*shape, dtype=BF):
    return jax.ShapeDtypeStruct(shape, dtype)


def shards(objects, probes, amplitudes, prop_phase, scan_rows, scan_cols, probe_choice):
    route = routes(lax.axis_size("region"))
    move = lambda x, way: lax.ppermute(x, AXES, route[way])
    first, second = (jnp.asarray(t) for t in dft_blocks())
    wave = jnp.stack([jnp.cos(prop_phase), jnp.sin(prop_phase)])
    half = arr(2, HALF, SIDE)

    full = arr(2, SIDE, SIDE)
    near = pltpu.VMEM((2, BAND + HALF, COLS), F32)
    early, late, band, rows, cols = call(
        edge_kernel, "edge",
        [pltpu.with_memory_space_constraint(x, pltpu.HBM) for x in (scan_rows, scan_cols, objects)],
        [arr(EDGE + 16, 128), arr(EDGE + 16, 128),
         arr(2, BAND, COLS, dtype=F32), arr(4, dtype=jnp.int32), arr(4, dtype=jnp.int32)],
        [pltpu.SemaphoreType.DMA((4,))],
        in_specs=[HB] * 3, out_specs=[VM] * 3 + [SM] * 2, vmem=50,
    )
    early = move(early, "early")
    late = move(late, "late")
    sent = call(mate_kernel, "mate", [rows, cols, band, early], [full, full], [near])
    mates = [move(x, "mate") for x in sent]
    own0, own1, spots = call(
        own_windows_kernel, "windows", [rows, cols, band, early, late],
        [full, full, arr(8, dtype=jnp.int32)], [near], out_specs=[VM, VM, SM],
    )
    optics = [probes, amplitudes, wave, first, second]
    work = [pltpu.VMEM((2, 2, SIDE, SIDE), BF), pltpu.VMEM((2, 2, SIDE, SIDE), F32)]
    wide_full = arr(2, SIDE, SIDE, dtype=F32)
    outer0, inband0, kept0, edge0 = call(
        functools.partial(solo_kernel, 0), "solo0", [rows, probe_choice, own0, mates[0]] + optics,
        [half, half, wide_full, half], work,
    )
    outer0 = move(outer0, "mate")
    inband0 = move(inband0, "mate")
    outer1, inband1, kept1, edges = call(
        functools.partial(solo_kernel, 1), "solo1",
        [rows, probe_choice, own1, mates[1]] + optics + [edge0],
        [half, half, wide_full, arr(2, 2, HALF, SIDE)], work, flops=10**11,
    )
    outer1 = move(outer1, "mate")
    inband1 = move(inband1, "mate")
    edges = move(edges, "early")
    relay0 = move(outer0, "late")
    (total,) = call(
        own_kernel, "own", [rows, cols, kept0, kept1, outer0, inband0],
        [arr(2, EXT, COLS, dtype=F32)], flops=10**11,
    )
    total, outer1 = lax.optimization_barrier((total, outer1))
    relay1 = move(outer1, "late")
    _, gradient = call(
        rest_kernel, "rest",
        [rows, cols, spots, total, outer1, inband1, edges, relay0, relay1],
        [arr(2, EXT, COLS, dtype=F32), arr(1, 2, BAND, COLS, dtype=F32)],
        [pltpu.SemaphoreType.DMA((2,))],
        out_specs=[VM, HB],
        aliases={3: 0},
    )
    return gradient


def solution(mesh):
    return jax.shard_map(
        shards,
        mesh=mesh,
        in_specs=(
            P("cuts", None, "region", None),
            P(),
            P("region", None, None),
            P(),
            P("region"),
            P("region"),
            P("region"),
        ),
        out_specs=P("cuts", None, "region", None),
        check_vma=False,
    )
```

```python
import functools

import jax
import jax.numpy as jnp
import ml_dtypes
import numpy as np
from jax import lax
from jax.experimental import pallas as pl
from jax.experimental.pallas import tpu as pltpu
from jax.sharding import PartitionSpec as P

modulus_floor = 0.25
AXES = ("cuts", "region")
BF = jnp.bfloat16
F32 = jnp.float32
SIDE = 256
HALF = 128
BAND = 256
COLS = 1024
EXT = BAND + 2 * HALF
EDGE = 2 * HALF * COLS // 128
WIDE = SIDE + 128
VM = pl.BlockSpec(memory_space=pltpu.VMEM)
SM = pl.BlockSpec(memory_space=pltpu.SMEM)
HB = pl.BlockSpec(memory_space=pltpu.HBM)


def routes(regions):
    at = lambda c, r: c * regions + r % regions
    both = [(c, r) for c in range(2) for r in range(regions)]
    return {
        "mate": [(at(c, r), at(1 - c, r)) for c, r in both],
        "direct": [(at(c, r), at(1 - c, r - 1 if c == 0 else r + 1)) for c, r in both],
        "early": [(at(c, r), at(c, r - 1 if c == 0 else r + 1)) for c, r in both],
        "late": [(at(c, r), at(c, r + 1 if c == 0 else r - 1)) for c, r in both],
    }


def dft_blocks():
    index = np.arange(SIDE)
    angles = (index[:, None] * index[None, :] % SIDE) * (2.0 * np.pi / SIDE)
    real = np.cos(angles) / np.sqrt(SIDE)
    imag = -np.sin(angles) / np.sqrt(SIDE)
    first = np.block([[real, -imag], [imag, real]]).astype(ml_dtypes.bfloat16)
    second = np.block([[real, imag], [-imag, real]]).astype(ml_dtypes.bfloat16)
    return first, second


def places(rows):
    up = [rows[i] < 0 for i in range(4)]
    first = lambda a, b: jnp.where(a, 0, jnp.where(b, 1, 2))
    last = lambda a, b: jnp.where(a, 3, jnp.where(b, 2, 1))
    no = [jnp.logical_not(u) for u in up]
    return first(up[0], up[1]), last(up[3], up[2]), first(no[0], no[1]), last(no[3], no[2])


def column_split(left):
    base = jnp.minimum(lax.shift_right_logical(left, 7), (COLS - WIDE) // 128) * 128
    return pl.multiple_of(base, 128), left - base


def row_split(top, most):
    base = jnp.minimum(lax.shift_right_logical(top, 3), most // 8) * 8
    return pl.multiple_of(base, 8), top - base


def cut_window(load, top, left, count, total):
    row_base, row_shift = row_split(top, total - count - 8)
    col_base, col_shift = column_split(left)
    block = load(pl.ds(row_base, count + 8), pl.ds(col_base, WIDE))
    block = pltpu.roll(block, lax.rem(count + 8 - row_shift, count + 8), 0)[:count]
    return pltpu.roll(block, lax.rem(WIDE - col_shift, WIDE), 1)[:, :SIDE]


def put_window(total_ref, channel, top, left, block):
    count = block.shape[0]
    row_base, row_shift = row_split(top, EXT - count - 8)
    col_base, col_shift = column_split(left)
    block = jnp.concatenate([block, jnp.zeros((count, WIDE - SIDE), F32)], axis=1)
    block = pltpu.roll(block, col_shift, 1)
    block = jnp.concatenate([block, jnp.zeros((8, WIDE), F32)], axis=0)
    block = pltpu.roll(block, row_shift, 0)
    where = (channel, pl.ds(row_base, count + 8), pl.ds(col_base, WIDE))
    total_ref[where] = total_ref[where] + block


def tagged(rows, cols, spots):
    line = lax.broadcasted_iota(jnp.int32, (16, 128), 0)
    lane = lax.broadcasted_iota(jnp.int32, (16, 128), 1)
    tile = jnp.zeros((16, 128), jnp.int32)
    for k, spot in enumerate(spots):
        left = cols[spot]
        parts = (rows[spot] + HALF, lax.shift_right_logical(left, 3), jnp.bitwise_and(left, 7))
        for n, part in enumerate(parts):
            tile = jnp.where((line == k) & (lane == n), part, tile)
    return tile.astype(F32).astype(BF)


def edge_kernel(rows_in, cols_in, objects_in, early, late, objects, rows, cols, sems):
    cut = lax.axis_index("cuts")
    copies = [
        pltpu.make_async_copy(rows_in, rows, sems.at[0]),
        pltpu.make_async_copy(cols_in, cols, sems.at[1]),
        pltpu.make_async_copy(objects_in.at[0, 0], objects.at[0], sems.at[2]),
        pltpu.make_async_copy(objects_in.at[0, 1], objects.at[1], sems.at[3]),
    ]
    for copy in copies:
        copy.start()
    copies[0].wait()
    copies[1].wait()
    u0, u1, l0, l1 = places(rows)
    up = cut == 0
    early[EDGE:] = tagged(rows, cols, (jnp.where(up, u0, l0), jnp.where(up, u1, l1)))
    late[EDGE:] = tagged(rows, cols, (jnp.where(up, l0, u0), jnp.where(up, l1, u1)))
    start = pl.multiple_of(jnp.where(up, 0, HALF), HALF)
    for channel in range(2):
        copies[2 + channel].wait()
        for k in range(COLS // 128):
            where = pl.ds((channel * (COLS // 128) + k) * HALF, HALF)
            lanes = slice(128 * k, 128 * (k + 1))
            early[where] = objects[channel, pl.ds(start, HALF), lanes].astype(BF)
            late[where] = objects[channel, pl.ds(HALF - start, HALF), lanes].astype(BF)


def cut_pair(rows, cols, objects, edge, lower, spots, outputs, near):
    start = pl.multiple_of(jnp.where(lower, BAND, 0), HALF)
    own = pl.multiple_of(jnp.where(lower, 0, HALF), HALF)
    for channel in range(2):
        for k in range(COLS // 128):
            near[channel, pl.ds(start, HALF), 128 * k : 128 * (k + 1)] = edge[
                pl.ds((channel * (COLS // 128) + k) * HALF, HALF)
            ].astype(F32)
        near[channel, pl.ds(own, BAND)] = objects[channel]
        for spot, output in zip(spots, outputs):
            output[channel] = cut_window(
                lambda r, c: near[channel, r, c], rows[spot] + own, cols[spot], SIDE, BAND + HALF
            ).astype(BF)


def mate_kernel(rows, cols, objects, early, window0, window1, near):
    lower = lax.axis_index("cuts") == 0
    u0, u1, l0, l1 = places(rows)
    spots = jnp.where(lower, l0, u0), jnp.where(lower, l1, u1)
    cut_pair(rows, cols, objects, early, lower, spots, (window0, window1), near)


def own_windows_kernel(rows, cols, objects, early, late, window0, window1, spots, near):
    lower = lax.axis_index("cuts") == 1
    u0, u1, l0, l1 = places(rows)
    mine = jnp.where(lower, l0, u0), jnp.where(lower, l1, u1)
    cut_pair(rows, cols, objects, late, lower, mine, (window0, window1), near)
    decode(early, late, spots)


def decode(early, late, spots):
    line = lax.broadcasted_iota(jnp.int32, (16, 128), 0)
    lane = lax.broadcasted_iota(jnp.int32, (16, 128), 1)
    for n, edge in enumerate((early, late)):
        tile = edge[EDGE:].astype(F32)
        left = jnp.where(lane == 1, tile * 8.0, jnp.where(lane == 2, tile, 0.0))
        top = jnp.where(lane == 0, tile, 0.0)
        for k in range(2):
            for m, part in enumerate((top, left)):
                spots[4 * n + 2 * k + m] = jnp.sum(jnp.where(line == k, part, 0.0)).astype(jnp.int32)


def transform(fields, left, right):
    count = len(fields)
    stacked = jnp.concatenate(
        [jnp.concatenate([f[part].astype(BF) for f in fields], axis=1) for part in range(2)], axis=0
    )
    middle = jnp.dot(left, stacked, preferred_element_type=F32).astype(BF)
    spans = [slice(SIDE * k, SIDE * (k + 1)) for k in range(count)]
    middle = jnp.concatenate(
        [jnp.concatenate([middle[:SIDE, s], middle[SIDE:, s]], axis=1) for s in spans], axis=0
    )
    result = jnp.dot(middle, right, preferred_element_type=F32)
    return [(result[s, :SIDE], result[s, SIDE:]) for s in spans]


def times(a, b):
    return a[0] * b[0] - a[1] * b[1], a[0] * b[1] + a[1] * b[0]


def conj_times(a, b):
    return a[0] * b[0] + a[1] * b[1], a[0] * b[1] - a[1] * b[0]


def wide(pair):
    return pair[0].astype(F32), pair[1].astype(F32)


def chain(incoming, patches, measured, wave, first, second, store):
    spots = range(len(incoming))
    propagator = (wave[0], wave[1])
    fields = [times(wide(incoming[k]()), patches[k](0)) for k in spots]
    fields = [times(propagator, f) for f in transform(fields, first, second)]
    psi = [(f[0].astype(BF), f[1].astype(BF)) for f in transform(fields, second, first)]
    fields = [times(wide(psi[k]), patches[k](1)) for k in spots]
    detected = []
    for k, (real, imag) in enumerate(transform(fields, first, second)):
        modulus = jnp.sqrt(real * real + imag * imag)
        factor = 1.0 - measured[k]() / jnp.maximum(modulus, modulus_floor)
        detected.append((real * factor, imag * factor))
    arriving = [(f[0].astype(BF), f[1].astype(BF)) for f in transform(detected, second, first)]
    arriving = [wide(f) for f in arriving]
    for k in spots:
        store(k, 1, conj_times(wide(psi[k]), arriving[k]))
    fields = [conj_times(patches[k](1), arriving[k]) for k in spots]
    fields = [conj_times(propagator, f) for f in transform(fields, first, second)]
    for k, (real, imag) in enumerate(transform(fields, second, first)):
        arrived = real.astype(BF).astype(F32), imag.astype(BF).astype(F32)
        store(k, 0, conj_times(wide(incoming[k]()), arrived))


def solo_kernel(
    number, rows, picks, own, mate, probes, amplitudes, wave, first, second, *refs
):
    if number == 0:
        sent_outer, sent_inband, kept, edge, held, made = refs
        edges = edge
    else:
        before, sent_outer, sent_inband, kept, both, held, made = refs
        both[0] = before[...]
        edges = both.at[1]
    cut = lax.axis_index("cuts")
    spots = places(rows)
    place = jnp.where(cut == 0, spots[number], spots[2 + number])
    start = pl.multiple_of(jnp.where(cut == 0, 0, HALF), HALF)
    held[cut] = own[...]
    held[1 - cut] = mate[...]

    def store(k, which, value):
        made[which, 0], made[which, 1] = value

    chain(
        [lambda: (probes[picks[place], 0], probes[picks[place], 1])],
        [lambda which: wide((held[which, 0], held[which, 1]))],
        [lambda: amplitudes[place]],
        wave, first[...], second[...], store,
    )
    depth = sent_inband.shape[1]
    inner = pl.multiple_of(jnp.where(cut == 0, SIDE - depth, 0), 64)
    for channel in range(2):
        sent_outer[channel] = made[1 - cut, channel, pl.ds(start, HALF)].astype(BF)
        sent_inband[channel] = made[1 - cut, channel, pl.ds(inner, depth)].astype(BF)
        kept[channel] = made[cut, channel]
        edges[channel] = made[cut, channel, pl.ds(start, HALF)].astype(BF)


def put_inband(put, rows, cols, number, inband, channel):
    upper = lax.axis_index("cuts") == 1
    spots = places(rows)
    spot = jnp.where(upper, spots[number], spots[2 + number])
    skip = jnp.where(upper, SIDE - inband.shape[1], 0)
    put(rows[spot] + HALF + skip, cols[spot], inband[channel].astype(F32))
    return rows[spot] + HALF + jnp.where(upper, 0, HALF), cols[spot]


def own_kernel(rows, cols, kept0, kept1, outer, inband, total):
    cut = lax.axis_index("cuts")
    places_here = places(rows)
    total[...] = jnp.zeros_like(total)
    for channel in range(2):
        put = functools.partial(put_window, total, channel)
        for number, kept in enumerate((kept0, kept1)):
            spot = jnp.where(cut == 0, places_here[number], places_here[2 + number])
            put(rows[spot] + HALF, cols[spot], kept[channel])
        top, left = put_inband(put, rows, cols, 0, inband, channel)
        put(top, left, outer[channel].astype(F32))


def rest_kernel(
    rows, cols, spots, given, inband, edges, relay0, relay1, total, output, sems
):
    cut = lax.axis_index("cuts")
    shift = jnp.where(cut == 0, BAND, -HALF)
    copies = []
    for channel in range(2):
        put = functools.partial(put_window, total, channel)
        put_inband(put, rows, cols, 1, inband, channel)
        for number, relay in enumerate((relay0, relay1)):
            k = 2 * number
            put(spots[k] + shift, spots[k + 1], edges[number, channel].astype(F32))
            put(spots[4 + k] + BAND - HALF - shift, spots[5 + k], relay[channel].astype(F32))
        copies.append(
            pltpu.make_async_copy(
                total.at[channel, pl.ds(HALF, BAND)], output.at[0, channel], sems.at[channel]
            )
        )
        copies[channel].start()
    for copy in copies:
        copy.wait()


def call(kernel, name, inputs, outputs, scratch=(), in_specs=None, out_specs=None, aliases={}, vmem=40, flops=1):
    scalars = [x for x in inputs if x.dtype == jnp.int32]
    return pl.pallas_call(
        kernel,
        name=name,
        out_shape=outputs,
        in_specs=in_specs or [SM] * len(scalars) + [VM] * (len(inputs) - len(scalars)),
        out_specs=out_specs or [VM] * len(outputs),
        scratch_shapes=list(scratch),
        input_output_aliases=aliases,
        cost_estimate=pl.CostEstimate(flops=flops, bytes_accessed=1, transcendentals=0),
        compiler_params=pltpu.CompilerParams(vmem_limit_bytes=vmem << 20),
    )(*inputs)


def arr(*shape, dtype=BF):
    return jax.ShapeDtypeStruct(shape, dtype)


def shards(objects, probes, amplitudes, prop_phase, scan_rows, scan_cols, probe_choice):
    route = routes(lax.axis_size("region"))
    move = lambda x, way: lax.ppermute(x, AXES, route[way])
    first, second = (jnp.asarray(t) for t in dft_blocks())
    wave = jnp.stack([jnp.cos(prop_phase), jnp.sin(prop_phase)])
    half = arr(2, HALF, SIDE)

    full = arr(2, SIDE, SIDE)
    near = pltpu.VMEM((2, BAND + HALF, COLS), F32)
    early, late, band, rows, cols = call(
        edge_kernel, "edge",
        [pltpu.with_memory_space_constraint(x, pltpu.HBM) for x in (scan_rows, scan_cols, objects)],
        [arr(EDGE + 16, 128), arr(EDGE + 16, 128),
         arr(2, BAND, COLS, dtype=F32), arr(4, dtype=jnp.int32), arr(4, dtype=jnp.int32)],
        [pltpu.SemaphoreType.DMA((4,))],
        in_specs=[HB] * 3, out_specs=[VM] * 3 + [SM] * 2, vmem=50,
    )
    early = move(early, "early")
    late = move(late, "late")
    sent = call(mate_kernel, "mate", [rows, cols, band, early], [full, full], [near])
    *sent, late = lax.optimization_barrier((*sent, late))
    mates = [move(x, "mate") for x in sent]
    own0, own1, spots = call(
        own_windows_kernel, "windows", [rows, cols, band, early, late],
        [full, full, arr(8, dtype=jnp.int32)], [near], out_specs=[VM, VM, SM],
    )
    optics = [probes, amplitudes, wave, first, second]
    work = [pltpu.VMEM((2, 2, SIDE, SIDE), BF), pltpu.VMEM((2, 2, SIDE, SIDE), F32)]
    wide_full = arr(2, SIDE, SIDE, dtype=F32)
    outer0, inband0, kept0, edge0 = call(
        functools.partial(solo_kernel, 0), "solo0", [rows, probe_choice, own0, mates[0]] + optics,
        [half, half, wide_full, half], work,
    )
    outer0 = move(outer0, "mate")
    inband0 = move(inband0, "mate")
    outer1, inband1, kept1, edges = call(
        functools.partial(solo_kernel, 1), "solo1",
        [rows, probe_choice, own1, mates[1]] + optics + [edge0],
        [half, arr(2, HALF + 64, SIDE), wide_full, arr(2, 2, HALF, SIDE)], work, flops=10**11,
    )
    relay1 = move(outer1, "direct")
    inband1 = move(inband1, "mate")
    edges = move(edges, "early")
    relay0 = move(outer0, "late")
    (total,) = call(
        own_kernel, "own", [rows, cols, kept0, kept1, outer0, inband0],
        [arr(2, EXT, COLS, dtype=F32)], flops=10**11,
    )
    _, gradient = call(
        rest_kernel, "rest",
        [rows, cols, spots, total, inband1, edges, relay0, relay1],
        [arr(2, EXT, COLS, dtype=F32), arr(1, 2, BAND, COLS, dtype=F32)],
        [pltpu.SemaphoreType.DMA((2,))],
        out_specs=[VM, HB],
        aliases={3: 0},
    )
    return gradient


def solution(mesh):
    return jax.shard_map(
        shards,
        mesh=mesh,
        in_specs=(
            P("cuts", None, "region", None),
            P(),
            P("region", None, None),
            P(),
            P("region"),
            P("region"),
            P("region"),
        ),
        out_specs=P("cuts", None, "region", None),
        check_vma=False,
    )
```

```python
import functools

import jax
import jax.numpy as jnp
import ml_dtypes
import numpy as np
from jax import lax
from jax.experimental import pallas as pl
from jax.experimental.pallas import tpu as pltpu
from jax.sharding import PartitionSpec as P

modulus_floor = 0.25
AXES = ("cuts", "region")
BF = jnp.bfloat16
F32 = jnp.float32
SIDE = 256
HALF = 128
BAND = 256
COLS = 1024
EXT = BAND + 2 * HALF
EDGE = 2 * HALF * COLS // 128
WIDE = SIDE + 128
VM = pl.BlockSpec(memory_space=pltpu.VMEM)
SM = pl.BlockSpec(memory_space=pltpu.SMEM)
HB = pl.BlockSpec(memory_space=pltpu.HBM)


def routes(regions):
    at = lambda c, r: c * regions + r % regions
    both = [(c, r) for c in range(2) for r in range(regions)]
    return {
        "mate": [(at(c, r), at(1 - c, r)) for c, r in both],
        "direct": [(at(c, r), at(1 - c, r - 1 if c == 0 else r + 1)) for c, r in both],
        "early": [(at(c, r), at(c, r - 1 if c == 0 else r + 1)) for c, r in both],
        "late": [(at(c, r), at(c, r + 1 if c == 0 else r - 1)) for c, r in both],
    }


def dft_blocks():
    index = np.arange(SIDE)
    angles = (index[:, None] * index[None, :] % SIDE) * (2.0 * np.pi / SIDE)
    real = np.cos(angles) / np.sqrt(SIDE)
    imag = -np.sin(angles) / np.sqrt(SIDE)
    first = np.block([[real, -imag], [imag, real]]).astype(ml_dtypes.bfloat16)
    second = np.block([[real, imag], [-imag, real]]).astype(ml_dtypes.bfloat16)
    return first, second


def places(rows):
    up = [rows[i] < 0 for i in range(4)]
    first = lambda a, b: jnp.where(a, 0, jnp.where(b, 1, 2))
    last = lambda a, b: jnp.where(a, 3, jnp.where(b, 2, 1))
    no = [jnp.logical_not(u) for u in up]
    return first(up[0], up[1]), last(up[3], up[2]), first(no[0], no[1]), last(no[3], no[2])


def column_split(left):
    base = jnp.minimum(lax.shift_right_logical(left, 7), (COLS - WIDE) // 128) * 128
    return pl.multiple_of(base, 128), left - base


def row_split(top, most):
    base = jnp.minimum(lax.shift_right_logical(top, 3), most // 8) * 8
    return pl.multiple_of(base, 8), top - base


def cut_window(load, top, left, count, total):
    row_base, row_shift = row_split(top, total - count - 8)
    col_base, col_shift = column_split(left)
    block = load(pl.ds(row_base, count + 8), pl.ds(col_base, WIDE))
    block = pltpu.roll(block, lax.rem(count + 8 - row_shift, count + 8), 0)[:count]
    return pltpu.roll(block, lax.rem(WIDE - col_shift, WIDE), 1)[:, :SIDE]


def put_window(total_ref, channel, top, left, block):
    count = block.shape[0]
    row_base, row_shift = row_split(top, EXT - count - 8)
    col_base, col_shift = column_split(left)
    block = jnp.concatenate([block, jnp.zeros((count, WIDE - SIDE), F32)], axis=1)
    block = pltpu.roll(block, col_shift, 1)
    block = jnp.concatenate([block, jnp.zeros((8, WIDE), F32)], axis=0)
    block = pltpu.roll(block, row_shift, 0)
    where = (channel, pl.ds(row_base, count + 8), pl.ds(col_base, WIDE))
    total_ref[where] = total_ref[where] + block


def tagged(rows, cols, spots):
    line = lax.broadcasted_iota(jnp.int32, (16, 128), 0)
    lane = lax.broadcasted_iota(jnp.int32, (16, 128), 1)
    tile = jnp.zeros((16, 128), jnp.int32)
    for k, spot in enumerate(spots):
        left = cols[spot]
        parts = (rows[spot] + HALF, lax.shift_right_logical(left, 3), jnp.bitwise_and(left, 7))
        for n, part in enumerate(parts):
            tile = jnp.where((line == k) & (lane == n), part, tile)
    return tile.astype(F32).astype(BF)


def edge_kernel(rows_in, cols_in, objects_in, early, late, objects, rows, cols, sems):
    cut = lax.axis_index("cuts")
    copies = [
        pltpu.make_async_copy(rows_in, rows, sems.at[0]),
        pltpu.make_async_copy(cols_in, cols, sems.at[1]),
        pltpu.make_async_copy(objects_in.at[0, 0], objects.at[0], sems.at[2]),
        pltpu.make_async_copy(objects_in.at[0, 1], objects.at[1], sems.at[3]),
    ]
    for copy in copies:
        copy.start()
    copies[0].wait()
    copies[1].wait()
    u0, u1, l0, l1 = places(rows)
    up = cut == 0
    early[EDGE:] = tagged(rows, cols, (jnp.where(up, u0, l0), jnp.where(up, u1, l1)))
    late[EDGE:] = tagged(rows, cols, (jnp.where(up, l0, u0), jnp.where(up, l1, u1)))
    start = pl.multiple_of(jnp.where(up, 0, HALF), HALF)
    for channel in range(2):
        copies[2 + channel].wait()
        for k in range(COLS // 128):
            where = pl.ds((channel * (COLS // 128) + k) * HALF, HALF)
            lanes = slice(128 * k, 128 * (k + 1))
            early[where] = objects[channel, pl.ds(start, HALF), lanes].astype(BF)
            late[where] = objects[channel, pl.ds(HALF - start, HALF), lanes].astype(BF)


def cut_pair(rows, cols, objects, edge, lower, spots, outputs, near):
    start = pl.multiple_of(jnp.where(lower, BAND, 0), HALF)
    own = pl.multiple_of(jnp.where(lower, 0, HALF), HALF)
    for channel in range(2):
        for k in range(COLS // 128):
            near[channel, pl.ds(start, HALF), 128 * k : 128 * (k + 1)] = edge[
                pl.ds((channel * (COLS // 128) + k) * HALF, HALF)
            ].astype(F32)
        near[channel, pl.ds(own, BAND)] = objects[channel]
        for spot, output in zip(spots, outputs):
            output[channel] = cut_window(
                lambda r, c: near[channel, r, c], rows[spot] + own, cols[spot], SIDE, BAND + HALF
            ).astype(BF)


def mate_kernel(rows, cols, objects, early, window0, window1, near):
    lower = lax.axis_index("cuts") == 0
    u0, u1, l0, l1 = places(rows)
    spots = jnp.where(lower, l0, u0), jnp.where(lower, l1, u1)
    cut_pair(rows, cols, objects, early, lower, spots, (window0, window1), near)


def own_windows_kernel(rows, cols, objects, early, late, window0, window1, spots, near):
    lower = lax.axis_index("cuts") == 1
    u0, u1, l0, l1 = places(rows)
    mine = jnp.where(lower, l0, u0), jnp.where(lower, l1, u1)
    cut_pair(rows, cols, objects, late, lower, mine, (window0, window1), near)
    decode(early, late, spots)


def decode(early, late, spots):
    line = lax.broadcasted_iota(jnp.int32, (16, 128), 0)
    lane = lax.broadcasted_iota(jnp.int32, (16, 128), 1)
    for n, edge in enumerate((early, late)):
        tile = edge[EDGE:].astype(F32)
        left = jnp.where(lane == 1, tile * 8.0, jnp.where(lane == 2, tile, 0.0))
        top = jnp.where(lane == 0, tile, 0.0)
        for k in range(2):
            for m, part in enumerate((top, left)):
                spots[4 * n + 2 * k + m] = jnp.sum(jnp.where(line == k, part, 0.0)).astype(jnp.int32)


def transform(fields, left, right):
    count = len(fields)
    stacked = jnp.concatenate(
        [jnp.concatenate([f[part].astype(BF) for f in fields], axis=1) for part in range(2)], axis=0
    )
    middle = jnp.dot(left, stacked, preferred_element_type=F32).astype(BF)
    spans = [slice(SIDE * k, SIDE * (k + 1)) for k in range(count)]
    middle = jnp.concatenate(
        [jnp.concatenate([middle[:SIDE, s], middle[SIDE:, s]], axis=1) for s in spans], axis=0
    )
    result = jnp.dot(middle, right, preferred_element_type=F32)
    return [(result[s, :SIDE], result[s, SIDE:]) for s in spans]


def times(a, b):
    return a[0] * b[0] - a[1] * b[1], a[0] * b[1] + a[1] * b[0]


def conj_times(a, b):
    return a[0] * b[0] + a[1] * b[1], a[0] * b[1] - a[1] * b[0]


def wide(pair):
    return pair[0].astype(F32), pair[1].astype(F32)


def chain(incoming, patches, measured, wave, first, second, store):
    spots = range(len(incoming))
    propagator = (wave[0], wave[1])
    fields = [times(wide(incoming[k]()), patches[k](0)) for k in spots]
    fields = [times(propagator, f) for f in transform(fields, first, second)]
    psi = [(f[0].astype(BF), f[1].astype(BF)) for f in transform(fields, second, first)]
    fields = [times(wide(psi[k]), patches[k](1)) for k in spots]
    detected = []
    for k, (real, imag) in enumerate(transform(fields, first, second)):
        modulus = jnp.sqrt(real * real + imag * imag)
        factor = 1.0 - measured[k]() / jnp.maximum(modulus, modulus_floor)
        detected.append((real * factor, imag * factor))
    arriving = [(f[0].astype(BF), f[1].astype(BF)) for f in transform(detected, second, first)]
    arriving = [wide(f) for f in arriving]
    for k in spots:
        store(k, 1, conj_times(wide(psi[k]), arriving[k]))
    fields = [conj_times(patches[k](1), arriving[k]) for k in spots]
    fields = [conj_times(propagator, f) for f in transform(fields, first, second)]
    for k, (real, imag) in enumerate(transform(fields, second, first)):
        arrived = real.astype(BF).astype(F32), imag.astype(BF).astype(F32)
        store(k, 0, conj_times(wide(incoming[k]()), arrived))


def solo_kernel(
    number, rows, picks, own, mate, probes, amplitudes, wave, first, second, *refs
):
    if number == 0:
        sent, kept, edges, held, made = refs
        sent_outer, sent_inband = sent.at[0], sent.at[1]
    else:
        before, sent_outer, sent_inband, kept, both, held, made = refs
        both[0] = before[...]
        edges = both.at[1]
    cut = lax.axis_index("cuts")
    spots = places(rows)
    place = jnp.where(cut == 0, spots[number], spots[2 + number])
    start = pl.multiple_of(jnp.where(cut == 0, 0, HALF), HALF)
    held[cut] = own[...]
    held[1 - cut] = mate[...]

    def store(k, which, value):
        made[which, 0], made[which, 1] = value

    chain(
        [lambda: (probes[picks[place], 0], probes[picks[place], 1])],
        [lambda which: wide((held[which, 0], held[which, 1]))],
        [lambda: amplitudes[place]],
        wave, first[...], second[...], store,
    )
    depth = sent_inband.shape[1]
    inner = pl.multiple_of(jnp.where(cut == 0, SIDE - depth, 0), 64)
    for channel in range(2):
        sent_outer[channel] = made[1 - cut, channel, pl.ds(start, HALF)].astype(BF)
        sent_inband[channel] = made[1 - cut, channel, pl.ds(inner, depth)].astype(BF)
        kept[channel] = made[cut, channel]
        edges[channel] = made[cut, channel, pl.ds(start, HALF)].astype(BF)


def put_inband(put, rows, cols, number, inband, channel):
    upper = lax.axis_index("cuts") == 1
    spots = places(rows)
    spot = jnp.where(upper, spots[number], spots[2 + number])
    skip = jnp.where(upper, SIDE - inband.shape[1], 0)
    put(rows[spot] + HALF + skip, cols[spot], inband[channel].astype(F32))
    return rows[spot] + HALF + jnp.where(upper, 0, HALF), cols[spot]


def own_kernel(rows, cols, kept0, kept1, back, total):
    cut = lax.axis_index("cuts")
    places_here = places(rows)
    total[...] = jnp.zeros_like(total)
    for channel in range(2):
        put = functools.partial(put_window, total, channel)
        for number, kept in enumerate((kept0, kept1)):
            spot = jnp.where(cut == 0, places_here[number], places_here[2 + number])
            put(rows[spot] + HALF, cols[spot], kept[channel])
        top, left = put_inband(put, rows, cols, 0, back.at[1], channel)
        put(top, left, back[0, channel].astype(F32))


def rest_kernel(
    rows, cols, spots, given, inband, edges, relay0, relay1, total, output, sems
):
    cut = lax.axis_index("cuts")
    shift = jnp.where(cut == 0, BAND, -HALF)
    copies = []
    for channel in range(2):
        put = functools.partial(put_window, total, channel)
        put_inband(put, rows, cols, 1, inband, channel)
        for number, relay in enumerate((relay0, relay1)):
            k = 2 * number
            put(spots[k] + shift, spots[k + 1], edges[number, channel].astype(F32))
            put(spots[4 + k] + BAND - HALF - shift, spots[5 + k], relay[channel].astype(F32))
        copies.append(
            pltpu.make_async_copy(
                total.at[channel, pl.ds(HALF, BAND)], output.at[0, channel], sems.at[channel]
            )
        )
        copies[channel].start()
    for copy in copies:
        copy.wait()


def call(kernel, name, inputs, outputs, scratch=(), in_specs=None, out_specs=None, aliases={}, vmem=40, flops=1):
    scalars = [x for x in inputs if x.dtype == jnp.int32]
    return pl.pallas_call(
        kernel,
        name=name,
        out_shape=outputs,
        in_specs=in_specs or [SM] * len(scalars) + [VM] * (len(inputs) - len(scalars)),
        out_specs=out_specs or [VM] * len(outputs),
        scratch_shapes=list(scratch),
        input_output_aliases=aliases,
        cost_estimate=pl.CostEstimate(flops=flops, bytes_accessed=1, transcendentals=0),
        compiler_params=pltpu.CompilerParams(vmem_limit_bytes=vmem << 20),
    )(*inputs)


def arr(*shape, dtype=BF):
    return jax.ShapeDtypeStruct(shape, dtype)


def shards(objects, probes, amplitudes, prop_phase, scan_rows, scan_cols, probe_choice):
    route = routes(lax.axis_size("region"))
    move = lambda x, way: lax.ppermute(x, AXES, route[way])
    first, second = (jnp.asarray(t) for t in dft_blocks())
    wave = jnp.stack([jnp.cos(prop_phase), jnp.sin(prop_phase)])
    half = arr(2, HALF, SIDE)

    full = arr(2, SIDE, SIDE)
    near = pltpu.VMEM((2, BAND + HALF, COLS), F32)
    early, late, band, rows, cols = call(
        edge_kernel, "edge",
        [pltpu.with_memory_space_constraint(x, pltpu.HBM) for x in (scan_rows, scan_cols, objects)],
        [arr(EDGE + 16, 128), arr(EDGE + 16, 128),
         arr(2, BAND, COLS, dtype=F32), arr(4, dtype=jnp.int32), arr(4, dtype=jnp.int32)],
        [pltpu.SemaphoreType.DMA((4,))],
        in_specs=[HB] * 3, out_specs=[VM] * 3 + [SM] * 2, vmem=50,
    )
    early = move(early, "early")
    late = move(late, "late")
    sent = call(mate_kernel, "mate", [rows, cols, band, early], [full, full], [near])
    sent0, sent1, late = lax.optimization_barrier((*sent, late))
    mate0 = move(sent0, "mate")
    mate1 = move(sent1, "mate")
    own0, own1, spots = call(
        own_windows_kernel, "windows", [rows, cols, band, early, late],
        [full, full, arr(8, dtype=jnp.int32)], [near], out_specs=[VM, VM, SM],
    )
    optics = [probes, amplitudes, wave, first, second]
    work = [pltpu.VMEM((2, 2, SIDE, SIDE), BF), pltpu.VMEM((2, 2, SIDE, SIDE), F32)]
    wide_full = arr(2, SIDE, SIDE, dtype=F32)
    back0, kept0, edge0 = call(
        functools.partial(solo_kernel, 0), "solo0", [rows, probe_choice, own0, mate0] + optics,
        [arr(2, 2, HALF, SIDE), wide_full, half], work,
    )
    back0 = move(back0, "mate")
    outer1, inband1, kept1, edges = call(
        functools.partial(solo_kernel, 1), "solo1",
        [rows, probe_choice, own1, mate1] + optics + [edge0],
        [half, arr(2, HALF + 64, SIDE), wide_full, arr(2, 2, HALF, SIDE)], work, flops=10**11,
    )
    inband1 = move(inband1, "mate")
    outer1, back0 = lax.optimization_barrier((outer1, back0))
    relay1 = move(outer1, "direct")
    edges = move(edges, "early")
    relay0 = move(back0[0], "late")
    (total,) = call(
        own_kernel, "own", [rows, cols, kept0, kept1, back0],
        [arr(2, EXT, COLS, dtype=F32)], flops=10**11,
    )
    _, gradient = call(
        rest_kernel, "rest",
        [rows, cols, spots, total, inband1, edges, relay0, relay1],
        [arr(2, EXT, COLS, dtype=F32), arr(1, 2, BAND, COLS, dtype=F32)],
        [pltpu.SemaphoreType.DMA((2,))],
        out_specs=[VM, HB],
        aliases={3: 0},
    )
    return gradient


def solution(mesh):
    return jax.shard_map(
        shards,
        mesh=mesh,
        in_specs=(
            P("cuts", None, "region", None),
            P(),
            P("region", None, None),
            P(),
            P("region"),
            P("region"),
            P("region"),
        ),
        out_specs=P("cuts", None, "region", None),
        check_vma=False,
    )
```

```python
import functools

import jax
import jax.numpy as jnp
import ml_dtypes
import numpy as np
from jax import lax
from jax.experimental import pallas as pl
from jax.experimental.pallas import tpu as pltpu
from jax.sharding import PartitionSpec as P

modulus_floor = 0.25
AXES = ("cuts", "region")
BF = jnp.bfloat16
F32 = jnp.float32
SIDE = 256
HALF = 128
BAND = 256
COLS = 1024
EXT = BAND + 2 * HALF
EDGE = 2 * HALF * COLS // 128
WIDE = SIDE + 128
VM = pl.BlockSpec(memory_space=pltpu.VMEM)
SM = pl.BlockSpec(memory_space=pltpu.SMEM)
HB = pl.BlockSpec(memory_space=pltpu.HBM)


def routes(regions):
    at = lambda c, r: c * regions + r % regions
    both = [(c, r) for c in range(2) for r in range(regions)]
    return {
        "mate": [(at(c, r), at(1 - c, r)) for c, r in both],
        "direct": [(at(c, r), at(1 - c, r - 1 if c == 0 else r + 1)) for c, r in both],
        "early": [(at(c, r), at(c, r - 1 if c == 0 else r + 1)) for c, r in both],
        "late": [(at(c, r), at(c, r + 1 if c == 0 else r - 1)) for c, r in both],
    }


def dft_blocks():
    index = np.arange(SIDE)
    angles = (index[:, None] * index[None, :] % SIDE) * (2.0 * np.pi / SIDE)
    real = np.cos(angles) / np.sqrt(SIDE)
    imag = -np.sin(angles) / np.sqrt(SIDE)
    first = np.block([[real, -imag], [imag, real]]).astype(ml_dtypes.bfloat16)
    second = np.block([[real, imag], [-imag, real]]).astype(ml_dtypes.bfloat16)
    return first, second


def places(rows):
    up = [rows[i] < 0 for i in range(4)]
    first = lambda a, b: jnp.where(a, 0, jnp.where(b, 1, 2))
    last = lambda a, b: jnp.where(a, 3, jnp.where(b, 2, 1))
    no = [jnp.logical_not(u) for u in up]
    return first(up[0], up[1]), last(up[3], up[2]), first(no[0], no[1]), last(no[3], no[2])


def column_split(left):
    base = jnp.minimum(lax.shift_right_logical(left, 7), (COLS - WIDE) // 128) * 128
    return pl.multiple_of(base, 128), left - base


def row_split(top, most):
    base = jnp.minimum(lax.shift_right_logical(top, 3), most // 8) * 8
    return pl.multiple_of(base, 8), top - base


def cut_window(load, top, left, count, total):
    row_base, row_shift = row_split(top, total - count - 8)
    col_base, col_shift = column_split(left)
    block = load(pl.ds(row_base, count + 8), pl.ds(col_base, WIDE))
    block = pltpu.roll(block, lax.rem(count + 8 - row_shift, count + 8), 0)[:count]
    return pltpu.roll(block, lax.rem(WIDE - col_shift, WIDE), 1)[:, :SIDE]


def put_window(total_ref, channel, top, left, block):
    count = block.shape[0]
    row_base, row_shift = row_split(top, EXT - count - 8)
    col_base, col_shift = column_split(left)
    block = jnp.concatenate([block, jnp.zeros((count, WIDE - SIDE), F32)], axis=1)
    block = pltpu.roll(block, col_shift, 1)
    block = jnp.concatenate([block, jnp.zeros((8, WIDE), F32)], axis=0)
    block = pltpu.roll(block, row_shift, 0)
    where = (channel, pl.ds(row_base, count + 8), pl.ds(col_base, WIDE))
    total_ref[where] = total_ref[where] + block


def tagged(rows, cols, spots):
    line = lax.broadcasted_iota(jnp.int32, (16, 128), 0)
    lane = lax.broadcasted_iota(jnp.int32, (16, 128), 1)
    tile = jnp.zeros((16, 128), jnp.int32)
    for k, spot in enumerate(spots):
        left = cols[spot]
        parts = (rows[spot] + HALF, lax.shift_right_logical(left, 3), jnp.bitwise_and(left, 7))
        for n, part in enumerate(parts):
            tile = jnp.where((line == k) & (lane == n), part, tile)
    return tile.astype(F32).astype(BF)


def edge_kernel(rows_in, cols_in, objects_in, early, late, objects, rows, cols, sems):
    cut = lax.axis_index("cuts")
    copies = [
        pltpu.make_async_copy(rows_in, rows, sems.at[0]),
        pltpu.make_async_copy(cols_in, cols, sems.at[1]),
        pltpu.make_async_copy(objects_in.at[0, 0], objects.at[0], sems.at[2]),
        pltpu.make_async_copy(objects_in.at[0, 1], objects.at[1], sems.at[3]),
    ]
    for copy in copies:
        copy.start()
    copies[0].wait()
    copies[1].wait()
    u0, u1, l0, l1 = places(rows)
    up = cut == 0
    early[EDGE:] = tagged(rows, cols, (jnp.where(up, u0, l0), jnp.where(up, u1, l1)))
    late[EDGE:] = tagged(rows, cols, (jnp.where(up, l0, u0), jnp.where(up, l1, u1)))
    start = pl.multiple_of(jnp.where(up, 0, HALF), HALF)
    for channel in range(2):
        copies[2 + channel].wait()
        for k in range(COLS // 128):
            where = pl.ds((channel * (COLS // 128) + k) * HALF, HALF)
            lanes = slice(128 * k, 128 * (k + 1))
            early[where] = objects[channel, pl.ds(start, HALF), lanes].astype(BF)
            late[where] = objects[channel, pl.ds(HALF - start, HALF), lanes].astype(BF)


def cut_pair(rows, cols, objects, edge, lower, spots, outputs, near):
    start = pl.multiple_of(jnp.where(lower, BAND, 0), HALF)
    own = pl.multiple_of(jnp.where(lower, 0, HALF), HALF)
    for channel in range(2):
        for k in range(COLS // 128):
            near[channel, pl.ds(start, HALF), 128 * k : 128 * (k + 1)] = edge[
                pl.ds((channel * (COLS // 128) + k) * HALF, HALF)
            ].astype(F32)
        near[channel, pl.ds(own, BAND)] = objects[channel]
        for spot, output in zip(spots, outputs):
            output[channel] = cut_window(
                lambda r, c: near[channel, r, c], rows[spot] + own, cols[spot], SIDE, BAND + HALF
            ).astype(BF)


def mate_kernel(rows, cols, objects, early, window0, window1, near):
    lower = lax.axis_index("cuts") == 0
    u0, u1, l0, l1 = places(rows)
    spots = jnp.where(lower, l0, u0), jnp.where(lower, l1, u1)
    cut_pair(rows, cols, objects, early, lower, spots, (window0, window1), near)


def own_windows_kernel(rows, cols, objects, early, late, window0, window1, spots, near):
    lower = lax.axis_index("cuts") == 1
    u0, u1, l0, l1 = places(rows)
    mine = jnp.where(lower, l0, u0), jnp.where(lower, l1, u1)
    cut_pair(rows, cols, objects, late, lower, mine, (window0, window1), near)
    decode(early, late, spots)


def decode(early, late, spots):
    line = lax.broadcasted_iota(jnp.int32, (16, 128), 0)
    lane = lax.broadcasted_iota(jnp.int32, (16, 128), 1)
    for n, edge in enumerate((early, late)):
        tile = edge[EDGE:].astype(F32)
        left = jnp.where(lane == 1, tile * 8.0, jnp.where(lane == 2, tile, 0.0))
        top = jnp.where(lane == 0, tile, 0.0)
        for k in range(2):
            for m, part in enumerate((top, left)):
                spots[4 * n + 2 * k + m] = jnp.sum(jnp.where(line == k, part, 0.0)).astype(jnp.int32)


def transform(fields, left, right):
    count = len(fields)
    stacked = jnp.concatenate(
        [jnp.concatenate([f[part].astype(BF) for f in fields], axis=1) for part in range(2)], axis=0
    )
    middle = jnp.dot(left, stacked, preferred_element_type=F32).astype(BF)
    spans = [slice(SIDE * k, SIDE * (k + 1)) for k in range(count)]
    middle = jnp.concatenate(
        [jnp.concatenate([middle[:SIDE, s], middle[SIDE:, s]], axis=1) for s in spans], axis=0
    )
    result = jnp.dot(middle, right, preferred_element_type=F32)
    return [(result[s, :SIDE], result[s, SIDE:]) for s in spans]


def times(a, b):
    return a[0] * b[0] - a[1] * b[1], a[0] * b[1] + a[1] * b[0]


def conj_times(a, b):
    return a[0] * b[0] + a[1] * b[1], a[0] * b[1] - a[1] * b[0]


def wide(pair):
    return pair[0].astype(F32), pair[1].astype(F32)


def chain(incoming, patches, measured, wave, first, second, store):
    spots = range(len(incoming))
    propagator = (wave[0], wave[1])
    fields = [times(wide(incoming[k]()), patches[k](0)) for k in spots]
    fields = [times(propagator, f) for f in transform(fields, first, second)]
    psi = [(f[0].astype(BF), f[1].astype(BF)) for f in transform(fields, second, first)]
    fields = [times(wide(psi[k]), patches[k](1)) for k in spots]
    detected = []
    for k, (real, imag) in enumerate(transform(fields, first, second)):
        modulus = jnp.sqrt(real * real + imag * imag)
        factor = 1.0 - measured[k]() / jnp.maximum(modulus, modulus_floor)
        detected.append((real * factor, imag * factor))
    arriving = [(f[0].astype(BF), f[1].astype(BF)) for f in transform(detected, second, first)]
    arriving = [wide(f) for f in arriving]
    for k in spots:
        store(k, 1, conj_times(wide(psi[k]), arriving[k]))
    fields = [conj_times(patches[k](1), arriving[k]) for k in spots]
    fields = [conj_times(propagator, f) for f in transform(fields, first, second)]
    for k, (real, imag) in enumerate(transform(fields, second, first)):
        arrived = real.astype(BF).astype(F32), imag.astype(BF).astype(F32)
        store(k, 0, conj_times(wide(incoming[k]()), arrived))


def solo_kernel(
    number, rows, picks, own, mate, probes, amplitudes, wave, first, second, *refs
):
    if number == 0:
        sent, kept, edges, held, made = refs
        sent_outer, sent_inband = sent.at[0], sent.at[1]
    else:
        before, sent_outer, sent_inband, kept, both, held, made = refs
        both[0] = before[...]
        edges = both.at[1]
    cut = lax.axis_index("cuts")
    spots = places(rows)
    place = jnp.where(cut == 0, spots[number], spots[2 + number])
    start = pl.multiple_of(jnp.where(cut == 0, 0, HALF), HALF)
    held[cut] = own[...]
    held[1 - cut] = mate[...]

    def store(k, which, value):
        made[which, 0], made[which, 1] = value

    chain(
        [lambda: (probes[picks[place], 0], probes[picks[place], 1])],
        [lambda which: wide((held[which, 0], held[which, 1]))],
        [lambda: amplitudes[place]],
        wave, first[...], second[...], store,
    )
    depth = sent_inband.shape[1]
    inner = pl.multiple_of(jnp.where(cut == 0, SIDE - depth, 0), 64)
    for channel in range(2):
        sent_outer[channel] = made[1 - cut, channel, pl.ds(start, HALF)].astype(BF)
        sent_inband[channel] = made[1 - cut, channel, pl.ds(inner, depth)].astype(BF)
        kept[channel] = made[cut, channel]
        edges[channel] = made[cut, channel, pl.ds(start, HALF)].astype(BF)


def put_inband(put, rows, cols, number, inband, channel):
    upper = lax.axis_index("cuts") == 1
    spots = places(rows)
    spot = jnp.where(upper, spots[number], spots[2 + number])
    skip = jnp.where(upper, SIDE - inband.shape[1], 0)
    put(rows[spot] + HALF + skip, cols[spot], inband[channel].astype(F32))
    return rows[spot] + HALF + jnp.where(upper, 0, HALF), cols[spot]


def own_kernel(rows, cols, kept0, kept1, back, total):
    cut = lax.axis_index("cuts")
    places_here = places(rows)
    total[...] = jnp.zeros_like(total)
    for channel in range(2):
        put = functools.partial(put_window, total, channel)
        for number, kept in enumerate((kept0, kept1)):
            spot = jnp.where(cut == 0, places_here[number], places_here[2 + number])
            put(rows[spot] + HALF, cols[spot], kept[channel])
        top, left = put_inband(put, rows, cols, 0, back.at[1], channel)
        put(top, left, back[0, channel].astype(F32))


def rest_kernel(
    rows, cols, spots, given, inband, edges, relay0, relay1, total, output, sems
):
    cut = lax.axis_index("cuts")
    shift = jnp.where(cut == 0, BAND, -HALF)
    copies = []
    for channel in range(2):
        put = functools.partial(put_window, total, channel)
        put_inband(put, rows, cols, 1, inband, channel)
        for number, relay in enumerate((relay0, relay1)):
            k = 2 * number
            put(spots[k] + shift, spots[k + 1], edges[number, channel].astype(F32))
            put(spots[4 + k] + BAND - HALF - shift, spots[5 + k], relay[channel].astype(F32))
        copies.append(
            pltpu.make_async_copy(
                total.at[channel, pl.ds(HALF, BAND)], output.at[0, channel], sems.at[channel]
            )
        )
        copies[channel].start()
    for copy in copies:
        copy.wait()


def call(kernel, name, inputs, outputs, scratch=(), in_specs=None, out_specs=None, aliases={}, vmem=40, flops=1):
    scalars = [x for x in inputs if x.dtype == jnp.int32]
    return pl.pallas_call(
        kernel,
        name=name,
        out_shape=outputs,
        in_specs=in_specs or [SM] * len(scalars) + [VM] * (len(inputs) - len(scalars)),
        out_specs=out_specs or [VM] * len(outputs),
        scratch_shapes=list(scratch),
        input_output_aliases=aliases,
        cost_estimate=pl.CostEstimate(flops=flops, bytes_accessed=1, transcendentals=0),
        compiler_params=pltpu.CompilerParams(vmem_limit_bytes=vmem << 20),
    )(*inputs)


def arr(*shape, dtype=BF):
    return jax.ShapeDtypeStruct(shape, dtype)


def shards(objects, probes, amplitudes, prop_phase, scan_rows, scan_cols, probe_choice):
    route = routes(lax.axis_size("region"))
    move = lambda x, way: lax.ppermute(x, AXES, route[way])
    first, second = (jnp.asarray(t) for t in dft_blocks())
    wave = jnp.stack([jnp.cos(prop_phase), jnp.sin(prop_phase)])
    half = arr(2, HALF, SIDE)

    full = arr(2, SIDE, SIDE)
    near = pltpu.VMEM((2, BAND + HALF, COLS), F32)
    early, late, band, rows, cols = call(
        edge_kernel, "edge",
        [pltpu.with_memory_space_constraint(x, pltpu.HBM) for x in (scan_rows, scan_cols, objects)],
        [arr(EDGE + 16, 128), arr(EDGE + 16, 128),
         arr(2, BAND, COLS, dtype=F32), arr(4, dtype=jnp.int32), arr(4, dtype=jnp.int32)],
        [pltpu.SemaphoreType.DMA((4,))],
        in_specs=[HB] * 3, out_specs=[VM] * 3 + [SM] * 2, vmem=50,
    )
    early = move(early, "early")
    late = move(late, "late")
    sent = call(mate_kernel, "mate", [rows, cols, band, early], [full, full], [near])
    sent0, late = lax.optimization_barrier((sent[0], late))
    mate0 = move(sent0, "mate")
    own0, own1, spots = call(
        own_windows_kernel, "windows", [rows, cols, band, early, late],
        [full, full, arr(8, dtype=jnp.int32)], [near], out_specs=[VM, VM, SM],
    )
    sent1, own1 = lax.optimization_barrier((sent[1], own1))
    mate1 = move(sent1, "mate")
    optics = [probes, amplitudes, wave, first, second]
    work = [pltpu.VMEM((2, 2, SIDE, SIDE), BF), pltpu.VMEM((2, 2, SIDE, SIDE), F32)]
    wide_full = arr(2, SIDE, SIDE, dtype=F32)
    back0, kept0, edge0 = call(
        functools.partial(solo_kernel, 0), "solo0", [rows, probe_choice, own0, mate0] + optics,
        [arr(2, 2, HALF, SIDE), wide_full, half], work, flops=10**11,
    )
    back0 = move(back0, "mate")
    outer1, inband1, kept1, edges = call(
        functools.partial(solo_kernel, 1), "solo1",
        [rows, probe_choice, own1, mate1] + optics + [edge0],
        [half, arr(2, HALF + 64, SIDE), wide_full, arr(2, 2, HALF, SIDE)], work, flops=10**11,
    )
    inband1 = move(inband1, "mate")
    outer1, back0 = lax.optimization_barrier((outer1, back0))
    relay1 = move(outer1, "direct")
    edges = move(edges, "early")
    relay0 = move(back0[0], "late")
    (total,) = call(
        own_kernel, "own", [rows, cols, kept0, kept1, back0],
        [arr(2, EXT, COLS, dtype=F32)], flops=10**11,
    )
    _, gradient = call(
        rest_kernel, "rest",
        [rows, cols, spots, total, inband1, edges, relay0, relay1],
        [arr(2, EXT, COLS, dtype=F32), arr(1, 2, BAND, COLS, dtype=F32)],
        [pltpu.SemaphoreType.DMA((2,))],
        out_specs=[VM, HB],
        aliases={3: 0},
    )
    return gradient


def solution(mesh):
    return jax.shard_map(
        shards,
        mesh=mesh,
        in_specs=(
            P("cuts", None, "region", None),
            P(),
            P("region", None, None),
            P(),
            P("region"),
            P("region"),
            P("region"),
        ),
        out_specs=P("cuts", None, "region", None),
        check_vma=False,
    )
```

```python
import functools

import jax
import jax.numpy as jnp
import ml_dtypes
import numpy as np
from jax import lax
from jax.experimental import pallas as pl
from jax.experimental.pallas import tpu as pltpu
from jax.sharding import PartitionSpec as P

modulus_floor = 0.25
AXES = ("cuts", "region")
BF = jnp.bfloat16
F32 = jnp.float32
SIDE = 256
HALF = 128
BAND = 256
COLS = 1024
EXT = BAND + 2 * HALF
EDGE = 2 * HALF * COLS // 128
WIDE = SIDE + 128
VM = pl.BlockSpec(memory_space=pltpu.VMEM)
SM = pl.BlockSpec(memory_space=pltpu.SMEM)
HB = pl.BlockSpec(memory_space=pltpu.HBM)


def routes(regions):
    at = lambda c, r: c * regions + r % regions
    both = [(c, r) for c in range(2) for r in range(regions)]
    return {
        "mate": [(at(c, r), at(1 - c, r)) for c, r in both],
        "direct": [(at(c, r), at(1 - c, r - 1 if c == 0 else r + 1)) for c, r in both],
        "early": [(at(c, r), at(c, r - 1 if c == 0 else r + 1)) for c, r in both],
        "late": [(at(c, r), at(c, r + 1 if c == 0 else r - 1)) for c, r in both],
    }


def dft_blocks():
    index = np.arange(SIDE)
    angles = (index[:, None] * index[None, :] % SIDE) * (2.0 * np.pi / SIDE)
    real = np.cos(angles) / np.sqrt(SIDE)
    imag = -np.sin(angles) / np.sqrt(SIDE)
    first = np.block([[real, -imag], [imag, real]]).astype(ml_dtypes.bfloat16)
    second = np.block([[real, imag], [-imag, real]]).astype(ml_dtypes.bfloat16)
    return first, second


def places(rows):
    up = [rows[i] < 0 for i in range(4)]
    first = lambda a, b: jnp.where(a, 0, jnp.where(b, 1, 2))
    last = lambda a, b: jnp.where(a, 3, jnp.where(b, 2, 1))
    no = [jnp.logical_not(u) for u in up]
    return first(up[0], up[1]), last(up[3], up[2]), first(no[0], no[1]), last(no[3], no[2])


def column_split(left):
    base = jnp.minimum(lax.shift_right_logical(left, 7), (COLS - WIDE) // 128) * 128
    return pl.multiple_of(base, 128), left - base


def row_split(top, most):
    base = jnp.minimum(lax.shift_right_logical(top, 3), most // 8) * 8
    return pl.multiple_of(base, 8), top - base


def cut_window(load, top, left, count, total):
    row_base, row_shift = row_split(top, total - count - 8)
    col_base, col_shift = column_split(left)
    block = load(pl.ds(row_base, count + 8), pl.ds(col_base, WIDE))
    block = pltpu.roll(block, lax.rem(count + 8 - row_shift, count + 8), 0)[:count]
    return pltpu.roll(block, lax.rem(WIDE - col_shift, WIDE), 1)[:, :SIDE]


def put_window(total_ref, channel, top, left, block):
    count = block.shape[0]
    row_base, row_shift = row_split(top, EXT - count - 8)
    col_base, col_shift = column_split(left)
    block = jnp.concatenate([block, jnp.zeros((count, WIDE - SIDE), F32)], axis=1)
    block = pltpu.roll(block, col_shift, 1)
    block = jnp.concatenate([block, jnp.zeros((8, WIDE), F32)], axis=0)
    block = pltpu.roll(block, row_shift, 0)
    where = (channel, pl.ds(row_base, count + 8), pl.ds(col_base, WIDE))
    total_ref[where] = total_ref[where] + block


def put_near(total_ref, channel, top, left, block, near):
    row = pl.multiple_of(HALF + near, HALF)
    col_base, col_shift = column_split(left)
    shift = top - row
    block = jnp.concatenate([block, jnp.zeros((HALF, WIDE - SIDE), F32)], axis=1)
    block = pltpu.roll(block, col_shift, 1)
    block = pltpu.roll(block, lax.rem(shift + 2 * HALF, HALF), 0)
    line = lax.broadcasted_iota(jnp.int32, block.shape, 0)
    kept = jnp.where((line >= shift) & (line < shift + HALF), block, 0.0)
    where = (channel, pl.ds(row, HALF), pl.ds(col_base, WIDE))
    total_ref[where] = total_ref[where] + kept


def tagged(rows, cols, spots):
    line = lax.broadcasted_iota(jnp.int32, (16, 128), 0)
    lane = lax.broadcasted_iota(jnp.int32, (16, 128), 1)
    tile = jnp.zeros((16, 128), jnp.int32)
    for k, spot in enumerate(spots):
        left = cols[spot]
        parts = (rows[spot] + HALF, lax.shift_right_logical(left, 3), jnp.bitwise_and(left, 7))
        for n, part in enumerate(parts):
            tile = jnp.where((line == k) & (lane == n), part, tile)
    return tile.astype(F32).astype(BF)


def edge_kernel(rows_in, cols_in, objects_in, early, late, objects, rows, cols, sems):
    cut = lax.axis_index("cuts")
    copies = [
        pltpu.make_async_copy(rows_in, rows, sems.at[0]),
        pltpu.make_async_copy(cols_in, cols, sems.at[1]),
        pltpu.make_async_copy(objects_in.at[0, 0], objects.at[0], sems.at[2]),
        pltpu.make_async_copy(objects_in.at[0, 1], objects.at[1], sems.at[3]),
    ]
    for copy in copies:
        copy.start()
    copies[0].wait()
    copies[1].wait()
    u0, u1, l0, l1 = places(rows)
    up = cut == 0
    early[EDGE:] = tagged(rows, cols, (jnp.where(up, u0, l0), jnp.where(up, u1, l1)))
    late[EDGE:] = tagged(rows, cols, (jnp.where(up, l0, u0), jnp.where(up, l1, u1)))
    start = pl.multiple_of(jnp.where(up, 0, HALF), HALF)
    for channel in range(2):
        copies[2 + channel].wait()
        for k in range(COLS // 128):
            where = pl.ds((channel * (COLS // 128) + k) * HALF, HALF)
            lanes = slice(128 * k, 128 * (k + 1))
            early[where] = objects[channel, pl.ds(start, HALF), lanes].astype(BF)
            late[where] = objects[channel, pl.ds(HALF - start, HALF), lanes].astype(BF)


def cut_pair(rows, cols, objects, edge, lower, spots, outputs, near):
    start = pl.multiple_of(jnp.where(lower, BAND, 0), HALF)
    own = pl.multiple_of(jnp.where(lower, 0, HALF), HALF)
    for channel in range(2):
        for k in range(COLS // 128):
            near[channel, pl.ds(start, HALF), 128 * k : 128 * (k + 1)] = edge[
                pl.ds((channel * (COLS // 128) + k) * HALF, HALF)
            ].astype(F32)
        near[channel, pl.ds(own, BAND)] = objects[channel]
        for spot, output in zip(spots, outputs):
            output[channel] = cut_window(
                lambda r, c: near[channel, r, c], rows[spot] + own, cols[spot], SIDE, BAND + HALF
            ).astype(BF)


def mate_kernel(rows, cols, objects, early, window0, window1, near):
    lower = lax.axis_index("cuts") == 0
    u0, u1, l0, l1 = places(rows)
    spots = jnp.where(lower, l0, u0), jnp.where(lower, l1, u1)
    cut_pair(rows, cols, objects, early, lower, spots, (window0, window1), near)


def own_windows_kernel(rows, cols, objects, early, late, window0, window1, spots, near):
    lower = lax.axis_index("cuts") == 1
    u0, u1, l0, l1 = places(rows)
    mine = jnp.where(lower, l0, u0), jnp.where(lower, l1, u1)
    cut_pair(rows, cols, objects, late, lower, mine, (window0, window1), near)
    decode(early, late, spots)


def decode(early, late, spots):
    line = lax.broadcasted_iota(jnp.int32, (16, 128), 0)
    lane = lax.broadcasted_iota(jnp.int32, (16, 128), 1)
    for n, edge in enumerate((early, late)):
        tile = edge[EDGE:].astype(F32)
        left = jnp.where(lane == 1, tile * 8.0, jnp.where(lane == 2, tile, 0.0))
        top = jnp.where(lane == 0, tile, 0.0)
        for k in range(2):
            for m, part in enumerate((top, left)):
                spots[4 * n + 2 * k + m] = jnp.sum(jnp.where(line == k, part, 0.0)).astype(jnp.int32)


def transform(fields, left, right):
    count = len(fields)
    stacked = jnp.concatenate(
        [jnp.concatenate([f[part].astype(BF) for f in fields], axis=1) for part in range(2)], axis=0
    )
    middle = jnp.dot(left, stacked, preferred_element_type=F32).astype(BF)
    spans = [slice(SIDE * k, SIDE * (k + 1)) for k in range(count)]
    middle = jnp.concatenate(
        [jnp.concatenate([middle[:SIDE, s], middle[SIDE:, s]], axis=1) for s in spans], axis=0
    )
    result = jnp.dot(middle, right, preferred_element_type=F32)
    return [(result[s, :SIDE], result[s, SIDE:]) for s in spans]


def times(a, b):
    return a[0] * b[0] - a[1] * b[1], a[0] * b[1] + a[1] * b[0]


def conj_times(a, b):
    return a[0] * b[0] + a[1] * b[1], a[0] * b[1] - a[1] * b[0]


def wide(pair):
    return pair[0].astype(F32), pair[1].astype(F32)


def chain(incoming, patches, measured, wave, first, second, store):
    spots = range(len(incoming))
    propagator = (wave[0], wave[1])
    fields = [times(wide(incoming[k]()), patches[k](0)) for k in spots]
    fields = [times(propagator, f) for f in transform(fields, first, second)]
    psi = [(f[0].astype(BF), f[1].astype(BF)) for f in transform(fields, second, first)]
    fields = [times(wide(psi[k]), patches[k](1)) for k in spots]
    detected = []
    for k, (real, imag) in enumerate(transform(fields, first, second)):
        modulus = jnp.sqrt(real * real + imag * imag)
        factor = 1.0 - measured[k]() / jnp.maximum(modulus, modulus_floor)
        detected.append((real * factor, imag * factor))
    arriving = [(f[0].astype(BF), f[1].astype(BF)) for f in transform(detected, second, first)]
    arriving = [wide(f) for f in arriving]
    for k in spots:
        store(k, 1, conj_times(wide(psi[k]), arriving[k]))
    fields = [conj_times(patches[k](1), arriving[k]) for k in spots]
    fields = [conj_times(propagator, f) for f in transform(fields, first, second)]
    for k, (real, imag) in enumerate(transform(fields, second, first)):
        arrived = real.astype(BF).astype(F32), imag.astype(BF).astype(F32)
        store(k, 0, conj_times(wide(incoming[k]()), arrived))


def solo_kernel(
    number, rows, picks, own, mate, probes, amplitudes, wave, first, second, *refs
):
    sent_outer, sent_inband, kept, edges, held, made = refs
    cut = lax.axis_index("cuts")
    spots = places(rows)
    place = jnp.where(cut == 0, spots[number], spots[2 + number])
    start = pl.multiple_of(jnp.where(cut == 0, 0, HALF), HALF)
    held[cut] = own[...]
    held[1 - cut] = mate[...]

    def store(k, which, value):
        made[which, 0], made[which, 1] = value

    chain(
        [lambda: (probes[picks[place], 0], probes[picks[place], 1])],
        [lambda which: wide((held[which, 0], held[which, 1]))],
        [lambda: amplitudes[place]],
        wave, first[...], second[...], store,
    )
    depth = sent_inband.shape[1]
    inner = pl.multiple_of(jnp.where(cut == 0, SIDE - depth, 0), 64)
    for channel in range(2):
        sent_outer[channel] = made[1 - cut, channel, pl.ds(start, HALF)].astype(BF)
        sent_inband[channel] = made[1 - cut, channel, pl.ds(inner, depth)].astype(BF)
        kept[channel] = made[cut, channel]
        edges[channel] = made[cut, channel, pl.ds(start, HALF)].astype(BF)


def put_inband(put, rows, cols, number, inband, channel):
    upper = lax.axis_index("cuts") == 1
    spots = places(rows)
    spot = jnp.where(upper, spots[number], spots[2 + number])
    skip = jnp.where(upper, SIDE - inband.shape[1], 0)
    put(rows[spot] + HALF + skip, cols[spot], inband[channel].astype(F32))
    return rows[spot] + HALF + jnp.where(upper, 0, HALF), cols[spot]


def own_kernel(rows, cols, kept0, kept1, outer, inband, total):
    cut = lax.axis_index("cuts")
    places_here = places(rows)
    total[...] = jnp.zeros_like(total)
    for channel in range(2):
        put = functools.partial(put_window, total, channel)
        for number, kept in enumerate((kept0, kept1)):
            spot = jnp.where(cut == 0, places_here[number], places_here[2 + number])
            put(rows[spot] + HALF, cols[spot], kept[channel])
        top, left = put_inband(put, rows, cols, 0, inband, channel)
        put(top, left, outer[channel].astype(F32))


def more_kernel(rows, cols, spots, given, inband, edge0, edge1, relay0, total):
    cut = lax.axis_index("cuts")
    shift = jnp.where(cut == 0, BAND, -HALF)
    for channel in range(2):
        put = functools.partial(put_window, total, channel)
        put_inband(put, rows, cols, 1, inband, channel)
        put(spots[0] + shift, spots[1], edge0[channel].astype(F32))
        put(spots[2] + shift, spots[3], edge1[channel].astype(F32))
        put(spots[4] + BAND - HALF - shift, spots[5], relay0[channel].astype(F32))


def last_kernel(spots, given, relay1, total, output, sems):
    cut = lax.axis_index("cuts")
    near = pl.multiple_of(jnp.where(cut == 0, 0, HALF), HALF)
    far = HALF - near

    def copy(channel, start, sem):
        return pltpu.make_async_copy(
            total.at[channel, pl.ds(pl.multiple_of(HALF + start, HALF), HALF)],
            output.at[0, channel, pl.ds(start, HALF)],
            sem,
        )

    copies = [copy(channel, far, sems.at[channel]) for channel in range(2)]
    for channel in range(2):
        copies[channel].start()
    top = spots[6] + jnp.where(cut == 0, -HALF, BAND)
    for channel in range(2):
        put_near(total, channel, top, spots[7], relay1[channel].astype(F32), near)
        copies.append(copy(channel, near, sems.at[2 + channel]))
        copies[2 + channel].start()
    for item in copies:
        item.wait()


def call(kernel, name, inputs, outputs, scratch=(), in_specs=None, out_specs=None, aliases={}, vmem=40, flops=1):
    scalars = [x for x in inputs if x.dtype == jnp.int32]
    return pl.pallas_call(
        kernel,
        name=name,
        out_shape=outputs,
        in_specs=in_specs or [SM] * len(scalars) + [VM] * (len(inputs) - len(scalars)),
        out_specs=out_specs or [VM] * len(outputs),
        scratch_shapes=list(scratch),
        input_output_aliases=aliases,
        cost_estimate=pl.CostEstimate(flops=flops, bytes_accessed=1, transcendentals=0),
        compiler_params=pltpu.CompilerParams(vmem_limit_bytes=vmem << 20),
    )(*inputs)


def arr(*shape, dtype=BF):
    return jax.ShapeDtypeStruct(shape, dtype)


def shards(objects, probes, amplitudes, prop_phase, scan_rows, scan_cols, probe_choice):
    route = routes(lax.axis_size("region"))
    move = lambda x, way: lax.ppermute(x, AXES, route[way])
    first, second = (jnp.asarray(t) for t in dft_blocks())
    wave = jnp.stack([jnp.cos(prop_phase), jnp.sin(prop_phase)])
    half = arr(2, HALF, SIDE)

    full = arr(2, SIDE, SIDE)
    near = pltpu.VMEM((2, BAND + HALF, COLS), F32)
    early, late, band, rows, cols = call(
        edge_kernel, "edge",
        [pltpu.with_memory_space_constraint(x, pltpu.HBM) for x in (scan_rows, scan_cols, objects)],
        [arr(EDGE + 16, 128), arr(EDGE + 16, 128),
         arr(2, BAND, COLS, dtype=F32), arr(4, dtype=jnp.int32), arr(4, dtype=jnp.int32)],
        [pltpu.SemaphoreType.DMA((4,))],
        in_specs=[HB] * 3, out_specs=[VM] * 3 + [SM] * 2, vmem=50,
    )
    early = move(early, "early")
    late = move(late, "late")
    sent = call(mate_kernel, "mate", [rows, cols, band, early], [full, full], [near])
    sent0, late = lax.optimization_barrier((sent[0], late))
    mate0 = move(sent0, "mate")
    own0, own1, spots = call(
        own_windows_kernel, "windows", [rows, cols, band, early, late],
        [full, full, arr(8, dtype=jnp.int32)], [near], out_specs=[VM, VM, SM],
    )
    sent1, own1 = lax.optimization_barrier((sent[1], own1))
    mate1 = move(sent1, "mate")
    optics = [probes, amplitudes, wave, first, second]
    work = [pltpu.VMEM((2, 2, SIDE, SIDE), BF), pltpu.VMEM((2, 2, SIDE, SIDE), F32)]
    wide_full = arr(2, SIDE, SIDE, dtype=F32)
    outer0, inband0, kept0, edge0 = call(
        functools.partial(solo_kernel, 0), "solo0", [rows, probe_choice, own0, mate0] + optics,
        [half, half, wide_full, half], work, flops=10**11,
    )
    outer0 = move(outer0, "mate")
    inband0 = move(inband0, "mate")
    edge0 = move(edge0, "early")
    outer1, inband1, kept1, edge1 = call(
        functools.partial(solo_kernel, 1), "solo1",
        [rows, probe_choice, own1, mate1] + optics,
        [half, arr(2, HALF + 64, SIDE), wide_full, half], work, flops=10**11,
    )
    inband1 = move(inband1, "mate")
    outer1, edge1, outer0 = lax.optimization_barrier((outer1, edge1, outer0))
    relay1 = move(outer1, "direct")
    edge1 = move(edge1, "early")
    relay0 = move(outer0, "late")
    (total,) = call(
        own_kernel, "own", [rows, cols, kept0, kept1, outer0, inband0],
        [arr(2, EXT, COLS, dtype=F32)], flops=10**11,
    )
    (total,) = call(
        more_kernel, "more",
        [rows, cols, spots, total, inband1, edge0, edge1, relay0],
        [arr(2, EXT, COLS, dtype=F32)], aliases={3: 0}, flops=10**11,
    )
    _, gradient = call(
        last_kernel, "last", [spots, total, relay1],
        [arr(2, EXT, COLS, dtype=F32), arr(1, 2, BAND, COLS, dtype=F32)],
        [pltpu.SemaphoreType.DMA((4,))],
        out_specs=[VM, HB],
        aliases={1: 0},
    )
    return gradient


def solution(mesh):
    return jax.shard_map(
        shards,
        mesh=mesh,
        in_specs=(
            P("cuts", None, "region", None),
            P(),
            P("region", None, None),
            P(),
            P("region"),
            P("region"),
            P("region"),
        ),
        out_specs=P("cuts", None, "region", None),
        check_vma=False,
    )
```

```python
import functools

import jax
import jax.numpy as jnp
import ml_dtypes
import numpy as np
from jax import lax
from jax.experimental import pallas as pl
from jax.experimental.pallas import tpu as pltpu
from jax.sharding import PartitionSpec as P

modulus_floor = 0.25
AXES = ("cuts", "region")
BF = jnp.bfloat16
F32 = jnp.float32
SIDE = 256
HALF = 128
BAND = 256
COLS = 1024
EXT = BAND + 2 * HALF
EDGE = 2 * HALF * COLS // 128
WIDE = SIDE + 128
VM = pl.BlockSpec(memory_space=pltpu.VMEM)
SM = pl.BlockSpec(memory_space=pltpu.SMEM)
HB = pl.BlockSpec(memory_space=pltpu.HBM)


def routes(regions):
    at = lambda c, r: c * regions + r % regions
    both = [(c, r) for c in range(2) for r in range(regions)]
    return {
        "mate": [(at(c, r), at(1 - c, r)) for c, r in both],
        "direct": [(at(c, r), at(1 - c, r - 1 if c == 0 else r + 1)) for c, r in both],
        "early": [(at(c, r), at(c, r - 1 if c == 0 else r + 1)) for c, r in both],
        "late": [(at(c, r), at(c, r + 1 if c == 0 else r - 1)) for c, r in both],
    }


def dft_blocks():
    index = np.arange(SIDE)
    angles = (index[:, None] * index[None, :] % SIDE) * (2.0 * np.pi / SIDE)
    real = np.cos(angles) / np.sqrt(SIDE)
    imag = -np.sin(angles) / np.sqrt(SIDE)
    first = np.block([[real, -imag], [imag, real]]).astype(ml_dtypes.bfloat16)
    second = np.block([[real, imag], [-imag, real]]).astype(ml_dtypes.bfloat16)
    return first, second


def places(rows):
    up = [rows[i] < 0 for i in range(4)]
    first = lambda a, b: jnp.where(a, 0, jnp.where(b, 1, 2))
    last = lambda a, b: jnp.where(a, 3, jnp.where(b, 2, 1))
    no = [jnp.logical_not(u) for u in up]
    return first(up[0], up[1]), last(up[3], up[2]), first(no[0], no[1]), last(no[3], no[2])


def column_split(left):
    base = jnp.minimum(lax.shift_right_logical(left, 7), (COLS - WIDE) // 128) * 128
    return pl.multiple_of(base, 128), left - base


def row_split(top, most):
    base = jnp.minimum(lax.shift_right_logical(top, 3), most // 8) * 8
    return pl.multiple_of(base, 8), top - base


def cut_window(load, top, left, count, total):
    row_base, row_shift = row_split(top, total - count - 8)
    col_base, col_shift = column_split(left)
    block = load(pl.ds(row_base, count + 8), pl.ds(col_base, WIDE))
    block = pltpu.roll(block, lax.rem(count + 8 - row_shift, count + 8), 0)[:count]
    return pltpu.roll(block, lax.rem(WIDE - col_shift, WIDE), 1)[:, :SIDE]


def put_window(total_ref, channel, top, left, block):
    count = block.shape[0]
    row_base, row_shift = row_split(top, EXT - count - 8)
    col_base, col_shift = column_split(left)
    block = jnp.concatenate([block, jnp.zeros((count, WIDE - SIDE), F32)], axis=1)
    block = pltpu.roll(block, col_shift, 1)
    block = jnp.concatenate([block, jnp.zeros((8, WIDE), F32)], axis=0)
    block = pltpu.roll(block, row_shift, 0)
    where = (channel, pl.ds(row_base, count + 8), pl.ds(col_base, WIDE))
    total_ref[where] = total_ref[where] + block


def tagged(rows, cols, spots):
    line = lax.broadcasted_iota(jnp.int32, (16, 128), 0)
    lane = lax.broadcasted_iota(jnp.int32, (16, 128), 1)
    tile = jnp.zeros((16, 128), jnp.int32)
    for k, spot in enumerate(spots):
        left = cols[spot]
        parts = (rows[spot] + HALF, lax.shift_right_logical(left, 3), jnp.bitwise_and(left, 7))
        for n, part in enumerate(parts):
            tile = jnp.where((line == k) & (lane == n), part, tile)
    return tile.astype(F32).astype(BF)


def edge_kernel(rows_in, cols_in, objects_in, early, late, objects, rows, cols, sems):
    cut = lax.axis_index("cuts")
    copies = [
        pltpu.make_async_copy(rows_in, rows, sems.at[0]),
        pltpu.make_async_copy(cols_in, cols, sems.at[1]),
        pltpu.make_async_copy(objects_in.at[0, 0], objects.at[0], sems.at[2]),
        pltpu.make_async_copy(objects_in.at[0, 1], objects.at[1], sems.at[3]),
    ]
    for copy in copies:
        copy.start()
    copies[0].wait()
    copies[1].wait()
    u0, u1, l0, l1 = places(rows)
    up = cut == 0
    early[EDGE:] = tagged(rows, cols, (jnp.where(up, u0, l0), jnp.where(up, u1, l1)))
    late[EDGE:] = tagged(rows, cols, (jnp.where(up, l0, u0), jnp.where(up, l1, u1)))
    start = pl.multiple_of(jnp.where(up, 0, HALF), HALF)
    for channel in range(2):
        copies[2 + channel].wait()
        for k in range(COLS // 128):
            where = pl.ds((channel * (COLS // 128) + k) * HALF, HALF)
            lanes = slice(128 * k, 128 * (k + 1))
            early[where] = objects[channel, pl.ds(start, HALF), lanes].astype(BF)
            late[where] = objects[channel, pl.ds(HALF - start, HALF), lanes].astype(BF)


def cut_pair(rows, cols, objects, edge, lower, spots, outputs, near):
    start = pl.multiple_of(jnp.where(lower, BAND, 0), HALF)
    own = pl.multiple_of(jnp.where(lower, 0, HALF), HALF)
    for channel in range(2):
        for k in range(COLS // 128):
            near[channel, pl.ds(start, HALF), 128 * k : 128 * (k + 1)] = edge[
                pl.ds((channel * (COLS // 128) + k) * HALF, HALF)
            ].astype(F32)
        near[channel, pl.ds(own, BAND)] = objects[channel]
        for spot, output in zip(spots, outputs):
            output[channel] = cut_window(
                lambda r, c: near[channel, r, c], rows[spot] + own, cols[spot], SIDE, BAND + HALF
            ).astype(BF)


def mate_kernel(rows, cols, objects, early, window0, window1, near):
    lower = lax.axis_index("cuts") == 0
    u0, u1, l0, l1 = places(rows)
    spots = jnp.where(lower, l0, u0), jnp.where(lower, l1, u1)
    cut_pair(rows, cols, objects, early, lower, spots, (window0, window1), near)


def own_windows_kernel(rows, cols, objects, early, late, window0, window1, spots, near):
    lower = lax.axis_index("cuts") == 1
    u0, u1, l0, l1 = places(rows)
    mine = jnp.where(lower, l0, u0), jnp.where(lower, l1, u1)
    cut_pair(rows, cols, objects, late, lower, mine, (window0, window1), near)
    decode(early, late, spots)


def decode(early, late, spots):
    line = lax.broadcasted_iota(jnp.int32, (16, 128), 0)
    lane = lax.broadcasted_iota(jnp.int32, (16, 128), 1)
    for n, edge in enumerate((early, late)):
        tile = edge[EDGE:].astype(F32)
        left = jnp.where(lane == 1, tile * 8.0, jnp.where(lane == 2, tile, 0.0))
        top = jnp.where(lane == 0, tile, 0.0)
        for k in range(2):
            for m, part in enumerate((top, left)):
                spots[4 * n + 2 * k + m] = jnp.sum(jnp.where(line == k, part, 0.0)).astype(jnp.int32)


def transform(fields, left, right):
    count = len(fields)
    stacked = jnp.concatenate(
        [jnp.concatenate([f[part].astype(BF) for f in fields], axis=1) for part in range(2)], axis=0
    )
    middle = jnp.dot(left, stacked, preferred_element_type=F32).astype(BF)
    spans = [slice(SIDE * k, SIDE * (k + 1)) for k in range(count)]
    middle = jnp.concatenate(
        [jnp.concatenate([middle[:SIDE, s], middle[SIDE:, s]], axis=1) for s in spans], axis=0
    )
    result = jnp.dot(middle, right, preferred_element_type=F32)
    return [(result[s, :SIDE], result[s, SIDE:]) for s in spans]


def times(a, b):
    return a[0] * b[0] - a[1] * b[1], a[0] * b[1] + a[1] * b[0]


def conj_times(a, b):
    return a[0] * b[0] + a[1] * b[1], a[0] * b[1] - a[1] * b[0]


def wide(pair):
    return pair[0].astype(F32), pair[1].astype(F32)


def chain(incoming, patches, measured, wave, first, second, store):
    spots = range(len(incoming))
    propagator = (wave[0], wave[1])
    fields = [times(wide(incoming[k]()), patches[k](0)) for k in spots]
    fields = [times(propagator, f) for f in transform(fields, first, second)]
    psi = [(f[0].astype(BF), f[1].astype(BF)) for f in transform(fields, second, first)]
    fields = [times(wide(psi[k]), patches[k](1)) for k in spots]
    detected = []
    for k, (real, imag) in enumerate(transform(fields, first, second)):
        modulus = jnp.sqrt(real * real + imag * imag)
        factor = 1.0 - measured[k]() / jnp.maximum(modulus, modulus_floor)
        detected.append((real * factor, imag * factor))
    arriving = [(f[0].astype(BF), f[1].astype(BF)) for f in transform(detected, second, first)]
    arriving = [wide(f) for f in arriving]
    for k in spots:
        store(k, 1, conj_times(wide(psi[k]), arriving[k]))
    fields = [conj_times(patches[k](1), arriving[k]) for k in spots]
    fields = [conj_times(propagator, f) for f in transform(fields, first, second)]
    for k, (real, imag) in enumerate(transform(fields, second, first)):
        arrived = real.astype(BF).astype(F32), imag.astype(BF).astype(F32)
        store(k, 0, conj_times(wide(incoming[k]()), arrived))


def solo_kernel(
    number, rows, picks, own, mate, probes, amplitudes, wave, first, second, *refs
):
    if number == 0:
        sent, kept, edges, held, made = refs
        sent_outer, sent_inband = sent.at[0], sent.at[1]
    else:
        before, sent_outer, sent_inband, kept, both, held, made = refs
        both[0] = before[...]
        edges = both.at[1]
    cut = lax.axis_index("cuts")
    spots = places(rows)
    place = jnp.where(cut == 0, spots[number], spots[2 + number])
    start = pl.multiple_of(jnp.where(cut == 0, 0, HALF), HALF)
    held[cut] = own[...]
    held[1 - cut] = mate[...]

    def store(k, which, value):
        made[which, 0], made[which, 1] = value

    chain(
        [lambda: (probes[picks[place], 0], probes[picks[place], 1])],
        [lambda which: wide((held[which, 0], held[which, 1]))],
        [lambda: amplitudes[place]],
        wave, first[...], second[...], store,
    )
    depth = sent_inband.shape[1]
    inner = pl.multiple_of(jnp.where(cut == 0, SIDE - depth, 0), 64)
    for channel in range(2):
        sent_outer[channel] = made[1 - cut, channel, pl.ds(start, HALF)].astype(BF)
        sent_inband[channel] = made[1 - cut, channel, pl.ds(inner, depth)].astype(BF)
        kept[channel] = made[cut, channel]
        edges[channel] = made[cut, channel, pl.ds(start, HALF)].astype(BF)


def put_inband(put, rows, cols, number, inband, channel):
    upper = lax.axis_index("cuts") == 1
    spots = places(rows)
    spot = jnp.where(upper, spots[number], spots[2 + number])
    skip = jnp.where(upper, SIDE - inband.shape[1], 0)
    put(rows[spot] + HALF + skip, cols[spot], inband[channel].astype(F32))
    return rows[spot] + HALF + jnp.where(upper, 0, HALF), cols[spot]


def own_kernel(rows, cols, kept0, kept1, back, total):
    cut = lax.axis_index("cuts")
    places_here = places(rows)
    total[...] = jnp.zeros_like(total)
    for channel in range(2):
        put = functools.partial(put_window, total, channel)
        for number, kept in enumerate((kept0, kept1)):
            spot = jnp.where(cut == 0, places_here[number], places_here[2 + number])
            put(rows[spot] + HALF, cols[spot], kept[channel])
        top, left = put_inband(put, rows, cols, 0, back.at[1], channel)
        put(top, left, back[0, channel].astype(F32))


def rest_kernel(
    rows, cols, spots, given, inband, edges, relay0, relay1, total, output, sems
):
    cut = lax.axis_index("cuts")
    shift = jnp.where(cut == 0, BAND, -HALF)
    copies = []
    for channel in range(2):
        put = functools.partial(put_window, total, channel)
        put_inband(put, rows, cols, 1, inband, channel)
        for number, relay in enumerate((relay0, relay1)):
            k = 2 * number
            put(spots[k] + shift, spots[k + 1], edges[number, channel].astype(F32))
            put(spots[4 + k] + BAND - HALF - shift, spots[5 + k], relay[channel].astype(F32))
        copies.append(
            pltpu.make_async_copy(
                total.at[channel, pl.ds(HALF, BAND)], output.at[0, channel], sems.at[channel]
            )
        )
        copies[channel].start()
    for copy in copies:
        copy.wait()


def call(kernel, name, inputs, outputs, scratch=(), in_specs=None, out_specs=None, aliases={}, vmem=40, flops=1):
    scalars = [x for x in inputs if x.dtype == jnp.int32]
    return pl.pallas_call(
        kernel,
        name=name,
        out_shape=outputs,
        in_specs=in_specs or [SM] * len(scalars) + [VM] * (len(inputs) - len(scalars)),
        out_specs=out_specs or [VM] * len(outputs),
        scratch_shapes=list(scratch),
        input_output_aliases=aliases,
        cost_estimate=pl.CostEstimate(flops=flops, bytes_accessed=1, transcendentals=0),
        compiler_params=pltpu.CompilerParams(vmem_limit_bytes=vmem << 20),
    )(*inputs)


def arr(*shape, dtype=BF):
    return jax.ShapeDtypeStruct(shape, dtype)


def shards(objects, probes, amplitudes, prop_phase, scan_rows, scan_cols, probe_choice):
    route = routes(lax.axis_size("region"))
    move = lambda x, way: lax.ppermute(x, AXES, route[way])
    first, second = (jnp.asarray(t) for t in dft_blocks())
    wave = jnp.stack([jnp.cos(prop_phase), jnp.sin(prop_phase)])
    half = arr(2, HALF, SIDE)

    full = arr(2, SIDE, SIDE)
    near = pltpu.VMEM((2, BAND + HALF, COLS), F32)
    early, late, band, rows, cols = call(
        edge_kernel, "edge",
        [pltpu.with_memory_space_constraint(x, pltpu.HBM) for x in (scan_rows, scan_cols, objects)],
        [arr(EDGE + 16, 128), arr(EDGE + 16, 128),
         arr(2, BAND, COLS, dtype=F32), arr(4, dtype=jnp.int32), arr(4, dtype=jnp.int32)],
        [pltpu.SemaphoreType.DMA((4,))],
        in_specs=[HB] * 3, out_specs=[VM] * 3 + [SM] * 2, vmem=50,
    )
    early = move(early, "early")
    late = move(late, "late")
    sent = call(mate_kernel, "mate", [rows, cols, band, early], [full, full], [near])
    mate0, mate1 = (move(x, "mate") for x in sent)
    own0, own1, spots = call(
        own_windows_kernel, "windows", [rows, cols, band, early, late],
        [full, full, arr(8, dtype=jnp.int32)], [near], out_specs=[VM, VM, SM],
    )
    optics = [probes, amplitudes, wave, first, second]
    work = [pltpu.VMEM((2, 2, SIDE, SIDE), BF), pltpu.VMEM((2, 2, SIDE, SIDE), F32)]
    wide_full = arr(2, SIDE, SIDE, dtype=F32)
    back0, kept0, edge0 = call(
        functools.partial(solo_kernel, 0), "solo0", [rows, probe_choice, own0, mate0] + optics,
        [arr(2, 2, HALF, SIDE), wide_full, half], work,
    )
    back0 = move(back0, "mate")
    outer1, inband1, kept1, edges = call(
        functools.partial(solo_kernel, 1), "solo1",
        [rows, probe_choice, own1, mate1] + optics + [edge0],
        [half, arr(2, HALF + 64, SIDE), wide_full, arr(2, 2, HALF, SIDE)], work, flops=10**11,
    )
    inband1 = move(inband1, "mate")
    outer1, back0 = lax.optimization_barrier((outer1, back0))
    relay1 = move(outer1, "direct")
    edges = move(edges, "early")
    relay0 = move(back0[0], "late")
    (total,) = call(
        own_kernel, "own", [rows, cols, kept0, kept1, back0],
        [arr(2, EXT, COLS, dtype=F32)], flops=10**11,
    )
    _, gradient = call(
        rest_kernel, "rest",
        [rows, cols, spots, total, inband1, edges, relay0, relay1],
        [arr(2, EXT, COLS, dtype=F32), arr(1, 2, BAND, COLS, dtype=F32)],
        [pltpu.SemaphoreType.DMA((2,))],
        out_specs=[VM, HB],
        aliases={3: 0},
    )
    return gradient


def solution(mesh):
    return jax.shard_map(
        shards,
        mesh=mesh,
        in_specs=(
            P("cuts", None, "region", None),
            P(),
            P("region", None, None),
            P(),
            P("region"),
            P("region"),
            P("region"),
        ),
        out_specs=P("cuts", None, "region", None),
        check_vma=False,
    )
```

```python
import functools

import jax
import jax.numpy as jnp
import ml_dtypes
import numpy as np
from jax import lax
from jax.experimental import pallas as pl
from jax.experimental.pallas import tpu as pltpu
from jax.sharding import PartitionSpec as P

modulus_floor = 0.25
AXES = ("cuts", "region")
BF = jnp.bfloat16
F32 = jnp.float32
SIDE = 256
HALF = 128
BAND = 256
COLS = 1024
EXT = BAND + 2 * HALF
EDGE = 2 * HALF * COLS // 128
WIDE = SIDE + 128
VM = pl.BlockSpec(memory_space=pltpu.VMEM)
SM = pl.BlockSpec(memory_space=pltpu.SMEM)
HB = pl.BlockSpec(memory_space=pltpu.HBM)


def routes(regions):
    at = lambda c, r: c * regions + r % regions
    both = [(c, r) for c in range(2) for r in range(regions)]
    return {
        "mate": [(at(c, r), at(1 - c, r)) for c, r in both],
        "direct": [(at(c, r), at(1 - c, r - 1 if c == 0 else r + 1)) for c, r in both],
        "early": [(at(c, r), at(c, r - 1 if c == 0 else r + 1)) for c, r in both],
        "late": [(at(c, r), at(c, r + 1 if c == 0 else r - 1)) for c, r in both],
    }


def dft_blocks():
    index = np.arange(SIDE)
    angles = (index[:, None] * index[None, :] % SIDE) * (2.0 * np.pi / SIDE)
    real = np.cos(angles) / np.sqrt(SIDE)
    imag = -np.sin(angles) / np.sqrt(SIDE)
    first = np.block([[real, -imag], [imag, real]]).astype(ml_dtypes.bfloat16)
    second = np.block([[real, imag], [-imag, real]]).astype(ml_dtypes.bfloat16)
    return first, second


def places(rows):
    up = [rows[i] < 0 for i in range(4)]
    first = lambda a, b: jnp.where(a, 0, jnp.where(b, 1, 2))
    last = lambda a, b: jnp.where(a, 3, jnp.where(b, 2, 1))
    no = [jnp.logical_not(u) for u in up]
    return first(up[0], up[1]), last(up[3], up[2]), first(no[0], no[1]), last(no[3], no[2])


def column_split(left):
    base = jnp.minimum(lax.shift_right_logical(left, 7), (COLS - WIDE) // 128) * 128
    return pl.multiple_of(base, 128), left - base


def row_split(top, most):
    base = jnp.minimum(lax.shift_right_logical(top, 3), most // 8) * 8
    return pl.multiple_of(base, 8), top - base


def cut_window(load, top, left, count, total):
    row_base, row_shift = row_split(top, total - count - 8)
    col_base, col_shift = column_split(left)
    block = load(pl.ds(row_base, count + 8), pl.ds(col_base, WIDE))
    block = pltpu.roll(block, lax.rem(count + 8 - row_shift, count + 8), 0)[:count]
    return pltpu.roll(block, lax.rem(WIDE - col_shift, WIDE), 1)[:, :SIDE]


def put_window(total_ref, channel, top, left, block):
    count = block.shape[0]
    row_base, row_shift = row_split(top, EXT - count - 8)
    col_base, col_shift = column_split(left)
    block = jnp.concatenate([block, jnp.zeros((count, WIDE - SIDE), F32)], axis=1)
    block = pltpu.roll(block, col_shift, 1)
    block = jnp.concatenate([block, jnp.zeros((8, WIDE), F32)], axis=0)
    block = pltpu.roll(block, row_shift, 0)
    where = (channel, pl.ds(row_base, count + 8), pl.ds(col_base, WIDE))
    total_ref[where] = total_ref[where] + block


def tagged(rows, cols, spots):
    line = lax.broadcasted_iota(jnp.int32, (16, 128), 0)
    lane = lax.broadcasted_iota(jnp.int32, (16, 128), 1)
    tile = jnp.zeros((16, 128), jnp.int32)
    for k, spot in enumerate(spots):
        left = cols[spot]
        parts = (rows[spot] + HALF, lax.shift_right_logical(left, 3), jnp.bitwise_and(left, 7))
        for n, part in enumerate(parts):
            tile = jnp.where((line == k) & (lane == n), part, tile)
    return tile.astype(F32).astype(BF)


def edge_kernel(rows_in, cols_in, objects_in, early, late, objects, rows, cols, sems):
    cut = lax.axis_index("cuts")
    copies = [
        pltpu.make_async_copy(rows_in, rows, sems.at[0]),
        pltpu.make_async_copy(cols_in, cols, sems.at[1]),
        pltpu.make_async_copy(objects_in.at[0, 0], objects.at[0], sems.at[2]),
        pltpu.make_async_copy(objects_in.at[0, 1], objects.at[1], sems.at[3]),
    ]
    for copy in copies:
        copy.start()
    copies[0].wait()
    copies[1].wait()
    u0, u1, l0, l1 = places(rows)
    up = cut == 0
    early[EDGE:] = tagged(rows, cols, (jnp.where(up, u0, l0), jnp.where(up, u1, l1)))
    late[EDGE:] = tagged(rows, cols, (jnp.where(up, l0, u0), jnp.where(up, l1, u1)))
    start = pl.multiple_of(jnp.where(up, 0, HALF), HALF)
    for channel in range(2):
        copies[2 + channel].wait()
        for k in range(COLS // 128):
            where = pl.ds((channel * (COLS // 128) + k) * HALF, HALF)
            lanes = slice(128 * k, 128 * (k + 1))
            early[where] = objects[channel, pl.ds(start, HALF), lanes].astype(BF)
            late[where] = objects[channel, pl.ds(HALF - start, HALF), lanes].astype(BF)


def cut_pair(rows, cols, objects, edge, lower, spots, outputs, near):
    start = pl.multiple_of(jnp.where(lower, BAND, 0), HALF)
    own = pl.multiple_of(jnp.where(lower, 0, HALF), HALF)
    for channel in range(2):
        for k in range(COLS // 128):
            near[channel, pl.ds(start, HALF), 128 * k : 128 * (k + 1)] = edge[
                pl.ds((channel * (COLS // 128) + k) * HALF, HALF)
            ].astype(F32)
        near[channel, pl.ds(own, BAND)] = objects[channel]
        for spot, output in zip(spots, outputs):
            output[channel] = cut_window(
                lambda r, c: near[channel, r, c], rows[spot] + own, cols[spot], SIDE, BAND + HALF
            ).astype(BF)


def mate_kernel(rows, cols, objects, early, window0, window1, near):
    lower = lax.axis_index("cuts") == 0
    u0, u1, l0, l1 = places(rows)
    spots = jnp.where(lower, l0, u0), jnp.where(lower, l1, u1)
    cut_pair(rows, cols, objects, early, lower, spots, (window0, window1), near)


def own_windows_kernel(rows, cols, objects, early, late, window0, window1, spots, near):
    lower = lax.axis_index("cuts") == 1
    u0, u1, l0, l1 = places(rows)
    mine = jnp.where(lower, l0, u0), jnp.where(lower, l1, u1)
    cut_pair(rows, cols, objects, late, lower, mine, (window0, window1), near)
    decode(early, late, spots)


def decode(early, late, spots):
    line = lax.broadcasted_iota(jnp.int32, (16, 128), 0)
    lane = lax.broadcasted_iota(jnp.int32, (16, 128), 1)
    for n, edge in enumerate((early, late)):
        tile = edge[EDGE:].astype(F32)
        left = jnp.where(lane == 1, tile * 8.0, jnp.where(lane == 2, tile, 0.0))
        top = jnp.where(lane == 0, tile, 0.0)
        for k in range(2):
            for m, part in enumerate((top, left)):
                spots[4 * n + 2 * k + m] = jnp.sum(jnp.where(line == k, part, 0.0)).astype(jnp.int32)


def transform(fields, left, right):
    count = len(fields)
    stacked = jnp.concatenate(
        [jnp.concatenate([f[part].astype(BF) for f in fields], axis=1) for part in range(2)], axis=0
    )
    middle = jnp.dot(left, stacked, preferred_element_type=F32).astype(BF)
    spans = [slice(SIDE * k, SIDE * (k + 1)) for k in range(count)]
    middle = jnp.concatenate(
        [jnp.concatenate([middle[:SIDE, s], middle[SIDE:, s]], axis=1) for s in spans], axis=0
    )
    result = jnp.dot(middle, right, preferred_element_type=F32)
    return [(result[s, :SIDE], result[s, SIDE:]) for s in spans]


def times(a, b):
    return a[0] * b[0] - a[1] * b[1], a[0] * b[1] + a[1] * b[0]


def conj_times(a, b):
    return a[0] * b[0] + a[1] * b[1], a[0] * b[1] - a[1] * b[0]


def wide(pair):
    return pair[0].astype(F32), pair[1].astype(F32)


def chain(incoming, patches, measured, wave, first, second, store):
    spots = range(len(incoming))
    propagator = (wave[0], wave[1])
    fields = [times(wide(incoming[k]()), patches[k](0)) for k in spots]
    fields = [times(propagator, f) for f in transform(fields, first, second)]
    psi = [(f[0].astype(BF), f[1].astype(BF)) for f in transform(fields, second, first)]
    fields = [times(wide(psi[k]), patches[k](1)) for k in spots]
    detected = []
    for k, (real, imag) in enumerate(transform(fields, first, second)):
        modulus = jnp.sqrt(real * real + imag * imag)
        factor = 1.0 - measured[k]() / jnp.maximum(modulus, modulus_floor)
        detected.append((real * factor, imag * factor))
    arriving = [(f[0].astype(BF), f[1].astype(BF)) for f in transform(detected, second, first)]
    arriving = [wide(f) for f in arriving]
    for k in spots:
        store(k, 1, conj_times(wide(psi[k]), arriving[k]))
    fields = [conj_times(patches[k](1), arriving[k]) for k in spots]
    fields = [conj_times(propagator, f) for f in transform(fields, first, second)]
    for k, (real, imag) in enumerate(transform(fields, second, first)):
        arrived = real.astype(BF).astype(F32), imag.astype(BF).astype(F32)
        store(k, 0, conj_times(wide(incoming[k]()), arrived))


def solo_kernel(
    number, rows, picks, own, mate, probes, amplitudes, wave, first, second, *refs
):
    if number == 0:
        sent, kept, edges, held, made = refs
        sent_outer, sent_inband = sent.at[0], sent.at[1]
    else:
        before, sent_outer, sent_inband, kept, both, held, made = refs
        both[0] = before[...]
        edges = both.at[1]
    cut = lax.axis_index("cuts")
    spots = places(rows)
    place = jnp.where(cut == 0, spots[number], spots[2 + number])
    start = pl.multiple_of(jnp.where(cut == 0, 0, HALF), HALF)
    held[cut] = own[...]
    held[1 - cut] = mate[...]

    def store(k, which, value):
        made[which, 0], made[which, 1] = value

    chain(
        [lambda: (probes[picks[place], 0], probes[picks[place], 1])],
        [lambda which: wide((held[which, 0], held[which, 1]))],
        [lambda: amplitudes[place]],
        wave, first[...], second[...], store,
    )
    depth = sent_inband.shape[1]
    inner = pl.multiple_of(jnp.where(cut == 0, SIDE - depth, 0), 64)
    for channel in range(2):
        sent_outer[channel] = made[1 - cut, channel, pl.ds(start, HALF)].astype(BF)
        sent_inband[channel] = made[1 - cut, channel, pl.ds(inner, depth)].astype(BF)
        kept[channel] = made[cut, channel]
        edges[channel] = made[cut, channel, pl.ds(start, HALF)].astype(BF)


def put_inband(put, rows, cols, number, inband, channel):
    upper = lax.axis_index("cuts") == 1
    spots = places(rows)
    spot = jnp.where(upper, spots[number], spots[2 + number])
    skip = jnp.where(upper, SIDE - inband.shape[1], 0)
    put(rows[spot] + HALF + skip, cols[spot], inband[channel].astype(F32))
    return rows[spot] + HALF + jnp.where(upper, 0, HALF), cols[spot]


def own_kernel(rows, cols, kept0, kept1, back, total):
    cut = lax.axis_index("cuts")
    places_here = places(rows)
    total[...] = jnp.zeros_like(total)
    for channel in range(2):
        put = functools.partial(put_window, total, channel)
        for number, kept in enumerate((kept0, kept1)):
            spot = jnp.where(cut == 0, places_here[number], places_here[2 + number])
            put(rows[spot] + HALF, cols[spot], kept[channel])
        top, left = put_inband(put, rows, cols, 0, back.at[1], channel)
        put(top, left, back[0, channel].astype(F32))


def rest_kernel(
    rows, cols, spots, given, inband, edges, relay0, relay1, total, output, sems
):
    cut = lax.axis_index("cuts")
    shift = jnp.where(cut == 0, BAND, -HALF)
    copies = []
    for channel in range(2):
        put = functools.partial(put_window, total, channel)
        put_inband(put, rows, cols, 1, inband, channel)
        for number, relay in enumerate((relay0, relay1)):
            k = 2 * number
            put(spots[k] + shift, spots[k + 1], edges[number, channel].astype(F32))
            put(spots[4 + k] + BAND - HALF - shift, spots[5 + k], relay[channel].astype(F32))
        copies.append(
            pltpu.make_async_copy(
                total.at[channel, pl.ds(HALF, BAND)], output.at[0, channel], sems.at[channel]
            )
        )
        copies[channel].start()
    for copy in copies:
        copy.wait()


def call(kernel, name, inputs, outputs, scratch=(), in_specs=None, out_specs=None, aliases={}, vmem=40, flops=1):
    scalars = [x for x in inputs if x.dtype == jnp.int32]
    return pl.pallas_call(
        kernel,
        name=name,
        out_shape=outputs,
        in_specs=in_specs or [SM] * len(scalars) + [VM] * (len(inputs) - len(scalars)),
        out_specs=out_specs or [VM] * len(outputs),
        scratch_shapes=list(scratch),
        input_output_aliases=aliases,
        cost_estimate=pl.CostEstimate(flops=flops, bytes_accessed=1, transcendentals=0),
        compiler_params=pltpu.CompilerParams(vmem_limit_bytes=vmem << 20),
    )(*inputs)


def arr(*shape, dtype=BF):
    return jax.ShapeDtypeStruct(shape, dtype)


def shards(objects, probes, amplitudes, prop_phase, scan_rows, scan_cols, probe_choice):
    route = routes(lax.axis_size("region"))
    move = lambda x, way: lax.ppermute(x, AXES, route[way])
    first, second = (jnp.asarray(t) for t in dft_blocks())
    wave = jnp.stack([jnp.cos(prop_phase), jnp.sin(prop_phase)])
    half = arr(2, HALF, SIDE)

    full = arr(2, SIDE, SIDE)
    near = pltpu.VMEM((2, BAND + HALF, COLS), F32)
    early, late, band, rows, cols = call(
        edge_kernel, "edge",
        [pltpu.with_memory_space_constraint(x, pltpu.HBM) for x in (scan_rows, scan_cols, objects)],
        [arr(EDGE + 16, 128), arr(EDGE + 16, 128),
         arr(2, BAND, COLS, dtype=F32), arr(4, dtype=jnp.int32), arr(4, dtype=jnp.int32)],
        [pltpu.SemaphoreType.DMA((4,))],
        in_specs=[HB] * 3, out_specs=[VM] * 3 + [SM] * 2, vmem=50,
    )
    early = move(early, "early")
    late = move(late, "late")
    sent = call(mate_kernel, "mate", [rows, cols, band, early], [full, full], [near])
    mate0 = move(sent[0], "mate")
    own0, own1, spots = call(
        own_windows_kernel, "windows", [rows, cols, band, early, late],
        [full, full, arr(8, dtype=jnp.int32)], [near], out_specs=[VM, VM, SM],
    )
    sent1, own1 = lax.optimization_barrier((sent[1], own1))
    mate1 = move(sent1, "mate")
    optics = [probes, amplitudes, wave, first, second]
    work = [pltpu.VMEM((2, 2, SIDE, SIDE), BF), pltpu.VMEM((2, 2, SIDE, SIDE), F32)]
    wide_full = arr(2, SIDE, SIDE, dtype=F32)
    back0, kept0, edge0 = call(
        functools.partial(solo_kernel, 0), "solo0", [rows, probe_choice, own0, mate0] + optics,
        [arr(2, 2, HALF, SIDE), wide_full, half], work, flops=10**11,
    )
    back0 = move(back0, "mate")
    outer1, inband1, kept1, edges = call(
        functools.partial(solo_kernel, 1), "solo1",
        [rows, probe_choice, own1, mate1] + optics + [edge0],
        [half, arr(2, HALF + 64, SIDE), wide_full, arr(2, 2, HALF, SIDE)], work, flops=10**11,
    )
    inband1 = move(inband1, "mate")
    outer1, back0 = lax.optimization_barrier((outer1, back0))
    relay1 = move(outer1, "direct")
    edges = move(edges, "early")
    relay0 = move(back0[0], "late")
    (total,) = call(
        own_kernel, "own", [rows, cols, kept0, kept1, back0],
        [arr(2, EXT, COLS, dtype=F32)], flops=10**11,
    )
    _, gradient = call(
        rest_kernel, "rest",
        [rows, cols, spots, total, inband1, edges, relay0, relay1],
        [arr(2, EXT, COLS, dtype=F32), arr(1, 2, BAND, COLS, dtype=F32)],
        [pltpu.SemaphoreType.DMA((2,))],
        out_specs=[VM, HB],
        aliases={3: 0},
    )
    return gradient


def solution(mesh):
    return jax.shard_map(
        shards,
        mesh=mesh,
        in_specs=(
            P("cuts", None, "region", None),
            P(),
            P("region", None, None),
            P(),
            P("region"),
            P("region"),
            P("region"),
        ),
        out_specs=P("cuts", None, "region", None),
        check_vma=False,
    )
```

```python
import functools

import jax
import jax.numpy as jnp
import ml_dtypes
import numpy as np
from jax import lax
from jax.experimental import pallas as pl
from jax.experimental.pallas import tpu as pltpu
from jax.sharding import PartitionSpec as P

modulus_floor = 0.25
AXES = ("cuts", "region")
BF = jnp.bfloat16
F32 = jnp.float32
SIDE = 256
HALF = 128
BAND = 256
COLS = 1024
EXT = BAND + 2 * HALF
EDGE = 2 * HALF * COLS // 128
WIDE = SIDE + 128
VM = pl.BlockSpec(memory_space=pltpu.VMEM)
SM = pl.BlockSpec(memory_space=pltpu.SMEM)
HB = pl.BlockSpec(memory_space=pltpu.HBM)


def routes(regions):
    at = lambda c, r: c * regions + r % regions
    both = [(c, r) for c in range(2) for r in range(regions)]
    return {
        "mate": [(at(c, r), at(1 - c, r)) for c, r in both],
        "direct": [(at(c, r), at(1 - c, r - 1 if c == 0 else r + 1)) for c, r in both],
        "early": [(at(c, r), at(c, r - 1 if c == 0 else r + 1)) for c, r in both],
        "late": [(at(c, r), at(c, r + 1 if c == 0 else r - 1)) for c, r in both],
    }


def dft_blocks():
    index = np.arange(SIDE)
    angles = (index[:, None] * index[None, :] % SIDE) * (2.0 * np.pi / SIDE)
    real = np.cos(angles) / np.sqrt(SIDE)
    imag = -np.sin(angles) / np.sqrt(SIDE)
    first = np.block([[real, -imag], [imag, real]]).astype(ml_dtypes.bfloat16)
    second = np.block([[real, imag], [-imag, real]]).astype(ml_dtypes.bfloat16)
    return first, second


def places(rows):
    up = [rows[i] < 0 for i in range(4)]
    first = lambda a, b: jnp.where(a, 0, jnp.where(b, 1, 2))
    last = lambda a, b: jnp.where(a, 3, jnp.where(b, 2, 1))
    no = [jnp.logical_not(u) for u in up]
    return first(up[0], up[1]), last(up[3], up[2]), first(no[0], no[1]), last(no[3], no[2])


def column_split(left):
    base = jnp.minimum(lax.shift_right_logical(left, 7), (COLS - WIDE) // 128) * 128
    return pl.multiple_of(base, 128), left - base


def row_split(top, most):
    base = jnp.minimum(lax.shift_right_logical(top, 3), most // 8) * 8
    return pl.multiple_of(base, 8), top - base


def cut_window(load, top, left, count, total):
    row_base, row_shift = row_split(top, total - count - 8)
    col_base, col_shift = column_split(left)
    block = load(pl.ds(row_base, count + 8), pl.ds(col_base, WIDE))
    block = pltpu.roll(block, lax.rem(count + 8 - row_shift, count + 8), 0)[:count]
    return pltpu.roll(block, lax.rem(WIDE - col_shift, WIDE), 1)[:, :SIDE]


def put_window(total_ref, channel, top, left, block):
    count = block.shape[0]
    row_base, row_shift = row_split(top, EXT - count - 8)
    col_base, col_shift = column_split(left)
    block = jnp.concatenate([block, jnp.zeros((count, WIDE - SIDE), F32)], axis=1)
    block = pltpu.roll(block, col_shift, 1)
    block = jnp.concatenate([block, jnp.zeros((8, WIDE), F32)], axis=0)
    block = pltpu.roll(block, row_shift, 0)
    where = (channel, pl.ds(row_base, count + 8), pl.ds(col_base, WIDE))
    total_ref[where] = total_ref[where] + block


def tagged(rows, cols, spots):
    line = lax.broadcasted_iota(jnp.int32, (16, 128), 0)
    lane = lax.broadcasted_iota(jnp.int32, (16, 128), 1)
    tile = jnp.zeros((16, 128), jnp.int32)
    for k, spot in enumerate(spots):
        left = cols[spot]
        parts = (rows[spot] + HALF, lax.shift_right_logical(left, 3), jnp.bitwise_and(left, 7))
        for n, part in enumerate(parts):
            tile = jnp.where((line == k) & (lane == n), part, tile)
    return tile.astype(F32).astype(BF)


def edge_kernel(rows_in, cols_in, objects_in, early, late, objects, rows, cols, sems):
    cut = lax.axis_index("cuts")
    copies = [
        pltpu.make_async_copy(rows_in, rows, sems.at[0]),
        pltpu.make_async_copy(cols_in, cols, sems.at[1]),
        pltpu.make_async_copy(objects_in.at[0, 0], objects.at[0], sems.at[2]),
        pltpu.make_async_copy(objects_in.at[0, 1], objects.at[1], sems.at[3]),
    ]
    for copy in copies:
        copy.start()
    copies[0].wait()
    copies[1].wait()
    u0, u1, l0, l1 = places(rows)
    up = cut == 0
    early[EDGE:] = tagged(rows, cols, (jnp.where(up, u0, l0), jnp.where(up, u1, l1)))
    late[EDGE:] = tagged(rows, cols, (jnp.where(up, l0, u0), jnp.where(up, l1, u1)))
    start = pl.multiple_of(jnp.where(up, 0, HALF), HALF)
    for channel in range(2):
        copies[2 + channel].wait()
        for k in range(COLS // 128):
            where = pl.ds((channel * (COLS // 128) + k) * HALF, HALF)
            lanes = slice(128 * k, 128 * (k + 1))
            early[where] = objects[channel, pl.ds(start, HALF), lanes].astype(BF)
            late[where] = objects[channel, pl.ds(HALF - start, HALF), lanes].astype(BF)


def cut_pair(rows, cols, objects, edge, lower, spots, outputs, near):
    start = pl.multiple_of(jnp.where(lower, BAND, 0), HALF)
    own = pl.multiple_of(jnp.where(lower, 0, HALF), HALF)
    for channel in range(2):
        for k in range(COLS // 128):
            near[channel, pl.ds(start, HALF), 128 * k : 128 * (k + 1)] = edge[
                pl.ds((channel * (COLS // 128) + k) * HALF, HALF)
            ].astype(F32)
        near[channel, pl.ds(own, BAND)] = objects[channel]
        for spot, output in zip(spots, outputs):
            output[channel] = cut_window(
                lambda r, c: near[channel, r, c], rows[spot] + own, cols[spot], SIDE, BAND + HALF
            ).astype(BF)


def mate_kernel(rows, cols, objects, early, window0, window1, near):
    lower = lax.axis_index("cuts") == 0
    u0, u1, l0, l1 = places(rows)
    spots = jnp.where(lower, l0, u0), jnp.where(lower, l1, u1)
    cut_pair(rows, cols, objects, early, lower, spots, (window0, window1), near)


def own_windows_kernel(rows, cols, objects, early, late, window0, window1, spots, near):
    lower = lax.axis_index("cuts") == 1
    u0, u1, l0, l1 = places(rows)
    mine = jnp.where(lower, l0, u0), jnp.where(lower, l1, u1)
    cut_pair(rows, cols, objects, late, lower, mine, (window0, window1), near)
    decode(early, late, spots)


def decode(early, late, spots):
    line = lax.broadcasted_iota(jnp.int32, (16, 128), 0)
    lane = lax.broadcasted_iota(jnp.int32, (16, 128), 1)
    for n, edge in enumerate((early, late)):
        tile = edge[EDGE:].astype(F32)
        left = jnp.where(lane == 1, tile * 8.0, jnp.where(lane == 2, tile, 0.0))
        top = jnp.where(lane == 0, tile, 0.0)
        for k in range(2):
            for m, part in enumerate((top, left)):
                spots[4 * n + 2 * k + m] = jnp.sum(jnp.where(line == k, part, 0.0)).astype(jnp.int32)


def transform(fields, left, right):
    count = len(fields)
    stacked = jnp.concatenate(
        [jnp.concatenate([f[part].astype(BF) for f in fields], axis=1) for part in range(2)], axis=0
    )
    middle = jnp.dot(left, stacked, preferred_element_type=F32).astype(BF)
    spans = [slice(SIDE * k, SIDE * (k + 1)) for k in range(count)]
    middle = jnp.concatenate(
        [jnp.concatenate([middle[:SIDE, s], middle[SIDE:, s]], axis=1) for s in spans], axis=0
    )
    result = jnp.dot(middle, right, preferred_element_type=F32)
    return [(result[s, :SIDE], result[s, SIDE:]) for s in spans]


def times(a, b):
    return a[0] * b[0] - a[1] * b[1], a[0] * b[1] + a[1] * b[0]


def conj_times(a, b):
    return a[0] * b[0] + a[1] * b[1], a[0] * b[1] - a[1] * b[0]


def wide(pair):
    return pair[0].astype(F32), pair[1].astype(F32)


def chain(incoming, patches, measured, wave, first, second, store):
    spots = range(len(incoming))
    propagator = (wave[0], wave[1])
    fields = [times(wide(incoming[k]()), patches[k](0)) for k in spots]
    fields = [times(propagator, f) for f in transform(fields, first, second)]
    psi = [(f[0].astype(BF), f[1].astype(BF)) for f in transform(fields, second, first)]
    fields = [times(wide(psi[k]), patches[k](1)) for k in spots]
    detected = []
    for k, (real, imag) in enumerate(transform(fields, first, second)):
        modulus = jnp.sqrt(real * real + imag * imag)
        factor = 1.0 - measured[k]() / jnp.maximum(modulus, modulus_floor)
        detected.append((real * factor, imag * factor))
    arriving = [(f[0].astype(BF), f[1].astype(BF)) for f in transform(detected, second, first)]
    arriving = [wide(f) for f in arriving]
    for k in spots:
        store(k, 1, conj_times(wide(psi[k]), arriving[k]))
    fields = [conj_times(patches[k](1), arriving[k]) for k in spots]
    fields = [conj_times(propagator, f) for f in transform(fields, first, second)]
    for k, (real, imag) in enumerate(transform(fields, second, first)):
        arrived = real.astype(BF).astype(F32), imag.astype(BF).astype(F32)
        store(k, 0, conj_times(wide(incoming[k]()), arrived))


def solo_kernel(
    number, rows, picks, own, mate, probes, amplitudes, wave, first, second, *refs
):
    if number == 0:
        sent_outer, sent_inband, kept, edges, held, made = refs
    else:
        outer_before, edge_before, outers, sent_inband, kept, both, held, made = refs
        outers[0] = outer_before[...]
        both[0] = edge_before[...]
        sent_outer, edges = outers.at[1], both.at[1]
    cut = lax.axis_index("cuts")
    spots = places(rows)
    place = jnp.where(cut == 0, spots[number], spots[2 + number])
    start = pl.multiple_of(jnp.where(cut == 0, 0, HALF), HALF)
    held[cut] = own[...]
    held[1 - cut] = mate[...]

    def store(k, which, value):
        made[which, 0], made[which, 1] = value

    chain(
        [lambda: (probes[picks[place], 0], probes[picks[place], 1])],
        [lambda which: wide((held[which, 0], held[which, 1]))],
        [lambda: amplitudes[place]],
        wave, first[...], second[...], store,
    )
    depth = sent_inband.shape[1]
    inner = pl.multiple_of(jnp.where(cut == 0, SIDE - depth, 0), 64)
    for channel in range(2):
        sent_outer[channel] = made[1 - cut, channel, pl.ds(start, HALF)].astype(BF)
        sent_inband[channel] = made[1 - cut, channel, pl.ds(inner, depth)].astype(BF)
        kept[channel] = made[cut, channel]
        edges[channel] = made[cut, channel, pl.ds(start, HALF)].astype(BF)


def put_inband(put, rows, cols, number, inband, channel):
    upper = lax.axis_index("cuts") == 1
    spots = places(rows)
    spot = jnp.where(upper, spots[number], spots[2 + number])
    skip = jnp.where(upper, SIDE - inband.shape[1], 0)
    put(rows[spot] + HALF + skip, cols[spot], inband[channel].astype(F32))


def own_kernel(rows, cols, kept0, kept1, inband, total):
    cut = lax.axis_index("cuts")
    places_here = places(rows)
    total[...] = jnp.zeros_like(total)
    for channel in range(2):
        put = functools.partial(put_window, total, channel)
        for number, kept in enumerate((kept0, kept1)):
            spot = jnp.where(cut == 0, places_here[number], places_here[2 + number])
            put(rows[spot] + HALF, cols[spot], kept[channel])
        put_inband(put, rows, cols, 0, inband, channel)


def rest_kernel(
    rows, cols, spots, given, inband, outers, edges, total, output, sems
):
    cut = lax.axis_index("cuts")
    shift = jnp.where(cut == 0, BAND, -HALF)
    copies = []
    for channel in range(2):
        put = functools.partial(put_window, total, channel)
        put_inband(put, rows, cols, 1, inband, channel)
        for number in range(2):
            k = 2 * number
            put(spots[k] + shift, spots[k + 1], edges[number, channel].astype(F32))
            top = spots[4 + k] + BAND - HALF - shift
            put(top, spots[5 + k], outers[number, channel].astype(F32))
        copies.append(
            pltpu.make_async_copy(
                total.at[channel, pl.ds(HALF, BAND)], output.at[0, channel], sems.at[channel]
            )
        )
        copies[channel].start()
    for copy in copies:
        copy.wait()


def call(kernel, name, inputs, outputs, scratch=(), in_specs=None, out_specs=None, aliases={}, vmem=40, flops=1):
    scalars = [x for x in inputs if x.dtype == jnp.int32]
    return pl.pallas_call(
        kernel,
        name=name,
        out_shape=outputs,
        in_specs=in_specs or [SM] * len(scalars) + [VM] * (len(inputs) - len(scalars)),
        out_specs=out_specs or [VM] * len(outputs),
        scratch_shapes=list(scratch),
        input_output_aliases=aliases,
        cost_estimate=pl.CostEstimate(flops=flops, bytes_accessed=1, transcendentals=0),
        compiler_params=pltpu.CompilerParams(vmem_limit_bytes=vmem << 20),
    )(*inputs)


def arr(*shape, dtype=BF):
    return jax.ShapeDtypeStruct(shape, dtype)


def shards(objects, probes, amplitudes, prop_phase, scan_rows, scan_cols, probe_choice):
    route = routes(lax.axis_size("region"))
    move = lambda x, way: lax.ppermute(x, AXES, route[way])
    first, second = (jnp.asarray(t) for t in dft_blocks())
    wave = jnp.stack([jnp.cos(prop_phase), jnp.sin(prop_phase)])
    half = arr(2, HALF, SIDE)

    full = arr(2, SIDE, SIDE)
    near = pltpu.VMEM((2, BAND + HALF, COLS), F32)
    early, late, band, rows, cols = call(
        edge_kernel, "edge",
        [pltpu.with_memory_space_constraint(x, pltpu.HBM) for x in (scan_rows, scan_cols, objects)],
        [arr(EDGE + 16, 128), arr(EDGE + 16, 128),
         arr(2, BAND, COLS, dtype=F32), arr(4, dtype=jnp.int32), arr(4, dtype=jnp.int32)],
        [pltpu.SemaphoreType.DMA((4,))],
        in_specs=[HB] * 3, out_specs=[VM] * 3 + [SM] * 2, vmem=50,
    )
    early = move(early, "early")
    late = move(late, "late")
    sent = call(mate_kernel, "mate", [rows, cols, band, early], [full, full], [near])
    mate0 = move(sent[0], "mate")
    own0, own1, spots = call(
        own_windows_kernel, "windows", [rows, cols, band, early, late],
        [full, full, arr(8, dtype=jnp.int32)], [near], out_specs=[VM, VM, SM],
    )
    sent1, own1 = lax.optimization_barrier((sent[1], own1))
    mate1 = move(sent1, "mate")
    optics = [probes, amplitudes, wave, first, second]
    work = [pltpu.VMEM((2, 2, SIDE, SIDE), BF), pltpu.VMEM((2, 2, SIDE, SIDE), F32)]
    wide_full = arr(2, SIDE, SIDE, dtype=F32)
    inner = arr(2, HALF + 64, SIDE)
    pair = arr(2, 2, HALF, SIDE)
    outer0, inband0, kept0, edge0 = call(
        functools.partial(solo_kernel, 0), "solo0", [rows, probe_choice, own0, mate0] + optics,
        [half, inner, wide_full, half], work, flops=10**11,
    )
    inband0 = move(inband0, "mate")
    outers, inband1, kept1, edges = call(
        functools.partial(solo_kernel, 1), "solo1",
        [rows, probe_choice, own1, mate1] + optics + [outer0, edge0],
        [pair, inner, wide_full, pair], work, flops=10**11,
    )
    inband1 = move(inband1, "mate")
    outers = move(outers, "direct")
    edges = move(edges, "early")
    (total,) = call(
        own_kernel, "own", [rows, cols, kept0, kept1, inband0],
        [arr(2, EXT, COLS, dtype=F32)], flops=10**11,
    )
    _, gradient = call(
        rest_kernel, "rest", [rows, cols, spots, total, inband1, outers, edges],
        [arr(2, EXT, COLS, dtype=F32), arr(1, 2, BAND, COLS, dtype=F32)],
        [pltpu.SemaphoreType.DMA((2,))],
        out_specs=[VM, HB],
        aliases={3: 0},
    )
    return gradient


def solution(mesh):
    return jax.shard_map(
        shards,
        mesh=mesh,
        in_specs=(
            P("cuts", None, "region", None),
            P(),
            P("region", None, None),
            P(),
            P("region"),
            P("region"),
            P("region"),
        ),
        out_specs=P("cuts", None, "region", None),
        check_vma=False,
    )
```

```python
import functools

import jax
import jax.numpy as jnp
import ml_dtypes
import numpy as np
from jax import lax
from jax.experimental import pallas as pl
from jax.experimental.pallas import tpu as pltpu
from jax.sharding import PartitionSpec as P

modulus_floor = 0.25
AXES = ("cuts", "region")
BF = jnp.bfloat16
F32 = jnp.float32
SIDE = 256
HALF = 128
BAND = 256
COLS = 1024
EXT = BAND + 2 * HALF
EDGE = 2 * HALF * COLS // 128
WIDE = SIDE + 128
VM = pl.BlockSpec(memory_space=pltpu.VMEM)
SM = pl.BlockSpec(memory_space=pltpu.SMEM)
HB = pl.BlockSpec(memory_space=pltpu.HBM)


def routes(regions):
    at = lambda c, r: c * regions + r % regions
    both = [(c, r) for c in range(2) for r in range(regions)]
    return {
        "mate": [(at(c, r), at(1 - c, r)) for c, r in both],
        "direct": [(at(c, r), at(1 - c, r - 1 if c == 0 else r + 1)) for c, r in both],
        "early": [(at(c, r), at(c, r - 1 if c == 0 else r + 1)) for c, r in both],
        "late": [(at(c, r), at(c, r + 1 if c == 0 else r - 1)) for c, r in both],
    }


def dft_blocks():
    index = np.arange(SIDE)
    angles = (index[:, None] * index[None, :] % SIDE) * (2.0 * np.pi / SIDE)
    real = np.cos(angles) / np.sqrt(SIDE)
    imag = -np.sin(angles) / np.sqrt(SIDE)
    first = np.block([[real, -imag], [imag, real]]).astype(ml_dtypes.bfloat16)
    second = np.block([[real, imag], [-imag, real]]).astype(ml_dtypes.bfloat16)
    return first, second


def places(rows):
    up = [rows[i] < 0 for i in range(4)]
    first = lambda a, b: jnp.where(a, 0, jnp.where(b, 1, 2))
    last = lambda a, b: jnp.where(a, 3, jnp.where(b, 2, 1))
    no = [jnp.logical_not(u) for u in up]
    return first(up[0], up[1]), last(up[3], up[2]), first(no[0], no[1]), last(no[3], no[2])


def column_split(left):
    base = jnp.minimum(lax.shift_right_logical(left, 7), (COLS - WIDE) // 128) * 128
    return pl.multiple_of(base, 128), left - base


def row_split(top, most):
    base = jnp.minimum(lax.shift_right_logical(top, 3), most // 8) * 8
    return pl.multiple_of(base, 8), top - base


def cut_window(load, top, left, count, total):
    row_base, row_shift = row_split(top, total - count - 8)
    col_base, col_shift = column_split(left)
    block = load(pl.ds(row_base, count + 8), pl.ds(col_base, WIDE))
    block = pltpu.roll(block, lax.rem(count + 8 - row_shift, count + 8), 0)[:count]
    return pltpu.roll(block, lax.rem(WIDE - col_shift, WIDE), 1)[:, :SIDE]


def put_window(total_ref, channel, top, left, block):
    count = block.shape[0]
    row_base, row_shift = row_split(top, EXT - count - 8)
    col_base, col_shift = column_split(left)
    block = jnp.concatenate([block, jnp.zeros((count, WIDE - SIDE), F32)], axis=1)
    block = pltpu.roll(block, col_shift, 1)
    block = jnp.concatenate([block, jnp.zeros((8, WIDE), F32)], axis=0)
    block = pltpu.roll(block, row_shift, 0)
    where = (channel, pl.ds(row_base, count + 8), pl.ds(col_base, WIDE))
    total_ref[where] = total_ref[where] + block


def put_near(total_ref, channel, top, left, block, near):
    row = pl.multiple_of(HALF + near, HALF)
    col_base, col_shift = column_split(left)
    shift = top - row
    block = jnp.concatenate([block, jnp.zeros((HALF, WIDE - SIDE), F32)], axis=1)
    block = pltpu.roll(block, col_shift, 1)
    block = pltpu.roll(block, lax.rem(shift + 2 * HALF, HALF), 0)
    line = lax.broadcasted_iota(jnp.int32, block.shape, 0)
    kept = jnp.where((line >= shift) & (line < shift + HALF), block, 0.0)
    where = (channel, pl.ds(row, HALF), pl.ds(col_base, WIDE))
    total_ref[where] = total_ref[where] + kept


def tagged(rows, cols, spots):
    line = lax.broadcasted_iota(jnp.int32, (16, 128), 0)
    lane = lax.broadcasted_iota(jnp.int32, (16, 128), 1)
    tile = jnp.zeros((16, 128), jnp.int32)
    for k, spot in enumerate(spots):
        left = cols[spot]
        parts = (rows[spot] + HALF, lax.shift_right_logical(left, 3), jnp.bitwise_and(left, 7))
        for n, part in enumerate(parts):
            tile = jnp.where((line == k) & (lane == n), part, tile)
    return tile.astype(F32).astype(BF)


def edge_kernel(rows_in, cols_in, objects_in, early, late, objects, rows, cols, sems):
    cut = lax.axis_index("cuts")
    copies = [
        pltpu.make_async_copy(rows_in, rows, sems.at[0]),
        pltpu.make_async_copy(cols_in, cols, sems.at[1]),
        pltpu.make_async_copy(objects_in.at[0, 0], objects.at[0], sems.at[2]),
        pltpu.make_async_copy(objects_in.at[0, 1], objects.at[1], sems.at[3]),
    ]
    for copy in copies:
        copy.start()
    copies[0].wait()
    copies[1].wait()
    u0, u1, l0, l1 = places(rows)
    up = cut == 0
    early[EDGE:] = tagged(rows, cols, (jnp.where(up, u0, l0), jnp.where(up, u1, l1)))
    late[EDGE:] = tagged(rows, cols, (jnp.where(up, l0, u0), jnp.where(up, l1, u1)))
    start = pl.multiple_of(jnp.where(up, 0, HALF), HALF)
    for channel in range(2):
        copies[2 + channel].wait()
        for k in range(COLS // 128):
            where = pl.ds((channel * (COLS // 128) + k) * HALF, HALF)
            lanes = slice(128 * k, 128 * (k + 1))
            early[where] = objects[channel, pl.ds(start, HALF), lanes].astype(BF)
            late[where] = objects[channel, pl.ds(HALF - start, HALF), lanes].astype(BF)


def strip_window(rows, cols, objects, edge, lower, spot, output, near):
    start = pl.multiple_of(jnp.where(lower, BAND, 0), HALF)
    own = pl.multiple_of(jnp.where(lower, 0, HALF), HALF)
    col_base, col_shift = column_split(cols[spot])
    row_base, row_shift = row_split(rows[spot] + own, HALF + BAND - SIDE - 8)
    count = SIDE + 8
    for channel in range(2):
        first = channel * COLS + col_base
        for k in range(WIDE // 128):
            near[channel, pl.ds(start, HALF), 128 * k : 128 * (k + 1)] = edge[
                pl.ds(pl.multiple_of(first + HALF * k, HALF), HALF)
            ].astype(F32)
        near[channel, pl.ds(own, BAND)] = objects[channel, :, pl.ds(col_base, WIDE)]
        block = near[channel, pl.ds(row_base, count)]
        block = pltpu.roll(block, lax.rem(count - row_shift, count), 0)[:SIDE]
        block = pltpu.roll(block, lax.rem(WIDE - col_shift, WIDE), 1)[:, :SIDE]
        output[channel] = block.astype(BF)


def mate_kernel(rows, cols, objects, early, window, near):
    lower = lax.axis_index("cuts") == 0
    u0, u1, l0, l1 = places(rows)
    spot = jnp.where(lower, l0, u0)
    strip_window(rows, cols, objects, early, lower, spot, window, near)


def windows_kernel(rows, cols, objects, early, late, sent, own0, own1, spots, near):
    lower = lax.axis_index("cuts") == 1
    u0, u1, l0, l1 = places(rows)
    other = jnp.where(lower, u1, l1)
    strip_window(rows, cols, objects, early, jnp.logical_not(lower), other, sent, near)
    for spot, output in ((jnp.where(lower, l0, u0), own0), (jnp.where(lower, l1, u1), own1)):
        strip_window(rows, cols, objects, late, lower, spot, output, near)
    decode(early, late, spots)


def decode(early, late, spots):
    line = lax.broadcasted_iota(jnp.int32, (16, 128), 0)
    lane = lax.broadcasted_iota(jnp.int32, (16, 128), 1)
    for n, edge in enumerate((early, late)):
        tile = edge[EDGE:].astype(F32)
        left = jnp.where(lane == 1, tile * 8.0, jnp.where(lane == 2, tile, 0.0))
        top = jnp.where(lane == 0, tile, 0.0)
        for k in range(2):
            for m, part in enumerate((top, left)):
                spots[4 * n + 2 * k + m] = jnp.sum(jnp.where(line == k, part, 0.0)).astype(jnp.int32)


def transform(fields, left, right):
    count = len(fields)
    stacked = jnp.concatenate(
        [jnp.concatenate([f[part].astype(BF) for f in fields], axis=1) for part in range(2)], axis=0
    )
    middle = jnp.dot(left, stacked, preferred_element_type=F32).astype(BF)
    spans = [slice(SIDE * k, SIDE * (k + 1)) for k in range(count)]
    middle = jnp.concatenate(
        [jnp.concatenate([middle[:SIDE, s], middle[SIDE:, s]], axis=1) for s in spans], axis=0
    )
    result = jnp.dot(middle, right, preferred_element_type=F32)
    return [(result[s, :SIDE], result[s, SIDE:]) for s in spans]


def times(a, b):
    return a[0] * b[0] - a[1] * b[1], a[0] * b[1] + a[1] * b[0]


def conj_times(a, b):
    return a[0] * b[0] + a[1] * b[1], a[0] * b[1] - a[1] * b[0]


def wide(pair):
    return pair[0].astype(F32), pair[1].astype(F32)


def chain(incoming, patches, measured, wave, first, second, store):
    spots = range(len(incoming))
    propagator = (wave[0], wave[1])
    fields = [times(wide(incoming[k]()), patches[k](0)) for k in spots]
    fields = [times(propagator, f) for f in transform(fields, first, second)]
    psi = [(f[0].astype(BF), f[1].astype(BF)) for f in transform(fields, second, first)]
    fields = [times(wide(psi[k]), patches[k](1)) for k in spots]
    detected = []
    for k, (real, imag) in enumerate(transform(fields, first, second)):
        modulus = jnp.sqrt(real * real + imag * imag)
        factor = 1.0 - measured[k]() / jnp.maximum(modulus, modulus_floor)
        detected.append((real * factor, imag * factor))
    arriving = [(f[0].astype(BF), f[1].astype(BF)) for f in transform(detected, second, first)]
    arriving = [wide(f) for f in arriving]
    for k in spots:
        store(k, 1, conj_times(wide(psi[k]), arriving[k]))
    fields = [conj_times(patches[k](1), arriving[k]) for k in spots]
    fields = [conj_times(propagator, f) for f in transform(fields, first, second)]
    for k, (real, imag) in enumerate(transform(fields, second, first)):
        arrived = real.astype(BF).astype(F32), imag.astype(BF).astype(F32)
        store(k, 0, conj_times(wide(incoming[k]()), arrived))


def solo_kernel(
    number, rows, picks, own, mate, probes, amplitudes, wave, first, second, *refs
):
    if number == 0:
        sent_outer, sent_inband, kept, edges, held, made = refs
    else:
        outer_before, edge_before, outers, sent_inband, kept, both, held, made = refs
        outers[0] = outer_before[...]
        both[0] = edge_before[...]
        sent_outer, edges = outers.at[1], both.at[1]
    cut = lax.axis_index("cuts")
    spots = places(rows)
    place = jnp.where(cut == 0, spots[number], spots[2 + number])
    start = pl.multiple_of(jnp.where(cut == 0, 0, HALF), HALF)
    held[cut] = own[...]
    held[1 - cut] = mate[...]

    def store(k, which, value):
        made[which, 0], made[which, 1] = value

    chain(
        [lambda: (probes[picks[place], 0], probes[picks[place], 1])],
        [lambda which: wide((held[which, 0], held[which, 1]))],
        [lambda: amplitudes[place]],
        wave, first[...], second[...], store,
    )
    depth = sent_inband.shape[1]
    inner = pl.multiple_of(jnp.where(cut == 0, SIDE - depth, 0), 64)
    for channel in range(2):
        sent_outer[channel] = made[1 - cut, channel, pl.ds(start, HALF)].astype(BF)
        sent_inband[channel] = made[1 - cut, channel, pl.ds(inner, depth)].astype(BF)
        kept[channel] = made[cut, channel]
        edges[channel] = made[cut, channel, pl.ds(start, HALF)].astype(BF)


def put_inband(put, rows, cols, number, inband, channel):
    upper = lax.axis_index("cuts") == 1
    spots = places(rows)
    spot = jnp.where(upper, spots[number], spots[2 + number])
    skip = jnp.where(upper, SIDE - inband.shape[1], 0)
    put(rows[spot] + HALF + skip, cols[spot], inband[channel].astype(F32))


def own_kernel(rows, cols, kept0, kept1, inband, total):
    cut = lax.axis_index("cuts")
    places_here = places(rows)
    total[...] = jnp.zeros_like(total)
    for channel in range(2):
        put = functools.partial(put_window, total, channel)
        for number, kept in enumerate((kept0, kept1)):
            spot = jnp.where(cut == 0, places_here[number], places_here[2 + number])
            put(rows[spot] + HALF, cols[spot], kept[channel])
        put_inband(put, rows, cols, 0, inband, channel)


def half_copy(total, output, channel, start, sem):
    return pltpu.make_async_copy(
        total.at[channel, pl.ds(pl.multiple_of(HALF + start, HALF), HALF)],
        output.at[0, channel, pl.ds(pl.multiple_of(start, HALF), HALF)],
        sem,
    )


def more_kernel(rows, cols, spots, given, inband, edges, total, output, sems):
    cut = lax.axis_index("cuts")
    shift = jnp.where(cut == 0, BAND, -HALF)
    far = jnp.where(cut == 0, HALF, 0)
    copies = []
    for channel in range(2):
        put = functools.partial(put_window, total, channel)
        put_inband(put, rows, cols, 1, inband, channel)
        for k in range(2):
            put(spots[2 * k] + shift, spots[2 * k + 1], edges[k, channel].astype(F32))
        copies.append(half_copy(total, output, channel, far, sems.at[channel]))
        copies[channel].start()
    for copy in copies:
        copy.wait()


def last_kernel(spots, given, outers, written, total, output, sems):
    cut = lax.axis_index("cuts")
    near = jnp.where(cut == 0, 0, HALF)
    shift = jnp.where(cut == 0, -HALF, BAND)
    copies = []
    for channel in range(2):
        for k in range(2):
            top, left = spots[4 + 2 * k] + shift, spots[5 + 2 * k]
            put_near(total, channel, top, left, outers[k, channel].astype(F32), near)
        copies.append(half_copy(total, output, channel, near, sems.at[channel]))
        copies[channel].start()
    for copy in copies:
        copy.wait()


def call(kernel, name, inputs, outputs, scratch=(), in_specs=None, out_specs=None, aliases={}, vmem=40, flops=1):
    scalars = [x for x in inputs if x.dtype == jnp.int32]
    return pl.pallas_call(
        kernel,
        name=name,
        out_shape=outputs,
        in_specs=in_specs or [SM] * len(scalars) + [VM] * (len(inputs) - len(scalars)),
        out_specs=out_specs or [VM] * len(outputs),
        scratch_shapes=list(scratch),
        input_output_aliases=aliases,
        cost_estimate=pl.CostEstimate(flops=flops, bytes_accessed=1, transcendentals=0),
        compiler_params=pltpu.CompilerParams(vmem_limit_bytes=vmem << 20),
    )(*inputs)


def arr(*shape, dtype=BF):
    return jax.ShapeDtypeStruct(shape, dtype)


def shards(objects, probes, amplitudes, prop_phase, scan_rows, scan_cols, probe_choice):
    route = routes(lax.axis_size("region"))
    move = lambda x, way: lax.ppermute(x, AXES, route[way])
    first, second = (jnp.asarray(t) for t in dft_blocks())
    wave = jnp.stack([jnp.cos(prop_phase), jnp.sin(prop_phase)])
    half = arr(2, HALF, SIDE)

    full = arr(2, SIDE, SIDE)
    near = pltpu.VMEM((2, BAND + HALF, WIDE), F32)
    early, late, band, rows, cols = call(
        edge_kernel, "edge",
        [pltpu.with_memory_space_constraint(x, pltpu.HBM) for x in (scan_rows, scan_cols, objects)],
        [arr(EDGE + 16, 128), arr(EDGE + 16, 128),
         arr(2, BAND, COLS, dtype=F32), arr(4, dtype=jnp.int32), arr(4, dtype=jnp.int32)],
        [pltpu.SemaphoreType.DMA((4,))],
        in_specs=[HB] * 3, out_specs=[VM] * 3 + [SM] * 2, vmem=50,
    )
    early = move(early, "early")
    late = move(late, "late")
    (sent0,) = call(mate_kernel, "mate", [rows, cols, band, early], [full], [near])
    mate0 = move(sent0, "mate")
    sent1, own0, own1, spots = call(
        windows_kernel, "windows", [rows, cols, band, early, late],
        [full, full, full, arr(8, dtype=jnp.int32)], [near], out_specs=[VM, VM, VM, SM],
    )
    mate1 = move(sent1, "mate")
    optics = [probes, amplitudes, wave, first, second]
    work = [pltpu.VMEM((2, 2, SIDE, SIDE), BF), pltpu.VMEM((2, 2, SIDE, SIDE), F32)]
    wide_full = arr(2, SIDE, SIDE, dtype=F32)
    inner = arr(2, HALF + 64, SIDE)
    pair = arr(2, 2, HALF, SIDE)
    outer0, inband0, kept0, edge0 = call(
        functools.partial(solo_kernel, 0), "solo0", [rows, probe_choice, own0, mate0] + optics,
        [half, inner, wide_full, half], work, flops=10**11,
    )
    inband0 = move(inband0, "mate")
    outers, inband1, kept1, edges = call(
        functools.partial(solo_kernel, 1), "solo1",
        [rows, probe_choice, own1, mate1] + optics + [outer0, edge0],
        [pair, inner, wide_full, pair], work, flops=10**11,
    )
    inband1 = move(inband1, "mate")
    outers = move(outers, "direct")
    edges = move(edges, "early")
    (total,) = call(
        own_kernel, "own", [rows, cols, kept0, kept1, inband0],
        [arr(2, EXT, COLS, dtype=F32)], flops=10**11,
    )
    results = [arr(2, EXT, COLS, dtype=F32), arr(1, 2, BAND, COLS, dtype=F32)]
    total, written = call(
        more_kernel, "more", [rows, cols, spots, total, inband1, edges], results,
        [pltpu.SemaphoreType.DMA((2,))], out_specs=[VM, HB], aliases={3: 0}, flops=10**11,
    )
    _, gradient = call(
        last_kernel, "last", [spots, total, outers, written], results,
        [pltpu.SemaphoreType.DMA((2,))],
        in_specs=[SM, VM, VM, HB], out_specs=[VM, HB], aliases={1: 0, 3: 1},
    )
    return gradient


def solution(mesh):
    return jax.shard_map(
        shards,
        mesh=mesh,
        in_specs=(
            P("cuts", None, "region", None),
            P(),
            P("region", None, None),
            P(),
            P("region"),
            P("region"),
            P("region"),
        ),
        out_specs=P("cuts", None, "region", None),
        check_vma=False,
    )
```

```python
import functools

import jax
import jax.numpy as jnp
import ml_dtypes
import numpy as np
from jax import lax
from jax.experimental import pallas as pl
from jax.experimental.pallas import tpu as pltpu
from jax.sharding import PartitionSpec as P

modulus_floor = 0.25
AXES = ("cuts", "region")
BF = jnp.bfloat16
F32 = jnp.float32
SIDE = 256
HALF = 128
BAND = 256
COLS = 1024
EXT = BAND + 2 * HALF
EDGE = 2 * HALF * COLS // 128
WIDE = SIDE + 128
VM = pl.BlockSpec(memory_space=pltpu.VMEM)
SM = pl.BlockSpec(memory_space=pltpu.SMEM)
HB = pl.BlockSpec(memory_space=pltpu.HBM)


def routes(regions):
    at = lambda c, r: c * regions + r % regions
    both = [(c, r) for c in range(2) for r in range(regions)]
    return {
        "mate": [(at(c, r), at(1 - c, r)) for c, r in both],
        "direct": [(at(c, r), at(1 - c, r - 1 if c == 0 else r + 1)) for c, r in both],
        "early": [(at(c, r), at(c, r - 1 if c == 0 else r + 1)) for c, r in both],
        "late": [(at(c, r), at(c, r + 1 if c == 0 else r - 1)) for c, r in both],
    }


def dft_blocks():
    index = np.arange(SIDE)
    angles = (index[:, None] * index[None, :] % SIDE) * (2.0 * np.pi / SIDE)
    real = np.cos(angles) / np.sqrt(SIDE)
    imag = -np.sin(angles) / np.sqrt(SIDE)
    first = np.block([[real, -imag], [imag, real]]).astype(ml_dtypes.bfloat16)
    second = np.block([[real, imag], [-imag, real]]).astype(ml_dtypes.bfloat16)
    return first, second


def places(rows):
    up = [rows[i] < 0 for i in range(4)]
    first = lambda a, b: jnp.where(a, 0, jnp.where(b, 1, 2))
    last = lambda a, b: jnp.where(a, 3, jnp.where(b, 2, 1))
    no = [jnp.logical_not(u) for u in up]
    return first(up[0], up[1]), last(up[3], up[2]), first(no[0], no[1]), last(no[3], no[2])


def column_split(left):
    base = jnp.minimum(lax.shift_right_logical(left, 7), (COLS - WIDE) // 128) * 128
    return pl.multiple_of(base, 128), left - base


def row_split(top, most):
    base = jnp.minimum(lax.shift_right_logical(top, 3), most // 8) * 8
    return pl.multiple_of(base, 8), top - base


def cut_window(load, top, left, count, total):
    row_base, row_shift = row_split(top, total - count - 8)
    col_base, col_shift = column_split(left)
    block = load(pl.ds(row_base, count + 8), pl.ds(col_base, WIDE))
    block = pltpu.roll(block, lax.rem(count + 8 - row_shift, count + 8), 0)[:count]
    return pltpu.roll(block, lax.rem(WIDE - col_shift, WIDE), 1)[:, :SIDE]


def put_window(total_ref, channel, top, left, block):
    count = block.shape[0]
    row_base, row_shift = row_split(top, EXT - count - 8)
    col_base, col_shift = column_split(left)
    block = jnp.concatenate([block, jnp.zeros((count, WIDE - SIDE), F32)], axis=1)
    block = pltpu.roll(block, col_shift, 1)
    block = jnp.concatenate([block, jnp.zeros((8, WIDE), F32)], axis=0)
    block = pltpu.roll(block, row_shift, 0)
    where = (channel, pl.ds(row_base, count + 8), pl.ds(col_base, WIDE))
    total_ref[where] = total_ref[where] + block


def put_near(total_ref, channel, top, left, block, near):
    row = pl.multiple_of(HALF + near, HALF)
    col_base, col_shift = column_split(left)
    shift = top - row
    block = jnp.concatenate([block, jnp.zeros((HALF, WIDE - SIDE), F32)], axis=1)
    block = pltpu.roll(block, col_shift, 1)
    block = pltpu.roll(block, lax.rem(shift + 2 * HALF, HALF), 0)
    line = lax.broadcasted_iota(jnp.int32, block.shape, 0)
    kept = jnp.where((line >= shift) & (line < shift + HALF), block, 0.0)
    where = (channel, pl.ds(row, HALF), pl.ds(col_base, WIDE))
    total_ref[where] = total_ref[where] + kept


def tagged(rows, cols, spots):
    line = lax.broadcasted_iota(jnp.int32, (16, 128), 0)
    lane = lax.broadcasted_iota(jnp.int32, (16, 128), 1)
    tile = jnp.zeros((16, 128), jnp.int32)
    for k, spot in enumerate(spots):
        left = cols[spot]
        parts = (rows[spot] + HALF, lax.shift_right_logical(left, 3), jnp.bitwise_and(left, 7))
        for n, part in enumerate(parts):
            tile = jnp.where((line == k) & (lane == n), part, tile)
    return tile.astype(F32).astype(BF)


def edge_kernel(rows_in, cols_in, objects_in, early, late, objects, rows, cols, sems):
    cut = lax.axis_index("cuts")
    copies = [
        pltpu.make_async_copy(rows_in, rows, sems.at[0]),
        pltpu.make_async_copy(cols_in, cols, sems.at[1]),
        pltpu.make_async_copy(objects_in.at[0, 0], objects.at[0], sems.at[2]),
        pltpu.make_async_copy(objects_in.at[0, 1], objects.at[1], sems.at[3]),
    ]
    for copy in copies:
        copy.start()
    copies[0].wait()
    copies[1].wait()
    u0, u1, l0, l1 = places(rows)
    up = cut == 0
    early[EDGE:] = tagged(rows, cols, (jnp.where(up, u0, l0), jnp.where(up, u1, l1)))
    late[EDGE:] = tagged(rows, cols, (jnp.where(up, l0, u0), jnp.where(up, l1, u1)))
    start = pl.multiple_of(jnp.where(up, 0, HALF), HALF)
    for channel in range(2):
        copies[2 + channel].wait()
        for k in range(COLS // 128):
            where = pl.ds((channel * (COLS // 128) + k) * HALF, HALF)
            lanes = slice(128 * k, 128 * (k + 1))
            early[where] = objects[channel, pl.ds(start, HALF), lanes].astype(BF)
            late[where] = objects[channel, pl.ds(HALF - start, HALF), lanes].astype(BF)


def strip_window(rows, cols, objects, edge, lower, spot, output, near):
    start = pl.multiple_of(jnp.where(lower, BAND, 0), HALF)
    own = pl.multiple_of(jnp.where(lower, 0, HALF), HALF)
    col_base, col_shift = column_split(cols[spot])
    row_base, row_shift = row_split(rows[spot] + own, HALF + BAND - SIDE - 8)
    count = SIDE + 8
    for channel in range(2):
        first = channel * COLS + col_base
        for k in range(WIDE // 128):
            near[channel, pl.ds(start, HALF), 128 * k : 128 * (k + 1)] = edge[
                pl.ds(pl.multiple_of(first + HALF * k, HALF), HALF)
            ].astype(F32)
        near[channel, pl.ds(own, BAND)] = objects[channel, :, pl.ds(col_base, WIDE)]
        block = near[channel, pl.ds(row_base, count)]
        block = pltpu.roll(block, lax.rem(count - row_shift, count), 0)[:SIDE]
        block = pltpu.roll(block, lax.rem(WIDE - col_shift, WIDE), 1)[:, :SIDE]
        output[channel] = block.astype(BF)


def mate_kernel(rows, cols, objects, early, window, near):
    lower = lax.axis_index("cuts") == 0
    u0, u1, l0, l1 = places(rows)
    spot = jnp.where(lower, l0, u0)
    strip_window(rows, cols, objects, early, lower, spot, window, near)


def windows_kernel(rows, cols, objects, early, late, sent, own0, own1, spots, near):
    lower = lax.axis_index("cuts") == 1
    u0, u1, l0, l1 = places(rows)
    other = jnp.where(lower, u1, l1)
    strip_window(rows, cols, objects, early, jnp.logical_not(lower), other, sent, near)
    for spot, output in ((jnp.where(lower, l0, u0), own0), (jnp.where(lower, l1, u1), own1)):
        strip_window(rows, cols, objects, late, lower, spot, output, near)
    decode(early, late, spots)


def decode(early, late, spots):
    line = lax.broadcasted_iota(jnp.int32, (16, 128), 0)
    lane = lax.broadcasted_iota(jnp.int32, (16, 128), 1)
    for n, edge in enumerate((early, late)):
        tile = edge[EDGE:].astype(F32)
        left = jnp.where(lane == 1, tile * 8.0, jnp.where(lane == 2, tile, 0.0))
        top = jnp.where(lane == 0, tile, 0.0)
        for k in range(2):
            for m, part in enumerate((top, left)):
                spots[4 * n + 2 * k + m] = jnp.sum(jnp.where(line == k, part, 0.0)).astype(jnp.int32)


def transform(fields, left, right):
    count = len(fields)
    stacked = jnp.concatenate(
        [jnp.concatenate([f[part].astype(BF) for f in fields], axis=1) for part in range(2)], axis=0
    )
    middle = jnp.dot(left, stacked, preferred_element_type=F32).astype(BF)
    spans = [slice(SIDE * k, SIDE * (k + 1)) for k in range(count)]
    middle = jnp.concatenate(
        [jnp.concatenate([middle[:SIDE, s], middle[SIDE:, s]], axis=1) for s in spans], axis=0
    )
    result = jnp.dot(middle, right, preferred_element_type=F32)
    return [(result[s, :SIDE], result[s, SIDE:]) for s in spans]


def times(a, b):
    return a[0] * b[0] - a[1] * b[1], a[0] * b[1] + a[1] * b[0]


def conj_times(a, b):
    return a[0] * b[0] + a[1] * b[1], a[0] * b[1] - a[1] * b[0]


def wide(pair):
    return pair[0].astype(F32), pair[1].astype(F32)


def chain(incoming, patches, measured, wave, first, second, store):
    spots = range(len(incoming))
    propagator = (wave[0], wave[1])
    fields = [times(wide(incoming[k]()), patches[k](0)) for k in spots]
    fields = [times(propagator, f) for f in transform(fields, first, second)]
    psi = [(f[0].astype(BF), f[1].astype(BF)) for f in transform(fields, second, first)]
    fields = [times(wide(psi[k]), patches[k](1)) for k in spots]
    detected = []
    for k, (real, imag) in enumerate(transform(fields, first, second)):
        modulus = jnp.sqrt(real * real + imag * imag)
        factor = 1.0 - measured[k]() / jnp.maximum(modulus, modulus_floor)
        detected.append((real * factor, imag * factor))
    arriving = [(f[0].astype(BF), f[1].astype(BF)) for f in transform(detected, second, first)]
    arriving = [wide(f) for f in arriving]
    for k in spots:
        store(k, 1, conj_times(wide(psi[k]), arriving[k]))
    fields = [conj_times(patches[k](1), arriving[k]) for k in spots]
    fields = [conj_times(propagator, f) for f in transform(fields, first, second)]
    for k, (real, imag) in enumerate(transform(fields, second, first)):
        arrived = real.astype(BF).astype(F32), imag.astype(BF).astype(F32)
        store(k, 0, conj_times(wide(incoming[k]()), arrived))


def solo_kernel(
    number, rows, picks, own, mate, probes, amplitudes, wave, first, second, *refs
):
    if number == 0:
        sent_outer, sent_inband, kept, edges, held, made = refs
    else:
        edge_before, sent_outer, sent_inband, kept, both, held, made = refs
        both[0] = edge_before[...]
        edges = both.at[1]
    cut = lax.axis_index("cuts")
    spots = places(rows)
    place = jnp.where(cut == 0, spots[number], spots[2 + number])
    start = pl.multiple_of(jnp.where(cut == 0, 0, HALF), HALF)
    held[cut] = own[...]
    held[1 - cut] = mate[...]

    def store(k, which, value):
        made[which, 0], made[which, 1] = value

    chain(
        [lambda: (probes[picks[place], 0], probes[picks[place], 1])],
        [lambda which: wide((held[which, 0], held[which, 1]))],
        [lambda: amplitudes[place]],
        wave, first[...], second[...], store,
    )
    depth = sent_inband.shape[1]
    inner = pl.multiple_of(jnp.where(cut == 0, SIDE - depth, 0), 64)
    for channel in range(2):
        sent_outer[channel] = made[1 - cut, channel, pl.ds(start, HALF)].astype(BF)
        sent_inband[channel] = made[1 - cut, channel, pl.ds(inner, depth)].astype(BF)
        kept[channel] = made[cut, channel]
        edges[channel] = made[cut, channel, pl.ds(start, HALF)].astype(BF)


def put_inband(put, rows, cols, number, inband, channel):
    upper = lax.axis_index("cuts") == 1
    spots = places(rows)
    spot = jnp.where(upper, spots[number], spots[2 + number])
    skip = jnp.where(upper, SIDE - inband.shape[1], 0)
    put(rows[spot] + HALF + skip, cols[spot], inband[channel].astype(F32))


def own_kernel(rows, cols, spots, kept0, kept1, inband, outer, total):
    cut = lax.axis_index("cuts")
    places_here = places(rows)
    total[...] = jnp.zeros_like(total)
    for channel in range(2):
        put = functools.partial(put_window, total, channel)
        for number, kept in enumerate((kept0, kept1)):
            spot = jnp.where(cut == 0, places_here[number], places_here[2 + number])
            put(rows[spot] + HALF, cols[spot], kept[channel])
        put_inband(put, rows, cols, 0, inband, channel)
        shift = jnp.where(cut == 0, -HALF, BAND)
        put(spots[4] + shift, spots[5], outer[channel].astype(F32))


def half_copy(total, output, channel, start, sem):
    return pltpu.make_async_copy(
        total.at[channel, pl.ds(pl.multiple_of(HALF + start, HALF), HALF)],
        output.at[0, channel, pl.ds(pl.multiple_of(start, HALF), HALF)],
        sem,
    )


def more_kernel(rows, cols, spots, given, inband, edges, total, output, sems):
    cut = lax.axis_index("cuts")
    shift = jnp.where(cut == 0, BAND, -HALF)
    far = jnp.where(cut == 0, HALF, 0)
    copies = []
    for channel in range(2):
        put = functools.partial(put_window, total, channel)
        put_inband(put, rows, cols, 1, inband, channel)
        for k in range(2):
            put(spots[2 * k] + shift, spots[2 * k + 1], edges[k, channel].astype(F32))
        copies.append(half_copy(total, output, channel, far, sems.at[channel]))
        copies[channel].start()
    for copy in copies:
        copy.wait()


def last_kernel(spots, given, outer, written, total, output, sems):
    cut = lax.axis_index("cuts")
    near = jnp.where(cut == 0, 0, HALF)
    shift = jnp.where(cut == 0, -HALF, BAND)
    copies = []
    for channel in range(2):
        put_near(total, channel, spots[6] + shift, spots[7], outer[channel].astype(F32), near)
        copies.append(half_copy(total, output, channel, near, sems.at[channel]))
        copies[channel].start()
    for copy in copies:
        copy.wait()


def call(kernel, name, inputs, outputs, scratch=(), in_specs=None, out_specs=None, aliases={}, vmem=40, flops=1):
    scalars = [x for x in inputs if x.dtype == jnp.int32]
    return pl.pallas_call(
        kernel,
        name=name,
        out_shape=outputs,
        in_specs=in_specs or [SM] * len(scalars) + [VM] * (len(inputs) - len(scalars)),
        out_specs=out_specs or [VM] * len(outputs),
        scratch_shapes=list(scratch),
        input_output_aliases=aliases,
        cost_estimate=pl.CostEstimate(flops=flops, bytes_accessed=1, transcendentals=0),
        compiler_params=pltpu.CompilerParams(vmem_limit_bytes=vmem << 20),
    )(*inputs)


def arr(*shape, dtype=BF):
    return jax.ShapeDtypeStruct(shape, dtype)


def shards(objects, probes, amplitudes, prop_phase, scan_rows, scan_cols, probe_choice):
    route = routes(lax.axis_size("region"))
    move = lambda x, way: lax.ppermute(x, AXES, route[way])
    first, second = (jnp.asarray(t) for t in dft_blocks())
    wave = jnp.stack([jnp.cos(prop_phase), jnp.sin(prop_phase)])
    half = arr(2, HALF, SIDE)

    full = arr(2, SIDE, SIDE)
    near = pltpu.VMEM((2, BAND + HALF, WIDE), F32)
    early, late, band, rows, cols = call(
        edge_kernel, "edge",
        [pltpu.with_memory_space_constraint(x, pltpu.HBM) for x in (scan_rows, scan_cols, objects)],
        [arr(EDGE + 16, 128), arr(EDGE + 16, 128),
         arr(2, BAND, COLS, dtype=F32), arr(4, dtype=jnp.int32), arr(4, dtype=jnp.int32)],
        [pltpu.SemaphoreType.DMA((4,))],
        in_specs=[HB] * 3, out_specs=[VM] * 3 + [SM] * 2, vmem=50,
    )
    early = move(early, "early")
    late = move(late, "late")
    (sent0,) = call(mate_kernel, "mate", [rows, cols, band, early], [full], [near])
    mate0 = move(sent0, "mate")
    sent1, own0, own1, spots = call(
        windows_kernel, "windows", [rows, cols, band, early, late],
        [full, full, full, arr(8, dtype=jnp.int32)], [near], out_specs=[VM, VM, VM, SM],
    )
    mate1 = move(sent1, "mate")
    optics = [probes, amplitudes, wave, first, second]
    work = [pltpu.VMEM((2, 2, SIDE, SIDE), BF), pltpu.VMEM((2, 2, SIDE, SIDE), F32)]
    wide_full = arr(2, SIDE, SIDE, dtype=F32)
    inner = arr(2, HALF + 64, SIDE)
    pair = arr(2, 2, HALF, SIDE)
    outer0, inband0, kept0, edge0 = call(
        functools.partial(solo_kernel, 0), "solo0", [rows, probe_choice, own0, mate0] + optics,
        [half, inner, wide_full, half], work, flops=10**11,
    )
    inband0 = move(inband0, "mate")
    outer0 = move(outer0, "direct")
    outer1, inband1, kept1, edges = call(
        functools.partial(solo_kernel, 1), "solo1",
        [rows, probe_choice, own1, mate1] + optics + [edge0],
        [half, inner, wide_full, pair], work, flops=10**11,
    )
    inband1 = move(inband1, "mate")
    outer1 = move(outer1, "direct")
    edges = move(edges, "early")
    (total,) = call(
        own_kernel, "own", [rows, cols, spots, kept0, kept1, inband0, outer0],
        [arr(2, EXT, COLS, dtype=F32)], flops=10**11,
    )
    results = [arr(2, EXT, COLS, dtype=F32), arr(1, 2, BAND, COLS, dtype=F32)]
    total, written = call(
        more_kernel, "more", [rows, cols, spots, total, inband1, edges], results,
        [pltpu.SemaphoreType.DMA((2,))], out_specs=[VM, HB], aliases={3: 0}, flops=10**11,
    )
    _, gradient = call(
        last_kernel, "last", [spots, total, outer1, written], results,
        [pltpu.SemaphoreType.DMA((2,))],
        in_specs=[SM, VM, VM, HB], out_specs=[VM, HB], aliases={1: 0, 3: 1},
    )
    return gradient


def solution(mesh):
    return jax.shard_map(
        shards,
        mesh=mesh,
        in_specs=(
            P("cuts", None, "region", None),
            P(),
            P("region", None, None),
            P(),
            P("region"),
            P("region"),
            P("region"),
        ),
        out_specs=P("cuts", None, "region", None),
        check_vma=False,
    )
```

```python
import functools

import jax
import jax.numpy as jnp
import ml_dtypes
import numpy as np
from jax import lax
from jax.experimental import pallas as pl
from jax.experimental.pallas import tpu as pltpu
from jax.sharding import PartitionSpec as P

modulus_floor = 0.25
AXES = ("cuts", "region")
BF = jnp.bfloat16
F32 = jnp.float32
SIDE = 256
HALF = 128
BAND = 256
COLS = 1024
EXT = BAND + 2 * HALF
EDGE = 2 * HALF * COLS // 128
WIDE = SIDE + 128
VM = pl.BlockSpec(memory_space=pltpu.VMEM)
SM = pl.BlockSpec(memory_space=pltpu.SMEM)
HB = pl.BlockSpec(memory_space=pltpu.HBM)


def routes(regions):
    at = lambda c, r: c * regions + r % regions
    both = [(c, r) for c in range(2) for r in range(regions)]
    return {
        "mate": [(at(c, r), at(1 - c, r)) for c, r in both],
        "direct": [(at(c, r), at(1 - c, r - 1 if c == 0 else r + 1)) for c, r in both],
        "early": [(at(c, r), at(c, r - 1 if c == 0 else r + 1)) for c, r in both],
        "late": [(at(c, r), at(c, r + 1 if c == 0 else r - 1)) for c, r in both],
    }


def dft_blocks():
    index = np.arange(SIDE)
    angles = (index[:, None] * index[None, :] % SIDE) * (2.0 * np.pi / SIDE)
    real = np.cos(angles) / np.sqrt(SIDE)
    imag = -np.sin(angles) / np.sqrt(SIDE)
    first = np.block([[real, -imag], [imag, real]]).astype(ml_dtypes.bfloat16)
    second = np.block([[real, imag], [-imag, real]]).astype(ml_dtypes.bfloat16)
    return first, second


def places(rows):
    up = [rows[i] < 0 for i in range(4)]
    first = lambda a, b: jnp.where(a, 0, jnp.where(b, 1, 2))
    last = lambda a, b: jnp.where(a, 3, jnp.where(b, 2, 1))
    no = [jnp.logical_not(u) for u in up]
    return first(up[0], up[1]), last(up[3], up[2]), first(no[0], no[1]), last(no[3], no[2])


def column_split(left):
    base = jnp.minimum(lax.shift_right_logical(left, 7), (COLS - WIDE) // 128) * 128
    return pl.multiple_of(base, 128), left - base


def row_split(top, most):
    base = jnp.minimum(lax.shift_right_logical(top, 3), most // 8) * 8
    return pl.multiple_of(base, 8), top - base


def cut_window(load, top, left, count, total):
    row_base, row_shift = row_split(top, total - count - 8)
    col_base, col_shift = column_split(left)
    block = load(pl.ds(row_base, count + 8), pl.ds(col_base, WIDE))
    block = pltpu.roll(block, lax.rem(count + 8 - row_shift, count + 8), 0)[:count]
    return pltpu.roll(block, lax.rem(WIDE - col_shift, WIDE), 1)[:, :SIDE]


def put_window(total_ref, channel, top, left, block):
    count = block.shape[0]
    row_base, row_shift = row_split(top, EXT - count - 8)
    col_base, col_shift = column_split(left)
    block = jnp.concatenate([block, jnp.zeros((count, WIDE - SIDE), F32)], axis=1)
    block = pltpu.roll(block, col_shift, 1)
    block = jnp.concatenate([block, jnp.zeros((8, WIDE), F32)], axis=0)
    block = pltpu.roll(block, row_shift, 0)
    where = (channel, pl.ds(row_base, count + 8), pl.ds(col_base, WIDE))
    total_ref[where] = total_ref[where] + block


def put_near(total_ref, channel, top, left, block, near):
    row = pl.multiple_of(HALF + near, HALF)
    col_base, col_shift = column_split(left)
    shift = top - row
    block = jnp.concatenate([block, jnp.zeros((HALF, WIDE - SIDE), F32)], axis=1)
    block = pltpu.roll(block, col_shift, 1)
    block = pltpu.roll(block, lax.rem(shift + 2 * HALF, HALF), 0)
    line = lax.broadcasted_iota(jnp.int32, block.shape, 0)
    kept = jnp.where((line >= shift) & (line < shift + HALF), block, 0.0)
    where = (channel, pl.ds(row, HALF), pl.ds(col_base, WIDE))
    total_ref[where] = total_ref[where] + kept


def tagged(rows, cols, spots):
    line = lax.broadcasted_iota(jnp.int32, (16, 128), 0)
    lane = lax.broadcasted_iota(jnp.int32, (16, 128), 1)
    tile = jnp.zeros((16, 128), jnp.int32)
    for k, spot in enumerate(spots):
        left = cols[spot]
        parts = (rows[spot] + HALF, lax.shift_right_logical(left, 3), jnp.bitwise_and(left, 7))
        for n, part in enumerate(parts):
            tile = jnp.where((line == k) & (lane == n), part, tile)
    return tile.astype(F32).astype(BF)


def edge_kernel(rows_in, cols_in, objects_in, early, late, objects, rows, cols, sems):
    cut = lax.axis_index("cuts")
    copies = [
        pltpu.make_async_copy(rows_in, rows, sems.at[0]),
        pltpu.make_async_copy(cols_in, cols, sems.at[1]),
        pltpu.make_async_copy(objects_in.at[0, 0], objects.at[0], sems.at[2]),
        pltpu.make_async_copy(objects_in.at[0, 1], objects.at[1], sems.at[3]),
    ]
    for copy in copies:
        copy.start()
    copies[0].wait()
    copies[1].wait()
    u0, u1, l0, l1 = places(rows)
    up = cut == 0
    early[EDGE:] = tagged(rows, cols, (jnp.where(up, u0, l0), jnp.where(up, u1, l1)))
    late[EDGE:] = tagged(rows, cols, (jnp.where(up, l0, u0), jnp.where(up, l1, u1)))
    start = pl.multiple_of(jnp.where(up, 0, HALF), HALF)
    for channel in range(2):
        copies[2 + channel].wait()
        for k in range(COLS // 128):
            where = pl.ds((channel * (COLS // 128) + k) * HALF, HALF)
            lanes = slice(128 * k, 128 * (k + 1))
            early[where] = objects[channel, pl.ds(start, HALF), lanes].astype(BF)
            late[where] = objects[channel, pl.ds(HALF - start, HALF), lanes].astype(BF)


def strip_window(rows, cols, objects, edge, lower, spot, output, near):
    start = pl.multiple_of(jnp.where(lower, BAND, 0), HALF)
    own = pl.multiple_of(jnp.where(lower, 0, HALF), HALF)
    col_base, col_shift = column_split(cols[spot])
    row_base, row_shift = row_split(rows[spot] + own, HALF + BAND - SIDE - 8)
    count = SIDE + 8
    for channel in range(2):
        first = channel * COLS + col_base
        for k in range(WIDE // 128):
            near[channel, pl.ds(start, HALF), 128 * k : 128 * (k + 1)] = edge[
                pl.ds(pl.multiple_of(first + HALF * k, HALF), HALF)
            ].astype(F32)
        near[channel, pl.ds(own, BAND)] = objects[channel, :, pl.ds(col_base, WIDE)]
        block = near[channel, pl.ds(row_base, count)]
        block = pltpu.roll(block, lax.rem(count - row_shift, count), 0)[:SIDE]
        block = pltpu.roll(block, lax.rem(WIDE - col_shift, WIDE), 1)[:, :SIDE]
        output[channel] = block.astype(BF)


def mate_kernel(rows, cols, objects, early, window, near):
    lower = lax.axis_index("cuts") == 0
    u0, u1, l0, l1 = places(rows)
    spot = jnp.where(lower, l0, u0)
    strip_window(rows, cols, objects, early, lower, spot, window, near)


def windows_kernel(rows, cols, objects, early, late, sent, own0, own1, spots, near):
    lower = lax.axis_index("cuts") == 1
    u0, u1, l0, l1 = places(rows)
    other = jnp.where(lower, u1, l1)
    strip_window(rows, cols, objects, early, jnp.logical_not(lower), other, sent, near)
    for spot, output in ((jnp.where(lower, l0, u0), own0), (jnp.where(lower, l1, u1), own1)):
        strip_window(rows, cols, objects, late, lower, spot, output, near)
    decode(early, late, spots)


def decode(early, late, spots):
    line = lax.broadcasted_iota(jnp.int32, (16, 128), 0)
    lane = lax.broadcasted_iota(jnp.int32, (16, 128), 1)
    for n, edge in enumerate((early, late)):
        tile = edge[EDGE:].astype(F32)
        left = jnp.where(lane == 1, tile * 8.0, jnp.where(lane == 2, tile, 0.0))
        top = jnp.where(lane == 0, tile, 0.0)
        for k in range(2):
            for m, part in enumerate((top, left)):
                spots[4 * n + 2 * k + m] = jnp.sum(jnp.where(line == k, part, 0.0)).astype(jnp.int32)


def transform(fields, left, right):
    count = len(fields)
    stacked = jnp.concatenate(
        [jnp.concatenate([f[part].astype(BF) for f in fields], axis=1) for part in range(2)], axis=0
    )
    middle = jnp.dot(left, stacked, preferred_element_type=F32).astype(BF)
    spans = [slice(SIDE * k, SIDE * (k + 1)) for k in range(count)]
    middle = jnp.concatenate(
        [jnp.concatenate([middle[:SIDE, s], middle[SIDE:, s]], axis=1) for s in spans], axis=0
    )
    result = jnp.dot(middle, right, preferred_element_type=F32)
    return [(result[s, :SIDE], result[s, SIDE:]) for s in spans]


def times(a, b):
    return a[0] * b[0] - a[1] * b[1], a[0] * b[1] + a[1] * b[0]


def conj_times(a, b):
    return a[0] * b[0] + a[1] * b[1], a[0] * b[1] - a[1] * b[0]


def wide(pair):
    return pair[0].astype(F32), pair[1].astype(F32)


def chain(incoming, patches, measured, wave, first, second, store):
    spots = range(len(incoming))
    propagator = (wave[0], wave[1])
    fields = [times(wide(incoming[k]()), patches[k](0)) for k in spots]
    fields = [times(propagator, f) for f in transform(fields, first, second)]
    psi = [(f[0].astype(BF), f[1].astype(BF)) for f in transform(fields, second, first)]
    fields = [times(wide(psi[k]), patches[k](1)) for k in spots]
    detected = []
    for k, (real, imag) in enumerate(transform(fields, first, second)):
        modulus = jnp.sqrt(real * real + imag * imag)
        factor = 1.0 - measured[k]() / jnp.maximum(modulus, modulus_floor)
        detected.append((real * factor, imag * factor))
    arriving = [(f[0].astype(BF), f[1].astype(BF)) for f in transform(detected, second, first)]
    arriving = [wide(f) for f in arriving]
    for k in spots:
        store(k, 1, conj_times(wide(psi[k]), arriving[k]))
    fields = [conj_times(patches[k](1), arriving[k]) for k in spots]
    fields = [conj_times(propagator, f) for f in transform(fields, first, second)]
    for k, (real, imag) in enumerate(transform(fields, second, first)):
        arrived = real.astype(BF).astype(F32), imag.astype(BF).astype(F32)
        store(k, 0, conj_times(wide(incoming[k]()), arrived))


def solo_kernel(
    number, rows, picks, own, mate, probes, amplitudes, wave, first, second, *refs
):
    if number == 0:
        sent_outer, sent_inband, kept, edges, held, made = refs
    else:
        outer_before, edge_before, outers, sent_inband, kept, both, held, made = refs
        outers[0] = outer_before[...]
        both[0] = edge_before[...]
        sent_outer, edges = outers.at[1], both.at[1]
    cut = lax.axis_index("cuts")
    spots = places(rows)
    place = jnp.where(cut == 0, spots[number], spots[2 + number])
    start = pl.multiple_of(jnp.where(cut == 0, 0, HALF), HALF)
    held[cut] = own[...]
    held[1 - cut] = mate[...]

    def store(k, which, value):
        made[which, 0], made[which, 1] = value

    chain(
        [lambda: (probes[picks[place], 0], probes[picks[place], 1])],
        [lambda which: wide((held[which, 0], held[which, 1]))],
        [lambda: amplitudes[place]],
        wave, first[...], second[...], store,
    )
    depth = sent_inband.shape[1]
    inner = pl.multiple_of(jnp.where(cut == 0, SIDE - depth, 0), 64)
    for channel in range(2):
        sent_outer[channel] = made[1 - cut, channel, pl.ds(start, HALF)].astype(BF)
        sent_inband[channel] = made[1 - cut, channel, pl.ds(inner, depth)].astype(BF)
        kept[channel] = made[cut, channel]
        edges[channel] = made[cut, channel, pl.ds(start, HALF)].astype(BF)


def put_inband(put, rows, cols, number, inband, channel):
    upper = lax.axis_index("cuts") == 1
    spots = places(rows)
    spot = jnp.where(upper, spots[number], spots[2 + number])
    skip = jnp.where(upper, SIDE - inband.shape[1], 0)
    put(rows[spot] + HALF + skip, cols[spot], inband[channel].astype(F32))


def own_kernel(rows, cols, kept0, kept1, inband, total):
    cut = lax.axis_index("cuts")
    places_here = places(rows)
    total[...] = jnp.zeros_like(total)
    for channel in range(2):
        put = functools.partial(put_window, total, channel)
        for number, kept in enumerate((kept0, kept1)):
            spot = jnp.where(cut == 0, places_here[number], places_here[2 + number])
            put(rows[spot] + HALF, cols[spot], kept[channel])
        put_inband(put, rows, cols, 0, inband, channel)


def half_copy(total, output, channel, start, sem):
    return pltpu.make_async_copy(
        total.at[channel, pl.ds(pl.multiple_of(HALF + start, HALF), HALF)],
        output.at[0, channel, pl.ds(pl.multiple_of(start, HALF), HALF)],
        sem,
    )


def more_kernel(rows, cols, spots, given, inband, edges, total, output, sems):
    cut = lax.axis_index("cuts")
    shift = jnp.where(cut == 0, BAND, -HALF)
    far = jnp.where(cut == 0, HALF, 0)
    copies = []
    for channel in range(2):
        put = functools.partial(put_window, total, channel)
        put_inband(put, rows, cols, 1, inband, channel)
        for k in range(2):
            put(spots[2 * k] + shift, spots[2 * k + 1], edges[k, channel].astype(F32))
        copies.append(half_copy(total, output, channel, far, sems.at[channel]))
        copies[channel].start()
    for copy in copies:
        copy.wait()


def last_kernel(spots, given, outers, written, total, output, sems):
    cut = lax.axis_index("cuts")
    near = jnp.where(cut == 0, 0, HALF)
    shift = jnp.where(cut == 0, -HALF, BAND)
    copies = []
    for channel in range(2):
        for k in range(2):
            top, left = spots[4 + 2 * k] + shift, spots[5 + 2 * k]
            put_near(total, channel, top, left, outers[k, channel].astype(F32), near)
        copies.append(half_copy(total, output, channel, near, sems.at[channel]))
        copies[channel].start()
    for copy in copies:
        copy.wait()


def call(kernel, name, inputs, outputs, scratch=(), in_specs=None, out_specs=None, aliases={}, vmem=40, flops=1):
    scalars = [x for x in inputs if x.dtype == jnp.int32]
    return pl.pallas_call(
        kernel,
        name=name,
        out_shape=outputs,
        in_specs=in_specs or [SM] * len(scalars) + [VM] * (len(inputs) - len(scalars)),
        out_specs=out_specs or [VM] * len(outputs),
        scratch_shapes=list(scratch),
        input_output_aliases=aliases,
        cost_estimate=pl.CostEstimate(flops=flops, bytes_accessed=1, transcendentals=0),
        compiler_params=pltpu.CompilerParams(vmem_limit_bytes=vmem << 20),
    )(*inputs)


def arr(*shape, dtype=BF):
    return jax.ShapeDtypeStruct(shape, dtype)


def shards(objects, probes, amplitudes, prop_phase, scan_rows, scan_cols, probe_choice):
    route = routes(lax.axis_size("region"))
    move = lambda x, way: lax.ppermute(x, AXES, route[way])
    first, second = (jnp.asarray(t) for t in dft_blocks())
    wave = jnp.stack([jnp.cos(prop_phase), jnp.sin(prop_phase)])
    half = arr(2, HALF, SIDE)

    full = arr(2, SIDE, SIDE)
    near = pltpu.VMEM((2, BAND + HALF, WIDE), F32)
    early, late, band, rows, cols = call(
        edge_kernel, "edge",
        [pltpu.with_memory_space_constraint(x, pltpu.HBM) for x in (scan_rows, scan_cols, objects)],
        [arr(EDGE + 16, 128), arr(EDGE + 16, 128),
         arr(2, BAND, COLS, dtype=F32), arr(4, dtype=jnp.int32), arr(4, dtype=jnp.int32)],
        [pltpu.SemaphoreType.DMA((4,))],
        in_specs=[HB] * 3, out_specs=[VM] * 3 + [SM] * 2, vmem=50,
    )
    early = move(early, "early")
    late = move(late, "late")
    (sent0,) = call(mate_kernel, "mate", [rows, cols, band, early], [full], [near])
    sent0, late = lax.optimization_barrier((sent0, late))
    mate0 = move(sent0, "mate")
    sent1, own0, own1, spots = call(
        windows_kernel, "windows", [rows, cols, band, early, late],
        [full, full, full, arr(8, dtype=jnp.int32)], [near], out_specs=[VM, VM, VM, SM],
    )
    mate1 = move(sent1, "mate")
    optics = [probes, amplitudes, wave, first, second]
    work = [pltpu.VMEM((2, 2, SIDE, SIDE), BF), pltpu.VMEM((2, 2, SIDE, SIDE), F32)]
    wide_full = arr(2, SIDE, SIDE, dtype=F32)
    inner = arr(2, HALF + 64, SIDE)
    pair = arr(2, 2, HALF, SIDE)
    outer0, inband0, kept0, edge0 = call(
        functools.partial(solo_kernel, 0), "solo0", [rows, probe_choice, own0, mate0] + optics,
        [half, inner, wide_full, half], work, flops=10**11,
    )
    inband0 = move(inband0, "mate")
    outers, inband1, kept1, edges = call(
        functools.partial(solo_kernel, 1), "solo1",
        [rows, probe_choice, own1, mate1] + optics + [outer0, edge0],
        [pair, inner, wide_full, pair], work, flops=10**11,
    )
    inband1 = move(inband1, "mate")
    outers = move(outers, "direct")
    edges = move(edges, "early")
    (total,) = call(
        own_kernel, "own", [rows, cols, kept0, kept1, inband0],
        [arr(2, EXT, COLS, dtype=F32)], flops=10**11,
    )
    results = [arr(2, EXT, COLS, dtype=F32), arr(1, 2, BAND, COLS, dtype=F32)]
    total, written = call(
        more_kernel, "more", [rows, cols, spots, total, inband1, edges], results,
        [pltpu.SemaphoreType.DMA((2,))], out_specs=[VM, HB], aliases={3: 0}, flops=10**11,
    )
    _, gradient = call(
        last_kernel, "last", [spots, total, outers, written], results,
        [pltpu.SemaphoreType.DMA((2,))],
        in_specs=[SM, VM, VM, HB], out_specs=[VM, HB], aliases={1: 0, 3: 1},
    )
    return gradient


def solution(mesh):
    return jax.shard_map(
        shards,
        mesh=mesh,
        in_specs=(
            P("cuts", None, "region", None),
            P(),
            P("region", None, None),
            P(),
            P("region"),
            P("region"),
            P("region"),
        ),
        out_specs=P("cuts", None, "region", None),
        check_vma=False,
    )
```

```python
import functools

import jax
import jax.numpy as jnp
import ml_dtypes
import numpy as np
from jax import lax
from jax.experimental import pallas as pl
from jax.experimental.pallas import tpu as pltpu
from jax.sharding import PartitionSpec as P

modulus_floor = 0.25
AXES = ("cuts", "region")
BF = jnp.bfloat16
F32 = jnp.float32
SIDE = 256
HALF = 128
BAND = 256
COLS = 1024
EXT = BAND + 2 * HALF
EDGE = 2 * HALF * COLS // 128
WIDE = SIDE + 128
VM = pl.BlockSpec(memory_space=pltpu.VMEM)
SM = pl.BlockSpec(memory_space=pltpu.SMEM)
HB = pl.BlockSpec(memory_space=pltpu.HBM)


def routes(regions):
    at = lambda c, r: c * regions + r % regions
    both = [(c, r) for c in range(2) for r in range(regions)]
    return {
        "mate": [(at(c, r), at(1 - c, r)) for c, r in both],
        "direct": [(at(c, r), at(1 - c, r - 1 if c == 0 else r + 1)) for c, r in both],
        "early": [(at(c, r), at(c, r - 1 if c == 0 else r + 1)) for c, r in both],
        "late": [(at(c, r), at(c, r + 1 if c == 0 else r - 1)) for c, r in both],
    }


def dft_blocks():
    index = np.arange(SIDE)
    angles = (index[:, None] * index[None, :] % SIDE) * (2.0 * np.pi / SIDE)
    real = np.cos(angles) / np.sqrt(SIDE)
    imag = -np.sin(angles) / np.sqrt(SIDE)
    first = np.block([[real, -imag], [imag, real]]).astype(ml_dtypes.bfloat16)
    second = np.block([[real, imag], [-imag, real]]).astype(ml_dtypes.bfloat16)
    return first, second


def places(rows):
    up = [rows[i] < 0 for i in range(4)]
    first = lambda a, b: jnp.where(a, 0, jnp.where(b, 1, 2))
    last = lambda a, b: jnp.where(a, 3, jnp.where(b, 2, 1))
    no = [jnp.logical_not(u) for u in up]
    return first(up[0], up[1]), last(up[3], up[2]), first(no[0], no[1]), last(no[3], no[2])


def column_split(left):
    base = jnp.minimum(lax.shift_right_logical(left, 7), (COLS - WIDE) // 128) * 128
    return pl.multiple_of(base, 128), left - base


def row_split(top, most):
    base = jnp.minimum(lax.shift_right_logical(top, 3), most // 8) * 8
    return pl.multiple_of(base, 8), top - base


def cut_window(load, top, left, count, total):
    row_base, row_shift = row_split(top, total - count - 8)
    col_base, col_shift = column_split(left)
    block = load(pl.ds(row_base, count + 8), pl.ds(col_base, WIDE))
    block = pltpu.roll(block, lax.rem(count + 8 - row_shift, count + 8), 0)[:count]
    return pltpu.roll(block, lax.rem(WIDE - col_shift, WIDE), 1)[:, :SIDE]


def put_window(total_ref, channel, top, left, block):
    count = block.shape[0]
    row_base, row_shift = row_split(top, EXT - count - 8)
    col_base, col_shift = column_split(left)
    block = jnp.concatenate([block, jnp.zeros((count, WIDE - SIDE), F32)], axis=1)
    block = pltpu.roll(block, col_shift, 1)
    block = jnp.concatenate([block, jnp.zeros((8, WIDE), F32)], axis=0)
    block = pltpu.roll(block, row_shift, 0)
    where = (channel, pl.ds(row_base, count + 8), pl.ds(col_base, WIDE))
    total_ref[where] = total_ref[where] + block


def put_near(total_ref, channel, top, left, block, near):
    row = pl.multiple_of(HALF + near, HALF)
    col_base, col_shift = column_split(left)
    shift = top - row
    block = jnp.concatenate([block, jnp.zeros((HALF, WIDE - SIDE), F32)], axis=1)
    block = pltpu.roll(block, col_shift, 1)
    block = pltpu.roll(block, lax.rem(shift + 2 * HALF, HALF), 0)
    line = lax.broadcasted_iota(jnp.int32, block.shape, 0)
    kept = jnp.where((line >= shift) & (line < shift + HALF), block, 0.0)
    where = (channel, pl.ds(row, HALF), pl.ds(col_base, WIDE))
    total_ref[where] = total_ref[where] + kept


def tagged(rows, cols, spots):
    line = lax.broadcasted_iota(jnp.int32, (16, 128), 0)
    lane = lax.broadcasted_iota(jnp.int32, (16, 128), 1)
    tile = jnp.zeros((16, 128), jnp.int32)
    for k, spot in enumerate(spots):
        left = cols[spot]
        parts = (rows[spot] + HALF, lax.shift_right_logical(left, 3), jnp.bitwise_and(left, 7))
        for n, part in enumerate(parts):
            tile = jnp.where((line == k) & (lane == n), part, tile)
    return tile.astype(F32).astype(BF)


def edge_kernel(rows_in, cols_in, objects_in, early, late, objects, rows, cols, sems):
    cut = lax.axis_index("cuts")
    copies = [
        pltpu.make_async_copy(rows_in, rows, sems.at[0]),
        pltpu.make_async_copy(cols_in, cols, sems.at[1]),
        pltpu.make_async_copy(objects_in.at[0, 0], objects.at[0], sems.at[2]),
        pltpu.make_async_copy(objects_in.at[0, 1], objects.at[1], sems.at[3]),
    ]
    for copy in copies:
        copy.start()
    copies[0].wait()
    copies[1].wait()
    u0, u1, l0, l1 = places(rows)
    up = cut == 0
    early[EDGE:] = tagged(rows, cols, (jnp.where(up, u0, l0), jnp.where(up, u1, l1)))
    late[EDGE:] = tagged(rows, cols, (jnp.where(up, l0, u0), jnp.where(up, l1, u1)))
    start = pl.multiple_of(jnp.where(up, 0, HALF), HALF)
    for channel in range(2):
        copies[2 + channel].wait()
        for k in range(COLS // 128):
            where = pl.ds((channel * (COLS // 128) + k) * HALF, HALF)
            lanes = slice(128 * k, 128 * (k + 1))
            early[where] = objects[channel, pl.ds(start, HALF), lanes].astype(BF)
            late[where] = objects[channel, pl.ds(HALF - start, HALF), lanes].astype(BF)


def strip_window(rows, cols, objects, edge, lower, spot, output, near):
    start = pl.multiple_of(jnp.where(lower, BAND, 0), HALF)
    own = pl.multiple_of(jnp.where(lower, 0, HALF), HALF)
    col_base, col_shift = column_split(cols[spot])
    row_base, row_shift = row_split(rows[spot] + own, HALF + BAND - SIDE - 8)
    count = SIDE + 8
    for channel in range(2):
        first = channel * COLS + col_base
        for k in range(WIDE // 128):
            near[channel, pl.ds(start, HALF), 128 * k : 128 * (k + 1)] = edge[
                pl.ds(pl.multiple_of(first + HALF * k, HALF), HALF)
            ].astype(F32)
        near[channel, pl.ds(own, BAND)] = objects[channel, :, pl.ds(col_base, WIDE)]
        block = near[channel, pl.ds(row_base, count)]
        block = pltpu.roll(block, lax.rem(count - row_shift, count), 0)[:SIDE]
        block = pltpu.roll(block, lax.rem(WIDE - col_shift, WIDE), 1)[:, :SIDE]
        output[channel] = block.astype(BF)


def mate_kernel(rows, cols, objects, early, window, near):
    lower = lax.axis_index("cuts") == 0
    u0, u1, l0, l1 = places(rows)
    spot = jnp.where(lower, l0, u0)
    strip_window(rows, cols, objects, early, lower, spot, window, near)


def windows_kernel(rows, cols, objects, early, late, sent, own0, own1, spots, near):
    lower = lax.axis_index("cuts") == 1
    u0, u1, l0, l1 = places(rows)
    other = jnp.where(lower, u1, l1)
    strip_window(rows, cols, objects, early, jnp.logical_not(lower), other, sent, near)
    for spot, output in ((jnp.where(lower, l0, u0), own0), (jnp.where(lower, l1, u1), own1)):
        strip_window(rows, cols, objects, late, lower, spot, output, near)
    decode(early, late, spots)


def decode(early, late, spots):
    line = lax.broadcasted_iota(jnp.int32, (16, 128), 0)
    lane = lax.broadcasted_iota(jnp.int32, (16, 128), 1)
    for n, edge in enumerate((early, late)):
        tile = edge[EDGE:].astype(F32)
        left = jnp.where(lane == 1, tile * 8.0, jnp.where(lane == 2, tile, 0.0))
        top = jnp.where(lane == 0, tile, 0.0)
        for k in range(2):
            for m, part in enumerate((top, left)):
                spots[4 * n + 2 * k + m] = jnp.sum(jnp.where(line == k, part, 0.0)).astype(jnp.int32)


def transform(fields, left, right):
    count = len(fields)
    stacked = jnp.concatenate(
        [jnp.concatenate([f[part].astype(BF) for f in fields], axis=1) for part in range(2)], axis=0
    )
    middle = jnp.dot(left, stacked, preferred_element_type=F32).astype(BF)
    spans = [slice(SIDE * k, SIDE * (k + 1)) for k in range(count)]
    middle = jnp.concatenate(
        [jnp.concatenate([middle[:SIDE, s], middle[SIDE:, s]], axis=1) for s in spans], axis=0
    )
    result = jnp.dot(middle, right, preferred_element_type=F32)
    return [(result[s, :SIDE], result[s, SIDE:]) for s in spans]


def times(a, b):
    return a[0] * b[0] - a[1] * b[1], a[0] * b[1] + a[1] * b[0]


def conj_times(a, b):
    return a[0] * b[0] + a[1] * b[1], a[0] * b[1] - a[1] * b[0]


def wide(pair):
    return pair[0].astype(F32), pair[1].astype(F32)


def chain(incoming, patches, measured, wave, first, second, store):
    spots = range(len(incoming))
    propagator = (wave[0], wave[1])
    fields = [times(wide(incoming[k]()), patches[k](0)) for k in spots]
    fields = [times(propagator, f) for f in transform(fields, first, second)]
    psi = [(f[0].astype(BF), f[1].astype(BF)) for f in transform(fields, second, first)]
    fields = [times(wide(psi[k]), patches[k](1)) for k in spots]
    detected = []
    for k, (real, imag) in enumerate(transform(fields, first, second)):
        modulus = jnp.sqrt(real * real + imag * imag)
        factor = 1.0 - measured[k]() / jnp.maximum(modulus, modulus_floor)
        detected.append((real * factor, imag * factor))
    arriving = [(f[0].astype(BF), f[1].astype(BF)) for f in transform(detected, second, first)]
    arriving = [wide(f) for f in arriving]
    for k in spots:
        store(k, 1, conj_times(wide(psi[k]), arriving[k]))
    fields = [conj_times(patches[k](1), arriving[k]) for k in spots]
    fields = [conj_times(propagator, f) for f in transform(fields, first, second)]
    for k, (real, imag) in enumerate(transform(fields, second, first)):
        arrived = real.astype(BF).astype(F32), imag.astype(BF).astype(F32)
        store(k, 0, conj_times(wide(incoming[k]()), arrived))


def solo_kernel(
    number, rows, picks, own, mate, probes, amplitudes, wave, first, second, *refs
):
    if number == 0:
        sent_outer, sent_inband, kept, edges, held, made = refs
    else:
        outer_before, edge_before, outers, sent_inband, kept, both, held, made = refs
        outers[0] = outer_before[...]
        both[0] = edge_before[...]
        sent_outer, edges = outers.at[1], both.at[1]
    cut = lax.axis_index("cuts")
    spots = places(rows)
    place = jnp.where(cut == 0, spots[number], spots[2 + number])
    start = pl.multiple_of(jnp.where(cut == 0, 0, HALF), HALF)
    held[cut] = own[...]
    held[1 - cut] = mate[...]

    def store(k, which, value):
        made[which, 0], made[which, 1] = value

    chain(
        [lambda: (probes[picks[place], 0], probes[picks[place], 1])],
        [lambda which: wide((held[which, 0], held[which, 1]))],
        [lambda: amplitudes[place]],
        wave, first[...], second[...], store,
    )
    depth = sent_inband.shape[1]
    inner = pl.multiple_of(jnp.where(cut == 0, SIDE - depth, 0), 64)
    for channel in range(2):
        sent_outer[channel] = made[1 - cut, channel, pl.ds(start, HALF)].astype(BF)
        sent_inband[channel] = made[1 - cut, channel, pl.ds(inner, depth)].astype(BF)
        kept[channel] = made[cut, channel]
        edges[channel] = made[cut, channel, pl.ds(start, HALF)].astype(BF)


def put_inband(put, rows, cols, number, inband, channel):
    upper = lax.axis_index("cuts") == 1
    spots = places(rows)
    spot = jnp.where(upper, spots[number], spots[2 + number])
    skip = jnp.where(upper, SIDE - inband.shape[1], 0)
    put(rows[spot] + HALF + skip, cols[spot], inband[channel].astype(F32))


def own_kernel(rows, cols, kept0, kept1, inband, total):
    cut = lax.axis_index("cuts")
    places_here = places(rows)
    total[...] = jnp.zeros_like(total)
    for channel in range(2):
        put = functools.partial(put_window, total, channel)
        for number, kept in enumerate((kept0, kept1)):
            spot = jnp.where(cut == 0, places_here[number], places_here[2 + number])
            put(rows[spot] + HALF, cols[spot], kept[channel])
        put_inband(put, rows, cols, 0, inband, channel)


def half_copy(total, output, channel, start, sem):
    return pltpu.make_async_copy(
        total.at[channel, pl.ds(pl.multiple_of(HALF + start, HALF), HALF)],
        output.at[0, channel, pl.ds(pl.multiple_of(start, HALF), HALF)],
        sem,
    )


def more_kernel(rows, cols, spots, given, inband, edges, total, output, sems):
    cut = lax.axis_index("cuts")
    shift = jnp.where(cut == 0, BAND, -HALF)
    far = jnp.where(cut == 0, HALF, 0)
    copies = []
    for channel in range(2):
        put = functools.partial(put_window, total, channel)
        put_inband(put, rows, cols, 1, inband, channel)
        for k in range(2):
            put(spots[2 * k] + shift, spots[2 * k + 1], edges[k, channel].astype(F32))
        copies.append(half_copy(total, output, channel, far, sems.at[channel]))
        copies[channel].start()
    for copy in copies:
        copy.wait()


def last_kernel(spots, given, outers, written, total, output, sems):
    cut = lax.axis_index("cuts")
    near = jnp.where(cut == 0, 0, HALF)
    shift = jnp.where(cut == 0, -HALF, BAND)
    copies = []
    for channel in range(2):
        for k in range(2):
            top, left = spots[4 + 2 * k] + shift, spots[5 + 2 * k]
            put_near(total, channel, top, left, outers[k, channel].astype(F32), near)
        copies.append(half_copy(total, output, channel, near, sems.at[channel]))
        copies[channel].start()
    for copy in copies:
        copy.wait()


def call(kernel, name, inputs, outputs, scratch=(), in_specs=None, out_specs=None, aliases={}, vmem=40, flops=1):
    scalars = [x for x in inputs if x.dtype == jnp.int32]
    return pl.pallas_call(
        kernel,
        name=name,
        out_shape=outputs,
        in_specs=in_specs or [SM] * len(scalars) + [VM] * (len(inputs) - len(scalars)),
        out_specs=out_specs or [VM] * len(outputs),
        scratch_shapes=list(scratch),
        input_output_aliases=aliases,
        cost_estimate=pl.CostEstimate(flops=flops, bytes_accessed=1, transcendentals=0),
        compiler_params=pltpu.CompilerParams(vmem_limit_bytes=vmem << 20),
    )(*inputs)


def arr(*shape, dtype=BF):
    return jax.ShapeDtypeStruct(shape, dtype)


def shards(objects, probes, amplitudes, prop_phase, scan_rows, scan_cols, probe_choice):
    route = routes(lax.axis_size("region"))
    move = lambda x, way: lax.ppermute(x, AXES, route[way])
    first, second = (jnp.asarray(t) for t in dft_blocks())
    wave = jnp.stack([jnp.cos(prop_phase), jnp.sin(prop_phase)])
    half = arr(2, HALF, SIDE)

    full = arr(2, SIDE, SIDE)
    near = pltpu.VMEM((2, BAND + HALF, WIDE), F32)
    early, late, band, rows, cols = call(
        edge_kernel, "edge",
        [pltpu.with_memory_space_constraint(x, pltpu.HBM) for x in (scan_rows, scan_cols, objects)],
        [arr(EDGE + 16, 128), arr(EDGE + 16, 128),
         arr(2, BAND, COLS, dtype=F32), arr(4, dtype=jnp.int32), arr(4, dtype=jnp.int32)],
        [pltpu.SemaphoreType.DMA((4,))],
        in_specs=[HB] * 3, out_specs=[VM] * 3 + [SM] * 2, vmem=50,
    )
    early = move(early, "early")
    late = move(late, "late")
    early, wave = lax.optimization_barrier((early, wave))
    (sent0,) = call(mate_kernel, "mate", [rows, cols, band, early], [full], [near])
    mate0 = move(sent0, "mate")
    sent1, own0, own1, spots = call(
        windows_kernel, "windows", [rows, cols, band, early, late],
        [full, full, full, arr(8, dtype=jnp.int32)], [near], out_specs=[VM, VM, VM, SM],
    )
    mate1 = move(sent1, "mate")
    optics = [probes, amplitudes, wave, first, second]
    work = [pltpu.VMEM((2, 2, SIDE, SIDE), BF), pltpu.VMEM((2, 2, SIDE, SIDE), F32)]
    wide_full = arr(2, SIDE, SIDE, dtype=F32)
    inner = arr(2, HALF + 64, SIDE)
    pair = arr(2, 2, HALF, SIDE)
    outer0, inband0, kept0, edge0 = call(
        functools.partial(solo_kernel, 0), "solo0", [rows, probe_choice, own0, mate0] + optics,
        [half, inner, wide_full, half], work, flops=10**11,
    )
    inband0 = move(inband0, "mate")
    outers, inband1, kept1, edges = call(
        functools.partial(solo_kernel, 1), "solo1",
        [rows, probe_choice, own1, mate1] + optics + [outer0, edge0],
        [pair, inner, wide_full, pair], work, flops=10**11,
    )
    inband1 = move(inband1, "mate")
    outers = move(outers, "direct")
    edges = move(edges, "early")
    (total,) = call(
        own_kernel, "own", [rows, cols, kept0, kept1, inband0],
        [arr(2, EXT, COLS, dtype=F32)], flops=10**11,
    )
    results = [arr(2, EXT, COLS, dtype=F32), arr(1, 2, BAND, COLS, dtype=F32)]
    total, written = call(
        more_kernel, "more", [rows, cols, spots, total, inband1, edges], results,
        [pltpu.SemaphoreType.DMA((2,))], out_specs=[VM, HB], aliases={3: 0}, flops=10**11,
    )
    _, gradient = call(
        last_kernel, "last", [spots, total, outers, written], results,
        [pltpu.SemaphoreType.DMA((2,))],
        in_specs=[SM, VM, VM, HB], out_specs=[VM, HB], aliases={1: 0, 3: 1},
    )
    return gradient


def solution(mesh):
    return jax.shard_map(
        shards,
        mesh=mesh,
        in_specs=(
            P("cuts", None, "region", None),
            P(),
            P("region", None, None),
            P(),
            P("region"),
            P("region"),
            P("region"),
        ),
        out_specs=P("cuts", None, "region", None),
        check_vma=False,
    )
```
